32 devices in a mesh: group: 8 (over y, x, core), replica: 4 (over z).
Axes of the slice: x: 2, y: 2, z: 4, core: 2. Of those that a mesh axis runs over, the one named last changes fastest.
Arguments:
- inputs: bfloat16 [64, 512, 768], P(('group', 'replica')), may hold values from -6 to 6
- cotangent: bfloat16 [64, 512, 768], P(('group', 'replica')), may hold values from -6 to 6
- lengths: int32 [64], P(('group', 'replica')), may hold values from 128 to 512, as said below
- query_weight: bfloat16 [768, 768], P('group'), may hold values from -0.21875 to 0.21875
- key_weight: bfloat16 [768, 768], P('group'), may hold values from -0.21875 to 0.21875
- value_weight: bfloat16 [768, 768], P('group'), may hold values from -0.21875 to 0.21875
- out_weight: bfloat16 [768, 768], P('group'), may hold values from -3.5 to 3.5
- in_weight: bfloat16 [768, 3072], P('group'), may hold values from -0.21875 to 0.21875
- back_weight: bfloat16 [3072, 768], P('group'), may hold values from -0.109375 to 0.109375
- query_bias: bfloat16 [768], P('group'), may hold values from -1.796875 to 1.796875
- value_bias: bfloat16 [768], P('group'), may hold values from -1.796875 to 1.796875
- out_bias: bfloat16 [768], P('group'), may hold values from -1.796875 to 1.796875
- in_bias: bfloat16 [3072], P('group'), may hold values from -1.796875 to 1.796875
- back_bias: bfloat16 [768], P('group'), may hold values from -1.796875 to 1.796875
- first_gain: bfloat16 [768], P('group'), may hold values from 0.5 to 1.5
- first_shift: bfloat16 [768], P('group'), may hold values from -1.796875 to 1.796875
- second_gain: bfloat16 [768], P('group'), may hold values from 0.5 to 1.5
- second_shift: bfloat16 [768], P('group'), may hold values from -1.796875 to 1.796875
Outputs:
- layer_out: bfloat16 [64, 512, 768], P(('group', 'replica'))
- input_grad: bfloat16 [64, 512, 768], P(('group', 'replica'))
- query_weight_grad: float32 [768, 768], P('group')
- key_weight_grad: float32 [768, 768], P('group')
- value_weight_grad: float32 [768, 768], P('group')
- out_weight_grad: float32 [768, 768], P('group')
- in_weight_grad: float32 [768, 3072], P('group')
- back_weight_grad: float32 [3072, 768], P('group')
- query_bias_grad: float32 [768], P('group')
- value_bias_grad: float32 [768], P('group')
- out_bias_grad: float32 [768], P('group')
- in_bias_grad: float32 [3072], P('group')
- back_bias_grad: float32 [768], P('group')
- first_gain_grad: float32 [768], P('group')
- first_shift_grad: float32 [768], P('group')
- second_gain_grad: float32 [768], P('group')
- second_shift_grad: float32 [768], P('group')
The draws below stay inside these ranges and needn't reach their ends.
Inputs may be any that keep to these rules, and one draw needn't show every extreme that they name: `lengths`: each sequence's valid tokens fill its first slots; some sequence has all 512 slots valid.
All inputs are finite; a program needn't handle non-finite values.
Results may differ from the reference program's by a relative error of at most 0.02.
Values may be sent and summed in bfloat16 or wider, within the bound.
No kernel may reach another device: no remote copies, remote signals or barrier semaphores. Data moves between devices by JAX's collectives and lax.ppermute only.
A program may use at most 192 MiB of HBM per device.

```python
import math
import jax
import jax.numpy as jnp
from jax import lax

D = 768
FF = 3072
HEADS = 12
HEAD_DIM = 64
SLOTS = 512
SEQS = 64


def draw_lengths(key, part):
    drawn = jax.random.randint(key, (SEQS,), SLOTS // 4, SLOTS + 1, dtype=jnp.int32)
    places = jnp.arange(SEQS, dtype=jnp.int32)
    drawn = jnp.where(places == 0, SLOTS, drawn)
    return jnp.where(places == 1, SLOTS // 4, drawn).astype(jnp.int32)


def block_levels(rng, shape, split, least, top_value):
    loudness, own = 1.0, jax.random.fold_in(rng, 6)
    for dim, blocks in split:
        heights = jnp.exp(jax.random.uniform(jax.random.fold_in(own, dim), (blocks,), jnp.float32, least / len(split), top_value / len(split)))
        loudness = loudness * jnp.repeat(heights, shape[dim] // blocks).reshape([-1 if axis == dim else 1 for axis in range(len(shape))])
    return loudness


def noise(key, shape, scale, limit, pieces=(), held_as=jnp.bfloat16):
    gain = block_levels(key, shape, pieces, -0.22, 0.18) if pieces else 1.0
    values = jax.random.normal(key, shape, jnp.float32) * scale * gain
    return jnp.minimum(jnp.maximum(values, -limit), limit).astype(held_as)


def setup_inputs(seed: int = 0) -> dict:
    streams_of = jax.random.split(jax.random.key(seed), 19)
    return {
        "inputs": noise(streams_of[0], (SEQS, SLOTS, D), 1.0, 6.0, ((0, 32),)),
        "cotangent": noise(streams_of[1], (SEQS, SLOTS, D), 1.0, 6.0, ((0, 32),)),
        "lengths": draw_lengths(jax.random.fold_in(streams_of[18], 71), 0),
        "query_weight": noise(streams_of[3], (D, D), D ** -0.5, 0.21875, ((0, 8),)),
        "key_weight": noise(streams_of[4], (D, D), D ** -0.5, 0.21875, ((0, 8),)),
        "value_weight": noise(streams_of[5], (D, D), D ** -0.5, 0.21875, ((0, 8),)),
        "out_weight": noise(streams_of[6], (D, D), (max(1, D // 256)) ** -0.5, 3.5, ((0, 8),)),
        "in_weight": noise(streams_of[7], (D, FF), D ** -0.5, 0.21875, ((0, 8),)),
        "back_weight": noise(streams_of[8], (FF, D), FF ** -0.5, 0.109375, ((0, 8),)),
        "query_bias": noise(streams_of[9], (D,), 0.3, 1.796875, ((0, 8),)),
        "value_bias": noise(streams_of[10], (D,), 0.3, 1.796875, ((0, 8),)),
        "out_bias": noise(streams_of[11], (D,), 0.3, 1.796875, ((0, 8),)),
        "in_bias": noise(streams_of[12], (FF,), 0.3, 1.796875, ((0, 8),)),
        "back_bias": noise(streams_of[13], (D,), 0.3, 1.796875, ((0, 8),)),
        "first_gain": jnp.clip(1.0 + 0.1 * jax.random.normal(streams_of[14], (D,), jnp.float32), 0.5, 1.5).astype(jnp.bfloat16),
        "first_shift": noise(streams_of[15], (D,), 0.3, 1.796875, ((0, 8),)),
        "second_gain": jnp.clip(1.0 + 0.1 * jax.random.normal(streams_of[16], (D,), jnp.float32), 0.5, 1.5).astype(jnp.bfloat16),
        "second_shift": noise(streams_of[17], (D,), 0.3, 1.796875, ((0, 8),)),
    }


@jax.custom_vjp
def low(v):
    return lax.optimization_barrier(v.astype(jnp.bfloat16)).astype(jnp.float32)

@jax.custom_vjp
def low_back(v):
    return v

def low_keep(v):
    return (low(v), None)

def low_pass(kept, grad):
    return (grad,)

def back_keep(v):
    return (v, None)

def back_low(kept, grad):
    return (low(grad),)
low.defvjp(low_keep, low_pass)
low_back.defvjp(back_keep, back_low)
NORM_EPS = 1e-12
HIGH = lax.Precision.HIGHEST

def both_ways(value):
    return low(low_back(value))

def project(left, right):
    return jnp.einsum('bsd,de->bse', left, right, precision=HIGH)

def layer_norm(hidden, norm_gain, norm_shift):
    centre = hidden - lax.optimization_barrier(jnp.mean(hidden, -1, keepdims=True))
    spread = lax.optimization_barrier(jnp.mean(centre * centre, -1, keepdims=True))
    return centre * lax.rsqrt(spread + NORM_EPS) * norm_gain + norm_shift

def forward(params, source, key_valid):
    query_weight, key_weight, value_weight, out_weight, in_weight, back_weight, query_bias, value_bias, out_bias, in_bias, back_bias, first_gain, first_shift, second_gain, second_shift = params
    batch_size = source.shape[0]
    score_scale = 1.0 / math.sqrt(HEAD_DIM)
    queries = both_ways(project(source, query_weight) + query_bias).reshape(batch_size, SLOTS, HEADS, HEAD_DIM)
    key_heads = both_ways(project(source, key_weight)).reshape(batch_size, SLOTS, HEADS, HEAD_DIM)
    value_heads = both_ways(project(source, value_weight) + value_bias).reshape(batch_size, SLOTS, HEADS, HEAD_DIM)
    scores = low_back(jnp.einsum('bqhd,bkhd->bhqk', queries, key_heads, precision=HIGH) * score_scale)
    scores = jnp.where(key_valid[:, None, None, :], scores, -1e+30)
    weights = low(jax.nn.softmax(scores, axis=-1))
    mixed_heads = jnp.einsum('bhqk,bkhd->bqhd', weights, value_heads, precision=HIGH)
    mixed_heads = both_ways(mixed_heads.reshape(batch_size, SLOTS, D))
    branch = low_back(project(mixed_heads, out_weight) + out_bias)
    after_attn = layer_norm(source + branch, first_gain, first_shift)
    hidden = low_back(project(low(after_attn), in_weight) + in_bias)
    active = low(jax.nn.gelu(hidden, approximate=False))
    ffn_out = low_back(project(active, back_weight) + back_bias)
    return layer_norm(after_attn + ffn_out, second_gain, second_shift)

def reference(inputs, cotangent, lengths, query_weight, key_weight, value_weight, out_weight, in_weight, back_weight, query_bias, value_bias, out_bias, in_bias, back_bias, first_gain, first_shift, second_gain, second_shift):
    params = tuple((param.astype(jnp.float32) for param in (query_weight, key_weight, value_weight, out_weight, in_weight, back_weight, query_bias, value_bias, out_bias, in_bias, back_bias, first_gain, first_shift, second_gain, second_shift)))
    group_rows = math.gcd(SEQS, max(1, 2048 // SLOTS))
    steps_count = SEQS // group_rows
    source_all = inputs.astype(jnp.float32).reshape(steps_count, group_rows, SLOTS, D)
    cotan_all = cotangent.astype(jnp.float32).reshape(steps_count, group_rows, SLOTS, D)
    length_all = lengths.reshape(steps_count, group_rows)

    def scan_step(totals, packed):
        source_part, cotangent_part, length_part = packed
        key_valid = jnp.arange(SLOTS, dtype=jnp.int32)[None, :] < length_part[:, None]
        result, pullback = jax.vjp(lambda params_in, source_in: forward(params_in, source_in, key_valid), params, source_part)
        weighted_cot = cotangent_part * key_valid[:, :, None].astype(jnp.float32)
        param_grads, source_grad = pullback(weighted_cot)
        totals = tuple((running + fresh for running, fresh in zip(totals, param_grads)))
        return (totals, (result.astype(jnp.bfloat16), source_grad.astype(jnp.bfloat16)))
    zero_grads = tuple((jnp.zeros_like(param) for param in params))
    totals, (results, source_grads) = lax.scan(scan_step, zero_grads, (source_all, cotan_all, length_all))
    layer_out = results.reshape(SEQS, SLOTS, D)
    input_grad = source_grads.reshape(SEQS, SLOTS, D)
    return (layer_out, input_grad, totals[0], totals[1], totals[2], totals[3], totals[4], totals[5], totals[6], totals[7], totals[8], totals[9], totals[10], totals[11], totals[12], totals[13], totals[14])
```

```python
import math

import jax
import jax.numpy as jnp
from jax import lax
from jax.sharding import PartitionSpec as P

HEADS = 12
HEAD_DIM = 64


NORM_EPS = 1e-12
inverse_root_two = 0.7071067811865476
inverse_root_tau = 0.3989422804014327


AXES = ("group", "replica")


def swap_with(array, group_mask, replica_mask=0):
    groups, replicas = lax.axis_size("group"), lax.axis_size("replica")
    pairs = [
        (g * replicas + r, (g ^ group_mask) * replicas + (r ^ replica_mask))
        for g in range(groups)
        for r in range(replicas)
    ]
    return lax.ppermute(array, AXES, pairs)


def after(array, *others):
    return lax.optimization_barrier((array,) + others)[0] if others else array


def gather_group(shard, bits, wait_for):
    plane = [1 << b for b in range(1, bits)]
    half = shard.shape[0] // 32 * 16
    orders = (plane, plane[::-1])
    cut = (slice(0, half), slice(half, None))
    shard = after(shard, *wait_for)
    pieces = {0: [shard]}
    first = []
    for mask in plane:
        pieces[mask] = [swap_with(shard, mask)]
        first.append(pieces[mask][0])
    halves = {d: [p[0][c] for c in cut] for d, p in pieces.items()}
    for count in range(2, len(plane) + 1):
        for d in range(2, 1 << bits, 2):
            if bin(d).count("1") != count:
                continue
            got = []
            for which, order in enumerate(orders):
                last = [m for m in order if m & d][-1]
                got.append(swap_with(halves[d ^ last][which], last))
            pieces[d] = got
            halves[d] = got
    for d in list(pieces):
        pieces[d | 1] = [swap_with(p, 1) for p in pieces[d]]
    return pieces, first


def place(pieces, me, group_size):
    rows = sum(p.shape[0] for p in pieces[0])
    full = jnp.zeros((group_size, rows, pieces[0][0].shape[1]), jnp.bfloat16)
    for d, parts in pieces.items():
        at = 0
        for part in parts:
            full = lax.dynamic_update_slice(full, part[None], (me ^ d, at, 0))
            at += part.shape[0]
    return full


def pick(array, axis, index):
    return lax.dynamic_index_in_dim(array, index, axis, keepdims=False)


def add_low(left, right):
    return (left.astype(jnp.float32) + right.astype(jnp.float32)).astype(jnp.bfloat16)


def reduce_all(chunks, me, bits):
    rows, model = chunks.shape[1:]
    chunks = chunks.reshape((2,) * bits + (rows, model))
    mine = [(me >> b) & 1 for b in range(bits)]
    axis = bits - 1
    received = swap_with(pick(chunks, axis, 1 - mine[0]), 1)
    chunks = add_low(pick(chunks, axis, mine[0]), received)
    half = rows // 32 * 16
    done = []
    for part, order in ((chunks[..., :half, :], 0), (chunks[..., half:, :], 1)):
        left = list(range(1, bits))
        for b in (left[:] if order == 0 else left[::-1]):
            axis = len(left) - 1 - left.index(b)
            received = swap_with(pick(part, axis, 1 - mine[b]), 1 << b)
            part = add_low(pick(part, axis, mine[b]), received)
            left.remove(b)
        done.append(part)
    total = jnp.concatenate(done)
    replicas = lax.axis_size("replica")
    if replicas == 1:
        return total
    at = lax.axis_index("replica")
    half = rows // 32 * 16
    pair = total.reshape(2, rows // 2, model)
    received = swap_with(pick(pair, 0, 1 - (at & 1)), 0, 1)
    kept = add_low(pick(pair, 0, at & 1), received)
    mask = 2
    while mask < replicas:
        kept = add_low(kept, swap_with(kept, 0, mask))
        mask *= 2
    other = swap_with(kept, 0, 1)
    low_first = jnp.concatenate([kept, other])
    high_first = jnp.concatenate([other, kept])
    return jnp.where((at & 1) == 0, low_first, high_first)


def project(left, right):
    return jnp.dot(left, right, preferred_element_type=jnp.float32)


def outer_sum(left, right):
    return jnp.einsum("rd,re->de", left, right, preferred_element_type=jnp.float32)


def back_project(grad_rows, weight_full):
    return jnp.einsum("re,de->rd", grad_rows, weight_full, preferred_element_type=jnp.float32)


def norm_forward(hidden, norm_gain, norm_shift):
    centre = hidden - jnp.mean(hidden, -1, keepdims=True)
    inverse = lax.rsqrt(jnp.mean(centre * centre, -1, keepdims=True) + NORM_EPS)
    normed = centre * inverse
    return (normed * norm_gain + norm_shift, normed, inverse)


def norm_backward(grad_out, norm_gain, normed, inverse):
    scaled = grad_out * norm_gain
    centred = (
        scaled
        - jnp.mean(scaled, -1, keepdims=True)
        - normed * jnp.mean(scaled * normed, -1, keepdims=True)
    )
    return (inverse * centred, jnp.sum(grad_out * normed, 0), jnp.sum(grad_out, 0))


def gelu_slope(hidden):
    normal_cdf = 0.5 * (1.0 + lax.erf(hidden * inverse_root_two))
    density = jnp.exp(-0.5 * hidden * hidden) * inverse_root_tau
    return normal_cdf + hidden * density


def per_device(
    inputs,
    cotangent,
    lengths,
    query_weight,
    key_weight,
    value_weight,
    out_weight,
    in_weight,
    back_weight,
    query_bias,
    value_bias,
    out_bias,
    in_bias,
    back_bias,
    first_gain,
    first_shift,
    second_gain,
    second_shift,
):
    me = lax.axis_index("group")
    group_size = lax.axis_size("group")
    bits = group_size.bit_length() - 1
    plane_bits = tuple(range(1, bits))
    small_shards = (
        query_bias, value_bias, out_bias, in_bias, back_bias,
        first_gain, first_shift, second_gain, second_shift,
    )
    small_sizes = tuple(a.shape[0] for a in small_shards)
    model = inputs.shape[2]
    small_rows = -(-sum(small_sizes) // (model * 16)) * 16
    small = jnp.concatenate(small_shards)
    small = jnp.pad(small, (0, small_rows * model - small.shape[0])).reshape(small_rows, model)
    shard_a = jnp.concatenate([query_weight, key_weight, value_weight, small])
    in_rows = in_weight.shape[0]
    in_cols = in_weight.shape[1] // model
    in_blocks = [in_weight[:, n * model : (n + 1) * model] for n in range(in_cols)]
    shard_b = jnp.concatenate([out_weight] + in_blocks)
    shard_c = back_weight
    gathered_a = gather_group(shard_a, bits, ())
    gathered_b = gather_group(shard_b, bits, gathered_a[1])
    gathered_c = gather_group(shard_c, bits, gathered_b[1])
    full_a = place(gathered_a[0], me, group_size)
    full_b = place(gathered_b[0], me, group_size)
    full_c = place(gathered_c[0], me, group_size)
    rows = query_weight.shape[0]
    full_query = full_a[:, :rows].reshape(model, model)
    full_key = full_a[:, rows : 2 * rows].reshape(model, model)
    full_value = full_a[:, 2 * rows : 3 * rows].reshape(model, model)
    flat_small = full_a[:, 3 * rows :].reshape(group_size, small_rows * model)
    small_full, at = [], 0
    for size in small_sizes:
        small_full.append(flat_small[:, at : at + size].reshape(-1))
        at += size
    full_out = full_b[:, :rows].reshape(model, model)
    full_in = jnp.concatenate(
        [full_b[:, rows + n * in_rows : rows + (n + 1) * in_rows] for n in range(in_cols)], axis=2
    ).reshape(model, in_cols * model)
    full_back = full_c.reshape(-1, model)
    (
        bias_query, bias_value, bias_out, bias_in, bias_back,
        gain_first, shift_first, gain_second, shift_second,
    ) = small_full
    seq_count, slot_count, model_width = inputs.shape
    total_rows = seq_count * slot_count
    block_rows = min(512, slot_count)
    seq_blocks = slot_count // block_rows
    item_count = seq_count * seq_blocks
    score_scale = 1.0 / math.sqrt(HEAD_DIM)
    flat_rows = inputs.reshape(total_rows, model_width)
    positions = lax.broadcasted_iota(jnp.int32, (seq_count, slot_count), 1)
    key_valid = positions < lengths[:, None]
    row_valid = key_valid.reshape(total_rows, 1).astype(jnp.float32)
    queries = (project(flat_rows, full_query) + bias_query.astype(jnp.float32)).astype(jnp.bfloat16)
    key_rows = project(flat_rows, full_key).astype(jnp.bfloat16)
    value_rows = (project(flat_rows, full_value) + bias_value.astype(jnp.float32)).astype(
        jnp.bfloat16
    )
    query_blocks = queries.reshape(item_count, block_rows, HEADS, HEAD_DIM)
    key_seqs = key_rows.reshape(seq_count, slot_count, HEADS, HEAD_DIM)
    value_seqs = value_rows.reshape(seq_count, slot_count, HEADS, HEAD_DIM)
    item_ids = jnp.arange(item_count, dtype=jnp.int32)

    def select_seq(item_id):
        seq_id = item_id // seq_blocks
        return (
            lax.dynamic_index_in_dim(key_seqs, seq_id, 0, False),
            lax.dynamic_index_in_dim(value_seqs, seq_id, 0, False),
            lax.dynamic_index_in_dim(key_valid, seq_id, 0, False),
        )

    def block_scores(query_part, key_part, valid_part):
        scores = (
            jnp.einsum("qhd,khd->hqk", query_part, key_part, preferred_element_type=jnp.float32)
            * score_scale
        )
        return jnp.where(valid_part[None, None, :], scores, -1e30)

    def attend(packed):
        query_part, item_id = packed
        key_part, value_part, valid_part = select_seq(item_id)
        scores = block_scores(query_part, key_part, valid_part)
        row_peak = jnp.max(scores, -1, keepdims=True)
        lifted = jnp.exp(scores - row_peak)
        normalizer = jnp.sum(lifted, -1, keepdims=True)
        soft_weights = (lifted / normalizer).astype(jnp.bfloat16)
        mixed_heads = jnp.einsum(
            "hqk,khd->qhd", soft_weights, value_part, preferred_element_type=jnp.float32
        )
        return (mixed_heads.astype(jnp.bfloat16), (row_peak + jnp.log(normalizer))[:, :, 0])

    mixed_blocks, log_sums = lax.map(attend, (query_blocks, item_ids))
    mixed_rows = mixed_blocks.reshape(total_rows, model_width)
    branch = project(mixed_rows, full_out) + bias_out.astype(jnp.float32)
    after_attn, normed_first, inverse_first = norm_forward(
        flat_rows.astype(jnp.float32) + branch,
        gain_first.astype(jnp.float32),
        shift_first.astype(jnp.float32),
    )
    after_low = after_attn.astype(jnp.bfloat16)
    hidden = project(after_low, full_in) + bias_in.astype(jnp.float32)
    active = jax.nn.gelu(hidden, approximate=False).astype(jnp.bfloat16)
    ffn_out = project(active, full_back) + bias_back.astype(jnp.float32)
    result_rows, normed_second, inverse_second = norm_forward(
        after_attn + ffn_out, gain_second.astype(jnp.float32), shift_second.astype(jnp.float32)
    )
    layer_out = result_rows.astype(jnp.bfloat16).reshape(seq_count, slot_count, model_width)
    back_query, back_key, back_value = full_query, full_key, full_value
    back_out, back_in, back_ffn = full_out, full_in, full_back
    gain_first_b, gain_second_b = gain_first, gain_second
    grad_result = cotangent.reshape(total_rows, model_width).astype(jnp.float32) * row_valid
    grad_h2, second_gain_grad, second_shift_grad = norm_backward(
        grad_result, gain_second_b.astype(jnp.float32), normed_second, inverse_second
    )
    grad_ffn = grad_h2.astype(jnp.bfloat16)
    back_bias_grad = jnp.sum(grad_ffn.astype(jnp.float32), 0)
    back_weight_grad = outer_sum(active, grad_ffn)
    grad_hidden = (back_project(grad_ffn, back_ffn) * gelu_slope(hidden)).astype(jnp.bfloat16)
    in_bias_grad = jnp.sum(grad_hidden.astype(jnp.float32), 0)
    in_weight_grad = outer_sum(after_low, grad_hidden)
    grad_after = back_project(grad_hidden, back_in) + grad_h2
    grad_h1, first_gain_grad, first_shift_grad = norm_backward(
        grad_after, gain_first_b.astype(jnp.float32), normed_first, inverse_first
    )
    grad_branch = grad_h1.astype(jnp.bfloat16)
    out_bias_grad = jnp.sum(grad_branch.astype(jnp.float32), 0)
    out_weight_grad = outer_sum(mixed_rows, grad_branch)
    grad_mixed = back_project(grad_branch, back_out).astype(jnp.bfloat16)

    def attend_back(packed):
        query_part, grad_part, lse_part, item_id = packed
        key_part, value_part, valid_part = select_seq(item_id)
        scores = block_scores(query_part, key_part, valid_part)
        soft_weights = jnp.exp(scores - lse_part[:, :, None])
        grad_weights = jnp.einsum(
            "qhd,khd->hqk", grad_part, value_part, preferred_element_type=jnp.float32
        )
        grad_values = jnp.einsum(
            "hqk,qhd->khd",
            soft_weights.astype(jnp.bfloat16),
            grad_part,
            preferred_element_type=jnp.float32,
        )
        row_inner = jnp.sum(soft_weights * grad_weights, -1, keepdims=True)
        grad_scores = (soft_weights * (grad_weights - row_inner)).astype(jnp.bfloat16)
        grad_queries = (
            jnp.einsum("hqk,khd->qhd", grad_scores, key_part, preferred_element_type=jnp.float32)
            * score_scale
        )
        grad_keys = (
            jnp.einsum("hqk,qhd->khd", grad_scores, query_part, preferred_element_type=jnp.float32)
            * score_scale
        )
        return (grad_queries, grad_keys, grad_values)

    query_grad_blocks, key_grad_items, value_grad_items = lax.map(
        attend_back,
        (
            query_blocks,
            grad_mixed.reshape(item_count, block_rows, HEADS, HEAD_DIM),
            log_sums,
            item_ids,
        ),
    )
    grad_queries = query_grad_blocks.reshape(total_rows, model_width).astype(jnp.bfloat16)
    grad_keys = key_grad_items.reshape(seq_count, seq_blocks, slot_count, model_width).sum(1)
    grad_keys = grad_keys.reshape(total_rows, model_width).astype(jnp.bfloat16)
    grad_values = value_grad_items.reshape(seq_count, seq_blocks, slot_count, model_width).sum(1)
    grad_values = grad_values.reshape(total_rows, model_width).astype(jnp.bfloat16)
    query_bias_grad = jnp.sum(grad_queries.astype(jnp.float32), 0)
    value_bias_grad = jnp.sum(grad_values.astype(jnp.float32), 0)
    query_weight_grad = outer_sum(flat_rows, grad_queries)
    key_weight_grad = outer_sum(flat_rows, grad_keys)
    value_weight_grad = outer_sum(flat_rows, grad_values)
    input_rows = (
        grad_h1
        + back_project(grad_queries, back_query)
        + back_project(grad_keys, back_key)
        + back_project(grad_values, back_value)
    )
    input_grad = input_rows.astype(jnp.bfloat16).reshape(seq_count, slot_count, model_width)
    by_group = lambda a: a.astype(jnp.bfloat16).reshape((group_size, -1, model))
    in_grad_blocks = [
        in_weight_grad[:, n * model : (n + 1) * model].astype(jnp.bfloat16).reshape(group_size, -1, model)
        for n in range(in_cols)
    ]
    small_grads = (
        query_bias_grad, value_bias_grad, out_bias_grad, in_bias_grad, back_bias_grad,
        first_gain_grad, first_shift_grad, second_gain_grad, second_shift_grad,
    )
    small_grad = jnp.concatenate([a.reshape(group_size, -1) for a in small_grads], axis=1)
    small_grad = jnp.pad(small_grad, ((0, 0), (0, small_rows * model - small_grad.shape[1])))
    small_grad = small_grad.astype(jnp.bfloat16).reshape(group_size, small_rows, model)
    sum_c = reduce_all(by_group(back_weight_grad), me, bits)
    sum_b = reduce_all(jnp.concatenate([by_group(out_weight_grad)] + in_grad_blocks, axis=1), me, bits)
    sum_a = reduce_all(
        jnp.concatenate(
            [by_group(query_weight_grad), by_group(key_weight_grad), by_group(value_weight_grad), small_grad],
            axis=1,
        ),
        me,
        bits,
    )
    wide = lambda a: a.astype(jnp.float32)
    flat_sum = sum_a[3 * rows :].reshape(-1)
    small_sums, at = [], 0
    for size in small_sizes:
        small_sums.append(wide(flat_sum[at : at + size]))
        at += size
    summed = (
        wide(sum_a[:rows]),
        wide(sum_a[rows : 2 * rows]),
        wide(sum_a[2 * rows : 3 * rows]),
        wide(sum_b[:rows]),
        wide(
            jnp.concatenate(
                [sum_b[rows + n * in_rows : rows + (n + 1) * in_rows] for n in range(in_cols)], axis=1
            )
        ),
        wide(sum_c),
    ) + tuple(small_sums)
    return (layer_out, input_grad) + summed


def solution(mesh):
    return jax.shard_map(
        per_device,
        mesh=mesh,
        in_specs=(
            P(("group", "replica"), None, None),
            P(("group", "replica"), None, None),
            P(("group", "replica")),
            P("group", None),
            P("group", None),
            P("group", None),
            P("group", None),
            P("group", None),
            P("group", None),
            P("group"),
            P("group"),
            P("group"),
            P("group"),
            P("group"),
            P("group"),
            P("group"),
            P("group"),
            P("group"),
        ),
        out_specs=(
            P(("group", "replica"), None, None),
            P(("group", "replica"), None, None),
            P("group", None),
            P("group", None),
            P("group", None),
            P("group", None),
            P("group", None),
            P("group", None),
            P("group"),
            P("group"),
            P("group"),
            P("group"),
            P("group"),
            P("group"),
            P("group"),
            P("group"),
            P("group"),
        ),
        check_vma=False,
    )
```

```python
import jax
import jax.numpy as jnp
from jax import lax
from jax.experimental import pallas as pl
from jax.experimental.pallas import tpu as pltpu
from jax.sharding import PartitionSpec as P

HEADS = 12
HEAD_DIM = 64


NORM_EPS = 1e-12
inverse_root_two = 0.7071067811865476
inverse_root_tau = 0.3989422804014327


AXES = ("group", "replica")


def swap_with(array, group_mask, replica_mask=0):
    groups, replicas = lax.axis_size("group"), lax.axis_size("replica")
    pairs = [
        (g * replicas + r, (g ^ group_mask) * replicas + (r ^ replica_mask))
        for g in range(groups)
        for r in range(replicas)
    ]
    return lax.ppermute(array, AXES, pairs)


def after(array, *others):
    return lax.optimization_barrier((array,) + others)[0] if others else array


def gather_group(shard, bits, wait_for):
    plane = [1 << b for b in range(1, bits)]
    half = shard.shape[0] // 32 * 16
    orders = (plane, plane[::-1])
    cut = (slice(0, half), slice(half, None))
    shard = after(shard, *wait_for)
    pieces = {0: [shard]}
    first = []
    for mask in plane:
        pieces[mask] = [swap_with(shard, mask)]
        first.append(pieces[mask][0])
    halves = {d: [p[0][c] for c in cut] for d, p in pieces.items()}
    for count in range(2, len(plane) + 1):
        for d in range(2, 1 << bits, 2):
            if bin(d).count("1") != count:
                continue
            got = []
            for which, order in enumerate(orders):
                last = [m for m in order if m & d][-1]
                got.append(swap_with(halves[d ^ last][which], last))
            pieces[d] = got
            halves[d] = got
    for d in list(pieces):
        pieces[d | 1] = [swap_with(p, 1) for p in pieces[d]]
    return pieces, first


def place(pieces, me, group_size):
    rows = sum(p.shape[0] for p in pieces[0])
    full = jnp.zeros((group_size, rows, pieces[0][0].shape[1]), jnp.bfloat16)
    for d, parts in pieces.items():
        at = 0
        for part in parts:
            full = lax.dynamic_update_slice(full, part[None], (me ^ d, at, 0))
            at += part.shape[0]
    return full


def pick(array, axis, index):
    return lax.dynamic_index_in_dim(array, index, axis, keepdims=False)


def add_low(left, right):
    return (left.astype(jnp.float32) + right.astype(jnp.float32)).astype(jnp.bfloat16)


def reduce_all(own, send, bits):
    rows, width = own.shape[1:]
    chunks = add_low(own, swap_with(send, 1)).reshape((2,) * (bits - 1) + (rows, width))
    half = rows // 32 * 16
    done = []
    for part, order in ((chunks[..., :half, :], 0), (chunks[..., half:, :], 1)):
        left = list(range(1, bits))
        for b in left[:] if order == 0 else left[::-1]:
            axis = len(left) - 1 - left.index(b)
            kept, away = (lax.index_in_dim(part, i, axis, keepdims=False) for i in (0, 1))
            part = add_low(kept, swap_with(away, 1 << b))
            left.remove(b)
        done.append(part)
    return sum_replicas(jnp.concatenate(done))


def sum_replicas(total):
    replicas = lax.axis_size("replica")
    if replicas == 1:
        return total
    rows, width = total.shape
    at = lax.axis_index("replica")
    pair = total.reshape(2, rows // 2, width)
    kept = add_low(pick(pair, 0, at & 1), swap_with(pick(pair, 0, 1 - (at & 1)), 0, 1))
    mask = 2
    while mask < replicas:
        kept = add_low(kept, swap_with(kept, 0, mask))
        mask *= 2
    other = swap_with(kept, 0, 1)
    return jnp.where(
        (at & 1) == 0, jnp.concatenate([kept, other]), jnp.concatenate([other, kept])
    )


def sum_everywhere(array, bits):
    for b in range(bits):
        array = array + swap_with(array, 1 << b)
    mask = 1
    while mask < lax.axis_size("replica"):
        array = array + swap_with(array, 0, mask)
        mask *= 2
    return array


VMEM_LIMIT = 60 * 1024 * 1024
GROUP_HEADS = 4
GROUP_COLS = GROUP_HEADS * HEAD_DIM


def nt(left, right):
    return lax.dot_general(left, right, (((1,), (1,)), ((), ())), preferred_element_type=jnp.float32)


def nn(left, right):
    return lax.dot_general(left, right, (((1,), (0,)), ((), ())), preferred_element_type=jnp.float32)


def tn(left, right):
    return lax.dot_general(left, right, (((0,), (0,)), ((), ())), preferred_element_type=jnp.float32)


def kernel_params(**more):
    return pltpu.CompilerParams(vmem_limit_bytes=VMEM_LIMIT, **more)


def cost(flops, moved):
    return pl.CostEstimate(flops=int(flops), bytes_accessed=int(moved), transcendentals=0)


def one_head(pair, head):
    lanes = lax.broadcasted_iota(jnp.int32, pair.shape, 1)
    keep = lanes < HEAD_DIM if head % 2 == 0 else lanes >= HEAD_DIM
    return jnp.where(keep, pair, jnp.zeros_like(pair))


def attend_kernel(lens, x, wq, wk, wv, bq, bv, q_out, k_out, v_out, mixed_out, probs_out):
    slots = x.shape[0]
    rows = x[...]
    q = ((nn(rows, wq[...]) + bq[...]).astype(jnp.bfloat16) * 0.125).astype(jnp.bfloat16)
    k = nn(rows, wk[...]).astype(jnp.bfloat16)
    v = (nn(rows, wv[...]) + bv[...]).astype(jnp.bfloat16)
    q_out[...] = q
    k_out[...] = k
    v_out[...] = v
    turned = v.astype(jnp.float32).T.astype(jnp.bfloat16)
    valid = lax.broadcasted_iota(jnp.int32, (slots, 1), 0) < lens[pl.program_id(0)]
    block = min(256, slots)
    for head in range(GROUP_HEADS):
        pair = slice(head // 2 * 128, head // 2 * 128 + 128)
        keys = one_head(k[:, pair], head)
        for at in range(0, slots, block):
            scores = nt(keys, q[at : at + block, pair])
            scores = jnp.where(valid, scores, -1e30)
            lifted = jnp.exp(scores - jnp.max(scores, axis=0, keepdims=True))
            share = 1.0 / jnp.sum(lifted, axis=0, keepdims=True)
            probs_out[head, :, at : at + block] = (lifted * share).astype(jnp.bfloat16)
    joined = jnp.concatenate(
        [
            nn(turned[h * HEAD_DIM : (h + 1) * HEAD_DIM], probs_out[h])
            for h in range(GROUP_HEADS)
        ]
    )
    mixed_out[...] = joined.T.astype(jnp.bfloat16)


def attend(lengths, rows, wq, wk, wv, bq, bv):
    seqs = lengths.shape[0]
    total, width = rows.shape
    slots = total // seqs
    groups = width // GROUP_COLS
    weight = pl.BlockSpec((width, GROUP_COLS), lambda s, j, lens: (0, j))
    bias = pl.BlockSpec((1, GROUP_COLS), lambda s, j, lens: (0, j))
    part = pl.BlockSpec((slots, GROUP_COLS), lambda s, j, lens: (s, j))
    table = jax.ShapeDtypeStruct((total, width), jnp.bfloat16)
    return pl.pallas_call(
        attend_kernel,
        out_shape=[table] * 4
        + [jax.ShapeDtypeStruct((seqs * groups * GROUP_HEADS, slots, slots), jnp.bfloat16)],
        grid_spec=pltpu.PrefetchScalarGridSpec(
            num_scalar_prefetch=1,
            grid=(seqs, groups),
            in_specs=[pl.BlockSpec((slots, width), lambda s, j, lens: (s, 0))]
            + [weight] * 3
            + [bias] * 2,
            out_specs=[part] * 4
            + [
                pl.BlockSpec(
                    (GROUP_HEADS, slots, slots), lambda s, j, lens: (s * groups + j, 0, 0)
                )
            ],
        ),
        compiler_params=kernel_params(),
        cost_estimate=cost(6 * total * width * width + 8 * total * slots * width, 3e7),
        name="attend",
    )(lengths, rows, wq, wk, wv, bq, bv)


def attend_back_kernel(q, k, v, grad, probs, grads_out, sums_out, held):
    slots = q.shape[0]
    block = min(256, slots)
    key_turned = k[...].astype(jnp.float32).T.astype(jnp.bfloat16)
    dq_parts = []
    for which in range(GROUP_HEADS // 2):
        pair = slice(which * 128, which * 128 + 128)
        grads, queries, values = grad[:, pair], q[:, pair], v[:, pair]
        dv = dk = None
        for head in (2 * which, 2 * which + 1):
            own_values = one_head(values, head)
            for at in range(0, slots, block):
                cols = slice(at, at + block)
                grad_probs = nt(own_values, grads[cols])
                soft = probs[head, :, cols].astype(jnp.float32)
                inner = jnp.sum(soft * grad_probs, axis=0, keepdims=True)
                held[:, cols] = (soft * (grad_probs - inner)).astype(jnp.bfloat16)
            scores_grad = held[...]
            more_v = nn(probs[head], one_head(grads, head))
            more_k = nn(scores_grad, one_head(queries, head))
            dv = more_v if dv is None else dv + more_v
            dk = more_k if dk is None else dk + more_k
            dq_parts.append(nn(key_turned[head * HEAD_DIM : (head + 1) * HEAD_DIM], scores_grad))
        grads_out[1, :, pair] = dk.astype(jnp.bfloat16)
        grads_out[2, :, pair] = dv.astype(jnp.bfloat16)
    grads_out[0] = (jnp.concatenate(dq_parts).T * 0.125).astype(jnp.bfloat16)
    sums_out[0, 0:1, :] = jnp.sum(grads_out[0].astype(jnp.float32), axis=0, keepdims=True)
    sums_out[0, 1:2, :] = jnp.sum(grads_out[2].astype(jnp.float32), axis=0, keepdims=True)


def attend_back(seqs, q, k, v, grad, probs):
    total, width = q.shape
    slots = total // seqs
    groups = width // GROUP_COLS
    part = pl.BlockSpec((slots, GROUP_COLS), lambda s, j: (s, j))
    return pl.pallas_call(
        attend_back_kernel,
        out_shape=[
            jax.ShapeDtypeStruct((3, total, width), jnp.bfloat16),
            jax.ShapeDtypeStruct((seqs, 2, width), jnp.float32),
        ],
        grid=(seqs, groups),
        in_specs=[part] * 4
        + [pl.BlockSpec((GROUP_HEADS, slots, slots), lambda s, j: (s * groups + j, 0, 0))],
        out_specs=[
            pl.BlockSpec((3, slots, GROUP_COLS), lambda s, j: (0, s, j)),
            pl.BlockSpec((1, 2, GROUP_COLS), lambda s, j: (s, 0, j)),
        ],
        scratch_shapes=[pltpu.VMEM((slots, slots), jnp.bfloat16)],
        compiler_params=kernel_params(),
        cost_estimate=cost(14 * total * slots * width, 3e7),
        name="attend_back",
    )(q, k, v, grad, probs)


def row_mean(array):
    return jnp.mean(array, -1, keepdims=True)


def feed_kernel(mixed, x, wo, wi, bo, g1, s1, bi, after_out, normed_out, inverse_out, active_out, slope_out):
    hidden_in = x[...].astype(jnp.float32) + (nn(mixed[...], wo[...]) + bo[...])
    centre = hidden_in - row_mean(hidden_in)
    inverse = lax.rsqrt(row_mean(centre * centre) + NORM_EPS)
    normed = centre * inverse
    after = (normed * g1[...] + s1[...]).astype(jnp.bfloat16)
    normed_out[...] = normed
    inverse_out[...] = jnp.broadcast_to(inverse, inverse_out.shape)
    after_out[...] = after
    width = after.shape[1]
    for at in range(0, wi.shape[1], width):
        cols = slice(at, at + width)
        hidden = nn(after, wi[:, cols]) + bi[:, cols]
        cdf = 0.5 * (1.0 + lax.erf(hidden * inverse_root_two))
        density = jnp.exp(-0.5 * hidden * hidden) * inverse_root_tau
        active_out[:, cols] = (hidden * cdf).astype(jnp.bfloat16)
        slope_out[:, cols] = (cdf + hidden * density).astype(jnp.bfloat16)


def whole(array):
    return pl.BlockSpec(array.shape, lambda *_: (0,) * array.ndim, pipeline_mode=pl.Buffered(1))


def by_rows(rows, width):
    return pl.BlockSpec((rows, width), lambda i, *_: (i, 0))


def shape(rows, width, dtype):
    return jax.ShapeDtypeStruct((rows, width), dtype)


def feed(mixed, x, wo, wi, bo, g1, s1, bi):
    total, width = x.shape
    wide = wi.shape[1]
    rows = min(256, total)
    bf, f32 = jnp.bfloat16, jnp.float32
    return pl.pallas_call(
        feed_kernel,
        out_shape=[
            shape(total, width, bf), shape(total, width, f32), shape(total, 128, f32),
            shape(total, wide, bf), shape(total, wide, bf),
        ],
        grid=(total // rows,),
        in_specs=[by_rows(rows, width)] * 2 + [whole(a) for a in (wo, wi, bo, g1, s1, bi)],
        out_specs=[by_rows(rows, n) for n in (width, width, 128, wide, wide)],
        compiler_params=kernel_params(),
        cost_estimate=cost(2 * total * width * (width + wide), 3e7),
        name="feed",
    )(mixed, x, wo, wi, bo, g1, s1, bi)


def column_sum(array):
    return jnp.sum(array, axis=0, keepdims=True)


def turn_kernel(lens, slots, active, normed1, slope, cot, wb, bb, g1, s1, g2, s2,
                layer_out, ffn_grad_out, hidden_grad_out, h2_grad_out, sums_out, wide_sums_out):
    step = pl.program_id(0)

    @pl.when(step == 0)
    def _():
        sums_out[...] = jnp.zeros_like(sums_out)
        wide_sums_out[...] = jnp.zeros_like(wide_sums_out)

    rows, width = normed1.shape
    after = normed1[...] * g1[...] + s1[...]
    h2 = after + (nn(active[...], wb[...]) + bb[...])
    centre = h2 - row_mean(h2)
    inverse = lax.rsqrt(row_mean(centre * centre) + NORM_EPS)
    normed = centre * inverse
    layer_out[...] = (normed * g2[...] + s2[...]).astype(jnp.bfloat16)
    first = step * rows
    place_in = first % slots + lax.broadcasted_iota(jnp.int32, (rows, 1), 0)
    grad = jnp.where(place_in < lens[first // slots], cot[...].astype(jnp.float32), 0.0)
    scaled = grad * g2[...]
    h2_grad = inverse * (scaled - row_mean(scaled) - normed * row_mean(scaled * normed))
    h2_grad_out[...] = h2_grad
    low = h2_grad.astype(jnp.bfloat16)
    ffn_grad_out[...] = low
    sums_out[0:1, :] += column_sum(grad * normed)
    sums_out[1:2, :] += column_sum(grad)
    sums_out[2:3, :] += column_sum(low.astype(jnp.float32))
    for at in range(0, wb.shape[0], width):
        cols = slice(at, at + width)
        piece = (nt(low, wb[cols, :]) * slope[:, cols].astype(jnp.float32)).astype(jnp.bfloat16)
        hidden_grad_out[:, cols] = piece
        wide_sums_out[:, cols] += column_sum(piece.astype(jnp.float32))


def turn(lengths, slots, active, normed1, slope, cot, wb, bb, g1, s1, g2, s2):
    total, width = normed1.shape
    wide = wb.shape[0]
    rows = min(256, slots)
    bf, f32 = jnp.bfloat16, jnp.float32
    fixed = lambda r, n: pl.BlockSpec((r, n), lambda i, *_: (0, 0))
    body = lambda lens, *refs: turn_kernel(lens, slots, *refs)
    return pl.pallas_call(
        body,
        out_shape=[
            shape(total, width, bf), shape(total, width, bf), shape(total, wide, bf),
            shape(total, width, f32), shape(8, width, f32), shape(1, wide, f32),
        ],
        grid_spec=pltpu.PrefetchScalarGridSpec(
            num_scalar_prefetch=1,
            grid=(total // rows,),
            in_specs=[by_rows(rows, n) for n in (wide, width, wide, width)]
            + [whole(a) for a in (wb, bb, g1, s1, g2, s2)],
            out_specs=[by_rows(rows, n) for n in (width, width, wide, width)]
            + [fixed(8, width), fixed(1, wide)],
        ),
        compiler_params=kernel_params(),
        cost_estimate=cost(4 * total * width * wide, 3e7),
        name="turn",
    )(lengths, active, normed1, slope, cot, wb, bb, g1, s1, g2, s2)


def return_kernel(hidden_grad, h2_grad, normed1, inverse1, wi, wo, g1,
                  h1_grad_out, branch_grad_out, mixed_grad_out, sums_out):
    @pl.when(pl.program_id(0) == 0)
    def _():
        sums_out[...] = jnp.zeros_like(sums_out)

    after_grad = nt(hidden_grad[...], wi[...]) + h2_grad[...]
    normed = normed1[...]
    scaled = after_grad * g1[...]
    h1_grad = inverse1[:, 0:1] * (scaled - row_mean(scaled) - normed * row_mean(scaled * normed))
    h1_grad_out[...] = h1_grad
    low = h1_grad.astype(jnp.bfloat16)
    branch_grad_out[...] = low
    mixed_grad_out[...] = nt(low, wo[...]).astype(jnp.bfloat16)
    sums_out[0:1, :] += column_sum(after_grad * normed)
    sums_out[1:2, :] += column_sum(after_grad)
    sums_out[2:3, :] += column_sum(low.astype(jnp.float32))


def return_grad(hidden_grad, h2_grad, normed1, inverse1, wi, wo, g1):
    total, width = normed1.shape
    wide = wi.shape[1]
    rows = min(256, total)
    bf, f32 = jnp.bfloat16, jnp.float32
    return pl.pallas_call(
        return_kernel,
        out_shape=[
            shape(total, width, f32), shape(total, width, bf), shape(total, width, bf), shape(8, width, f32),
        ],
        grid=(total // rows,),
        in_specs=[by_rows(rows, n) for n in (wide, width, width, 128)] + [whole(a) for a in (wi, wo, g1)],
        out_specs=[by_rows(rows, width)] * 3 + [pl.BlockSpec((8, width), lambda i: (0, 0))],
        compiler_params=kernel_params(),
        cost_estimate=cost(2 * total * width * (width + wide), 3e7),
        name="return_grad",
    )(hidden_grad, h2_grad, normed1, inverse1, wi, wo, g1)


def input_kernel(h1_grad, grads, wq, wk, wv, out):
    total = h1_grad[...] + nt(grads[0], wq[...]) + nt(grads[1], wk[...]) + nt(grads[2], wv[...])
    out[...] = total.astype(jnp.bfloat16)


def input_grad_of(h1_grad, grads, wq, wk, wv):
    total, width = h1_grad.shape
    rows = min(256, total)
    return pl.pallas_call(
        input_kernel,
        out_shape=shape(total, width, jnp.bfloat16),
        grid=(total // rows,),
        in_specs=[by_rows(rows, width), pl.BlockSpec((3, rows, width), lambda i: (0, i, 0))]
        + [whole(a) for a in (wq, wk, wv)],
        out_specs=by_rows(rows, width),
        compiler_params=kernel_params(),
        cost_estimate=cost(6 * total * width * width, 2e7),
        name="input_grad",
    )(h1_grad, grads, wq, wk, wv)


def store_chunks(product, me, own, send):
    count = 2 * own.shape[0]
    rows = product.shape[0] // count
    for g in range(count):
        chunk = product[g * rows : (g + 1) * rows].astype(jnp.bfloat16)
        apart = g ^ me

        @pl.when(apart % 2 == 0)
        def _():
            own[apart // 2] = chunk

        @pl.when(apart % 2 == 1)
        def _():
            send[apart // 2] = chunk


def halves(count, rows, blocks, width):
    return [jax.ShapeDtypeStruct((count // 2, rows * blocks, width), jnp.bfloat16)] * 2


def back_weight_kernel(me, active, grad, own, send):
    step = pl.program_id(0)
    product = tn(active[...], grad[...]).astype(jnp.bfloat16)
    half = pl.num_programs(0) // 2

    @pl.when(step < half)
    def _():
        send[0] = product

    @pl.when(step >= half)
    def _():
        own[0] = product


def plain_weight_kernel(me, active, grad, own, send):
    store_chunks(tn(active[...], grad[...]), me[0], own, send)


def back_weight(me, active, grad, count):
    total, wide = active.shape
    width = grad.shape[1]
    rows = wide // count
    half = count // 2
    common = dict(
        out_shape=halves(count, rows, 1, width),
        compiler_params=kernel_params(),
        cost_estimate=cost(2 * total * wide * width, 1.3e7),
        name="back_weight",
    )
    if rows % 128 == 0:
        chunk = lambda t, me: ((2 * (t % half) + 1 - t // half) ^ me[0])
        return pl.pallas_call(
            back_weight_kernel,
            grid_spec=pltpu.PrefetchScalarGridSpec(
                num_scalar_prefetch=1,
                grid=(count,),
                in_specs=[pl.BlockSpec((total, rows), lambda t, me: (0, chunk(t, me))), whole(grad)],
                out_specs=[
                    pl.BlockSpec((1, rows, width), lambda t, me: (jnp.maximum(t - half, 0), 0, 0)),
                    pl.BlockSpec((1, rows, width), lambda t, me: (jnp.minimum(t, half - 1), 0, 0)),
                ],
            ),
            **common,
        )(me, active, grad)
    block = 256
    return pl.pallas_call(
        plain_weight_kernel,
        grid_spec=pltpu.PrefetchScalarGridSpec(
            num_scalar_prefetch=1,
            grid=(width // block,),
            in_specs=[whole(active), pl.BlockSpec((total, block), lambda j, me: (0, j))],
            out_specs=[pl.BlockSpec((half, rows, block), lambda j, me: (0, 0, j))] * 2,
        ),
        **common,
    )(me, active, grad)


def in_out_kernel(me, after, hidden_grad, mixed, branch_grad, own, send):
    last = pl.program_id(0) == pl.num_programs(0) - 1

    @pl.when(jnp.logical_not(last))
    def _():
        store_chunks(tn(after[...], hidden_grad[...]), me[0], own, send)

    @pl.when(last)
    def _():
        store_chunks(tn(mixed[...], branch_grad[...]), me[0], own, send)


def in_out_weight(me, after, hidden_grad, mixed, branch_grad, count):
    total, width = after.shape
    blocks = hidden_grad.shape[1] // width
    rows = width // count
    return pl.pallas_call(
        in_out_kernel,
        out_shape=halves(count, rows, blocks + 1, width),
        grid_spec=pltpu.PrefetchScalarGridSpec(
            num_scalar_prefetch=1,
            grid=(blocks + 1,),
            in_specs=[
                whole(after),
                pl.BlockSpec((total, width), lambda j, me: (0, jnp.minimum(j, blocks - 1))),
                whole(mixed),
                whole(branch_grad),
            ],
            out_specs=[pl.BlockSpec((count // 2, rows, width), lambda j, me: (0, j, 0))] * 2,
        ),
        compiler_params=kernel_params(),
        cost_estimate=cost(2 * total * width * width * (blocks + 1), 2e7),
        name="in_out_weight",
    )(me, after, hidden_grad, mixed, branch_grad)


def qkv_weight_kernel(me, rows, grads, own, send):
    store_chunks(tn(rows[...], grads[0]), me[0], own, send)


def qkv_weight(me, rows, grads, count):
    total, width = rows.shape
    chunk = width // count
    return pl.pallas_call(
        qkv_weight_kernel,
        out_shape=halves(count, chunk, 3, width),
        grid_spec=pltpu.PrefetchScalarGridSpec(
            num_scalar_prefetch=1,
            grid=(3,),
            in_specs=[whole(rows), pl.BlockSpec((1, total, width), lambda j, me: (j, 0, 0))],
            out_specs=[pl.BlockSpec((count // 2, chunk, width), lambda j, me: (0, j, 0))] * 2,
        ),
        compiler_params=kernel_params(),
        cost_estimate=cost(6 * total * width * width, 1e7),
        name="qkv_weight",
    )(me, rows, grads)


def pack_kernel(*refs):
    out = refs[-1]
    out[...] = jnp.zeros_like(out)
    at = 0
    for ref in refs[:-1]:
        size = ref.shape[1]
        for first in range(0, size, 128):
            n = min(128, size - first)
            out[at : at + 1, 0:n] = ref[:, first : first + n].astype(jnp.float32)
            at += 1


def spread_kernel(me, table, vectors_out, wide_out):
    count = table.shape[0]
    chunk = vectors_out.shape[1] // count
    wide_chunk = wide_out.shape[1] // count
    for g in range(count):
        tile = table[g ^ me[0]]
        vectors_out[:, g * chunk : (g + 1) * chunk] = tile[0:8, 0:chunk]
        for n, first in enumerate(range(0, wide_chunk, 128)):
            size = min(128, wide_chunk - first)
            wide_out[:, g * wide_chunk + first : g * wide_chunk + first + size] = tile[8 + n : 9 + n, 0:size]


def collect_kernel(me, vectors, wide, *outs):
    count = vectors.shape[1] // outs[0].shape[1]
    for g in range(count):

        @pl.when(g == me[0])
        def _():
            for i in range(8):
                n = outs[i].shape[1]
                outs[i][...] = vectors[i : i + 1, g * n : (g + 1) * n]
            n = outs[8].shape[1]
            outs[8][...] = wide[:, g * n : (g + 1) * n]


SMEM = lambda: pl.BlockSpec(memory_space=pltpu.SMEM)
VMEM = lambda: pl.BlockSpec(memory_space=pltpu.VMEM)


def pack(vectors):
    return pl.pallas_call(
        pack_kernel, out_shape=shape(16, 128, jnp.float32), in_specs=[VMEM()] * len(vectors), out_specs=VMEM(),
        compiler_params=kernel_params(), name="pack",
    )(*[v.reshape(1, -1) for v in vectors])


def spread(me, table, width, wide):
    return pl.pallas_call(
        spread_kernel, out_shape=[shape(8, width, jnp.float32), shape(1, wide, jnp.float32)],
        in_specs=[SMEM(), VMEM()], out_specs=[VMEM()] * 2, compiler_params=kernel_params(), name="spread",
    )(me, table)


def collect(me, vectors, wide, count):
    sizes = [vectors.shape[1] // count] * 8 + [wide.shape[1] // count]
    outs = pl.pallas_call(
        collect_kernel, out_shape=[shape(1, n, jnp.float32) for n in sizes],
        in_specs=[SMEM(), VMEM(), VMEM()], out_specs=[VMEM()] * 9, compiler_params=kernel_params(), name="collect",
    )(me, vectors, wide)
    return [o.reshape(-1) for o in outs]


def per_device(
    inputs, cotangent, lengths,
    query_weight, key_weight, value_weight, out_weight, in_weight, back_weight_shard,
    query_bias, value_bias, out_bias, in_bias, back_bias,
    first_gain, first_shift, second_gain, second_shift,
):
    index = lax.axis_index("group")
    me = index.reshape(1).astype(jnp.int32)
    count = lax.axis_size("group")
    bits = count.bit_length() - 1
    seqs, slots, width = inputs.shape
    total = seqs * slots
    chunk = query_weight.shape[0]
    wide = in_weight.shape[1]
    blocks = wide // width
    x = inputs.reshape(total, width)
    cot = cotangent.reshape(total, width)

    table = pack(
        [query_bias, value_bias, out_bias, back_bias, first_gain, first_shift, second_gain, second_shift, in_bias]
    )[None]
    in_blocks = [in_weight[:, n * width : (n + 1) * width] for n in range(blocks)]
    got_a = gather_group(jnp.concatenate([query_weight, key_weight, value_weight]), bits, ())
    for b in range(bits - 1, -1, -1):
        table = jnp.stack([table, swap_with(table, 1 << b)], axis=1).reshape((-1,) + table.shape[1:])
    got_b = gather_group(jnp.concatenate([out_weight] + in_blocks), bits, got_a[1])
    got_c = gather_group(back_weight_shard, bits, got_b[1])
    vectors, bi = spread(me, table, width, wide)
    bq, bv, bo, bb, g1, s1, g2, s2 = (vectors[i : i + 1] for i in range(8))
    full_a = place(got_a[0], index, count)
    full_b = place(got_b[0], index, count)
    full_c = place(got_c[0], index, count)
    wq, wk, wv = (full_a[:, n * chunk : (n + 1) * chunk].reshape(width, width) for n in range(3))
    wo = full_b[:, :chunk].reshape(width, width)
    wi = jnp.concatenate(
        [full_b[:, n * chunk : (n + 1) * chunk] for n in range(1, blocks + 1)], axis=2
    ).reshape(width, wide)
    wb = full_c.reshape(wide, width)

    q, k, v, mixed, probs = attend(lengths, x, wq, wk, wv, bq, bv)
    after_low, normed1, inverse1, active, slope = feed(mixed, x, wo, wi, bo, g1, s1, bi)
    layer_out, ffn_grad, hidden_grad, h2_grad, sums2, in_bias_sum = turn(
        lengths, slots, active, normed1, slope, cot, wb, bb, g1, s1, g2, s2
    )
    sum_c = reduce_all(*back_weight(me, active, ffn_grad, count), bits)
    h1_grad, branch_grad, mixed_grad, sums1 = return_grad(hidden_grad, h2_grad, normed1, inverse1, wi, wo, g1)
    sum_b = reduce_all(*in_out_weight(me, after_low, hidden_grad, mixed, branch_grad, count), bits)
    grads, attend_sums = attend_back(seqs, q, k, v, mixed_grad, probs)
    sum_a = reduce_all(*qkv_weight(me, x, grads, count), bits)
    input_grad = input_grad_of(h1_grad, grads, wq, wk, wv)

    small = jnp.concatenate(
        [
            jnp.sum(attend_sums, 0), sums1[2:3], sums2[2:3], sums1[0:2], sums2[0:2],
            in_bias_sum.reshape(blocks, width),
        ]
    )
    small = sum_everywhere(small, bits)
    vector_grads = collect(me, small[0:8], small[8:].reshape(1, wide), count)
    grad_q, grad_v, grad_o, grad_b, grad_g1, grad_s1, grad_g2, grad_s2, grad_i = vector_grads
    up = lambda a: a.astype(jnp.float32)
    in_sum = jnp.concatenate([sum_b[n * chunk : (n + 1) * chunk] for n in range(blocks)], axis=1)
    return (
        layer_out.reshape(inputs.shape), input_grad.reshape(inputs.shape),
        up(sum_a[:chunk]), up(sum_a[chunk : 2 * chunk]), up(sum_a[2 * chunk :]),
        up(sum_b[blocks * chunk :]), up(in_sum), up(sum_c),
        grad_q, grad_v, grad_o, grad_i, grad_b, grad_g1, grad_s1, grad_g2, grad_s2,
    )


def solution(mesh):
    return jax.shard_map(
        per_device,
        mesh=mesh,
        in_specs=(
            P(("group", "replica"), None, None),
            P(("group", "replica"), None, None),
            P(("group", "replica")),
            P("group", None),
            P("group", None),
            P("group", None),
            P("group", None),
            P("group", None),
            P("group", None),
            P("group"),
            P("group"),
            P("group"),
            P("group"),
            P("group"),
            P("group"),
            P("group"),
            P("group"),
            P("group"),
        ),
        out_specs=(
            P(("group", "replica"), None, None),
            P(("group", "replica"), None, None),
            P("group", None),
            P("group", None),
            P("group", None),
            P("group", None),
            P("group", None),
            P("group", None),
            P("group"),
            P("group"),
            P("group"),
            P("group"),
            P("group"),
            P("group"),
            P("group"),
            P("group"),
            P("group"),
        ),
        check_vma=False,
    )
```

```python
import functools

import jax
import jax.numpy as jnp
from jax import lax
from jax.experimental import pallas as pl
from jax.experimental.pallas import tpu as pltpu
from jax.sharding import PartitionSpec as P

HEADS = 12
HEAD_DIM = 64


NORM_EPS = 1e-12
inverse_root_two = 0.7071067811865476
inverse_root_tau = 0.3989422804014327


AXES = ("group", "replica")


def swap_with(array, group_mask, replica_mask=0):
    groups, replicas = lax.axis_size("group"), lax.axis_size("replica")
    pairs = [
        (g * replicas + r, (g ^ group_mask) * replicas + (r ^ replica_mask))
        for g in range(groups)
        for r in range(replicas)
    ]
    return lax.ppermute(array, AXES, pairs)


def after(array, *others):
    return lax.optimization_barrier((array,) + others)[0] if others else array


def gather_group(shard, bits, wait_for):
    plane = [1 << b for b in range(1, bits)]
    half = shard.shape[0] // 32 * 16
    orders = (plane, plane[::-1])
    cut = (slice(0, half), slice(half, None))
    shard = after(shard, *wait_for)
    pieces = {0: [shard]}
    first = []
    for mask in plane:
        pieces[mask] = [swap_with(shard, mask)]
        first.append(pieces[mask][0])
    halves = {d: [p[0][c] for c in cut] for d, p in pieces.items()}
    for count in range(2, len(plane) + 1):
        for d in range(2, 1 << bits, 2):
            if bin(d).count("1") != count:
                continue
            got = []
            for which, order in enumerate(orders):
                last = [m for m in order if m & d][-1]
                got.append(swap_with(halves[d ^ last][which], last))
            pieces[d] = got
            halves[d] = got
            last_got = got
    for d in list(pieces):
        pieces[d | 1] = [swap_with(p, 1) for p in pieces[d]]
    return pieces, first, last_got


def place(pieces, me, group_size):
    rows = sum(p.shape[0] for p in pieces[0])
    full = jnp.zeros((group_size, rows, pieces[0][0].shape[1]), jnp.bfloat16)
    for d, parts in pieces.items():
        at = 0
        for part in parts:
            full = lax.dynamic_update_slice(full, part[None], (me ^ d, at, 0))
            at += part.shape[0]
    return full


def pick(array, axis, index):
    return lax.dynamic_index_in_dim(array, index, axis, keepdims=False)


def add_low(left, right):
    return (left.astype(jnp.float32) + right.astype(jnp.float32)).astype(jnp.bfloat16)


def reduction(own, send, bits):
    received = swap_with(send, 1)
    yield [received]
    rows, width = own.shape[1:]
    chunks = add_low(own, received).reshape((2,) * (bits - 1) + (rows, width))
    half = rows // 32 * 16
    parts = [chunks[..., :half, :], chunks[..., half:, :]]
    lefts = [list(range(1, bits)), list(range(1, bits))]
    for _ in range(1, bits):
        kept, received = [], []
        for part, left, end in zip(parts, lefts, (0, -1)):
            b = left[end]
            axis = len(left) - 1 - left.index(b)
            keep, away = (lax.index_in_dim(part, i, axis, keepdims=False) for i in (0, 1))
            kept.append(keep)
            received.append(swap_with(away, 1 << b))
            left.remove(b)
        yield received
        parts = [add_low(keep, got) for keep, got in zip(kept, received)]
    total = jnp.concatenate(parts)
    replicas = lax.axis_size("replica")
    if replicas > 1:
        at = lax.axis_index("replica")
        pair = total.reshape(2, rows // 2, width)
        received = swap_with(pick(pair, 0, 1 - (at & 1)), 0, 1)
        yield [received]
        kept = add_low(pick(pair, 0, at & 1), received)
        mask = 2
        while mask < replicas:
            received = swap_with(kept, 0, mask)
            yield [received]
            kept = add_low(kept, received)
            mask *= 2
        other = swap_with(kept, 0, 1)
        yield [other]
        total = jnp.where(
            (at & 1) == 0, jnp.concatenate([kept, other]), jnp.concatenate([other, kept])
        )
    yield total


def finish(steps):
    *_, last = steps
    return last


def sum_everywhere(array, bits):
    for b in range(bits):
        array = array + swap_with(array, 1 << b)
    mask = 1
    while mask < lax.axis_size("replica"):
        array = array + swap_with(array, 0, mask)
        mask *= 2
    return array


class Gathered:
    def __init__(self, pieces, me, count, chunk, segments):
        self.me, self.chunk = me, chunk
        self.arrays, self.copies = [], []
        if chunk % 16:
            full = place(pieces, me[0], count)
            self.plain(full, count, segments)
            return
        for d, parts in pieces.items():
            at = 0
            for part in parts:
                for target, low, size, column in segments:
                    start, stop = max(at, low), min(at + part.shape[0], low + size)
                    if start < stop:
                        self.copies.append(
                            (len(self.arrays), start - at, stop - start, target, d, start - low, column)
                        )
                self.arrays.append(part)
                at += part.shape[0]
        self.fixed = False

    def plain(self, full, count, segments):
        width = full.shape[2]
        for target, low, size, column in segments:
            self.copies.append((len(self.arrays), 0, count * size, target, 0, 0, column))
            self.arrays.append(full[:, low : low + size].reshape(count * size, width))
        self.fixed = True

    def specs(self):
        return [pl.BlockSpec(memory_space=pl.ANY)] * len(self.arrays)

    def transfers(self, me, refs, targets, sems, only=None):
        out = []
        for n, (which, row, rows, target, d, inner, column) in enumerate(self.copies):
            if only is not None and target not in only:
                continue
            size = self.chunk
            if self.fixed:
                first = 0
            else:
                first = pl.multiple_of((me ^ d) * size + inner, 16)
            width = self.arrays[which].shape[1]
            out.append(
                pltpu.make_async_copy(
                    refs[which].at[pl.ds(row, rows)],
                    targets[target].at[pl.ds(first, rows), pl.ds(column, width)],
                    sems.at[n],
                )
            )
        return out


def fetch(plan, me, refs, targets, sems, first_step, only=None):
    @pl.when(first_step)
    def _():
        for copy in plan.transfers(me, refs, targets, sems, only):
            copy.start()


def arrive(plan, me, refs, targets, sems, first_step, only=None):
    @pl.when(first_step)
    def _():
        for copy in plan.transfers(me, refs, targets, sems, only):
            copy.wait()


VMEM_LIMIT = 60 * 1024 * 1024
GROUP_HEADS = 4
GROUP_COLS = GROUP_HEADS * HEAD_DIM


def nt(left, right):
    return lax.dot_general(left, right, (((1,), (1,)), ((), ())), preferred_element_type=jnp.float32)


def nn(left, right):
    return lax.dot_general(left, right, (((1,), (0,)), ((), ())), preferred_element_type=jnp.float32)


def tn(left, right):
    return lax.dot_general(left, right, (((0,), (0,)), ((), ())), preferred_element_type=jnp.float32)


def kernel_params(**more):
    return pltpu.CompilerParams(vmem_limit_bytes=VMEM_LIMIT, **more)


def cost(flops, moved):
    return pl.CostEstimate(flops=int(flops), bytes_accessed=int(moved), transcendentals=0)


def one_head(pair, head):
    lanes = lax.broadcasted_iota(jnp.int32, pair.shape, 1)
    keep = lanes < HEAD_DIM if head % 2 == 0 else lanes >= HEAD_DIM
    return jnp.where(keep, pair, jnp.zeros_like(pair))


def attend_kernel(plan, seq, aliased, lens, me, x, bq, bv, *refs):
    pieces = len(plan.arrays)
    q_out, k_out, v_out, mixed_out, probs_out, wq, wk, wv, sems = refs[pieces + aliased :]
    group = pl.program_id(0)
    fetch(plan, me[0], refs, (wq, wk, wv), sems, group == 0)
    arrive(plan, me[0], refs, (wq, wk, wv), sems, group == 0)
    cols = pl.ds(pl.multiple_of(group * GROUP_COLS, GROUP_COLS), GROUP_COLS)
    slots = x.shape[0]
    rows = x[...]
    q = ((nn(rows, wq[:, cols]) + bq[...]).astype(jnp.bfloat16) * 0.125).astype(jnp.bfloat16)
    k = nn(rows, wk[:, cols]).astype(jnp.bfloat16)
    v = (nn(rows, wv[:, cols]) + bv[...]).astype(jnp.bfloat16)
    q_out[...] = q
    k_out[...] = k
    v_out[...] = v
    turned = v.astype(jnp.float32).T.astype(jnp.bfloat16)
    valid = lax.broadcasted_iota(jnp.int32, (slots, 1), 0) < lens[seq]
    block = min(256, slots)
    for head in range(GROUP_HEADS):
        pair = slice(head // 2 * 128, head // 2 * 128 + 128)
        keys = one_head(k[:, pair], head)
        for at in range(0, slots, block):
            scores = nt(keys, q[at : at + block, pair])
            scores = jnp.where(valid, scores, -1e30)
            lifted = jnp.exp(scores - jnp.max(scores, axis=0, keepdims=True))
            share = 1.0 / jnp.sum(lifted, axis=0, keepdims=True)
            probs_out[head, :, at : at + block] = (lifted * share).astype(jnp.bfloat16)
    joined = jnp.concatenate(
        [
            nn(turned[h * HEAD_DIM : (h + 1) * HEAD_DIM], probs_out[h])
            for h in range(GROUP_HEADS)
        ]
    )
    mixed_out[...] = joined.T.astype(jnp.bfloat16)


def attend(lengths, seq, rows, plan, bq, bv, before=()):
    seqs = lengths.shape[0]
    total, width = rows.shape
    slots = total // seqs
    groups = width // GROUP_COLS
    bias = pl.BlockSpec((1, GROUP_COLS), lambda j, *_: (0, j))
    part = pl.BlockSpec((slots, GROUP_COLS), lambda j, *_: (seq, j))
    table = jax.ShapeDtypeStruct((total, width), jnp.bfloat16)
    anywhere = pl.BlockSpec(memory_space=pl.ANY)
    first_alias = 5 + len(plan.arrays)
    return pl.pallas_call(
        functools.partial(attend_kernel, plan, seq, len(before)),
        out_shape=[table] * 4
        + [jax.ShapeDtypeStruct((seqs * groups * GROUP_HEADS, slots, slots), jnp.bfloat16)],
        grid_spec=pltpu.PrefetchScalarGridSpec(
            num_scalar_prefetch=2,
            grid=(groups,),
            in_specs=[pl.BlockSpec((slots, width), lambda j, *_: (seq, 0))]
            + [bias] * 2
            + plan.specs()
            + [anywhere] * len(before),
            out_specs=[part] * 4
            + [pl.BlockSpec((GROUP_HEADS, slots, slots), lambda j, *_: (seq * groups + j, 0, 0))],
            scratch_shapes=[pltpu.VMEM((width, width), jnp.bfloat16)] * 3
            + [pltpu.SemaphoreType.DMA((len(plan.copies),))],
        ),
        input_output_aliases={first_alias + n: n for n in range(len(before))},
        compiler_params=kernel_params(),
        cost_estimate=cost((6 * total * width * width + 8 * total * slots * width) / seqs, 1.5e7),
        name=f"attend{seq}",
    )(lengths, plan.me, rows, bq, bv, *plan.arrays, *before)


def attend_back_kernel(q, k, v, grad, probs, *refs):
    grads_out, sums_out, held = refs[-3:]
    slots = q.shape[0]
    block = min(256, slots)
    key_turned = k[...].astype(jnp.float32).T.astype(jnp.bfloat16)
    dq_parts = []
    for which in range(GROUP_HEADS // 2):
        pair = slice(which * 128, which * 128 + 128)
        grads, queries, values = grad[:, pair], q[:, pair], v[:, pair]
        dv = dk = None
        for head in (2 * which, 2 * which + 1):
            own_values = one_head(values, head)
            for at in range(0, slots, block):
                cols = slice(at, at + block)
                grad_probs = nt(own_values, grads[cols])
                soft = probs[head, :, cols].astype(jnp.float32)
                inner = jnp.sum(soft * grad_probs, axis=0, keepdims=True)
                held[:, cols] = (soft * (grad_probs - inner)).astype(jnp.bfloat16)
            scores_grad = held[...]
            more_v = nn(probs[head], one_head(grads, head))
            more_k = nn(scores_grad, one_head(queries, head))
            dv = more_v if dv is None else dv + more_v
            dk = more_k if dk is None else dk + more_k
            dq_parts.append(nn(key_turned[head * HEAD_DIM : (head + 1) * HEAD_DIM], scores_grad))
        grads_out[1, :, pair] = dk.astype(jnp.bfloat16)
        grads_out[2, :, pair] = dv.astype(jnp.bfloat16)
    grads_out[0] = (jnp.concatenate(dq_parts).T * 0.125).astype(jnp.bfloat16)
    sums_out[0, 0:1, :] = jnp.sum(grads_out[0].astype(jnp.float32), axis=0, keepdims=True)
    sums_out[0, 1:2, :] = jnp.sum(grads_out[2].astype(jnp.float32), axis=0, keepdims=True)


def attend_back(seqs, seq, q, k, v, grad, probs, before=()):
    total, width = q.shape
    slots = total // seqs
    groups = width // GROUP_COLS
    part = pl.BlockSpec((slots, GROUP_COLS), lambda j: (seq, j))
    return pl.pallas_call(
        attend_back_kernel,
        out_shape=[
            jax.ShapeDtypeStruct((3, total, width), jnp.bfloat16),
            jax.ShapeDtypeStruct((1, 2, width), jnp.float32),
        ],
        grid=(groups,),
        in_specs=[part] * 4
        + [pl.BlockSpec((GROUP_HEADS, slots, slots), lambda j: (seq * groups + j, 0, 0))]
        + [pl.BlockSpec(memory_space=pl.ANY)] * len(before),
        out_specs=[
            pl.BlockSpec((3, slots, GROUP_COLS), lambda j: (0, seq, j)),
            pl.BlockSpec((1, 2, GROUP_COLS), lambda j: (0, 0, j)),
        ],
        scratch_shapes=[pltpu.VMEM((slots, slots), jnp.bfloat16)],
        input_output_aliases={5: 0} if before else {},
        compiler_params=kernel_params(),
        cost_estimate=cost(14 * total * slots * width / seqs, 1.5e7),
        name=f"attend_back{seq}",
    )(q, k, v, grad, probs, *before)


def row_mean(array):
    return jnp.mean(array, -1, keepdims=True)


def feed_kernel(plan, aliased, me, mixed, x, bo, g1, s1, bi, *refs):
    after_out, normed_out, inverse_out, active_out, slope_out, wo, wi, sems = refs[len(plan.arrays) + aliased :]
    first = pl.program_id(0) == 0
    fetch(plan, me[0], refs, (wo, wi), sems, first)
    arrive(plan, me[0], refs, (wo, wi), sems, first, (0,))
    hidden_in = x[...].astype(jnp.float32) + (nn(mixed[...], wo[...]) + bo[...])
    centre = hidden_in - row_mean(hidden_in)
    inverse = lax.rsqrt(row_mean(centre * centre) + NORM_EPS)
    normed = centre * inverse
    after = (normed * g1[...] + s1[...]).astype(jnp.bfloat16)
    normed_out[...] = normed
    inverse_out[...] = jnp.broadcast_to(inverse, inverse_out.shape)
    after_out[...] = after
    arrive(plan, me[0], refs, (wo, wi), sems, first, (1,))
    width = after.shape[1]
    for at in range(0, wi.shape[1], width):
        cols = slice(at, at + width)
        hidden = nn(after, wi[:, cols]) + bi[:, cols]
        cdf = 0.5 * (1.0 + lax.erf(hidden * inverse_root_two))
        density = jnp.exp(-0.5 * hidden * hidden) * inverse_root_tau
        active_out[:, cols] = (hidden * cdf).astype(jnp.bfloat16)
        slope_out[:, cols] = (cdf + hidden * density).astype(jnp.bfloat16)


def whole(array):
    return pl.BlockSpec(array.shape, lambda *_: (0,) * array.ndim, pipeline_mode=pl.Buffered(1))


def by_rows(rows, width):
    return pl.BlockSpec((rows, width), lambda i, *_: (i, 0))


def shape(rows, width, dtype):
    return jax.ShapeDtypeStruct((rows, width), dtype)


def row_blocks(total, parts, part):
    rows = min(256, total // parts)
    steps = total // parts // rows
    spec = lambda width: pl.BlockSpec((rows, width), lambda i, *_: (i + part * steps, 0))
    return rows, steps, spec


ANYWHERE = lambda: pl.BlockSpec(memory_space=pl.ANY)


def feed(parts, part, mixed, x, plan, bo, g1, s1, bi, before=()):
    total, width = x.shape
    wide = bi.shape[1]
    rows, steps, spec = row_blocks(total, parts, part)
    bf, f32 = jnp.bfloat16, jnp.float32
    aliases = {7 + len(plan.arrays) + n: n for n in range(len(before))}
    return pl.pallas_call(
        functools.partial(feed_kernel, plan, len(before)),
        out_shape=[
            shape(total, width, bf), shape(total, width, f32), shape(total, 128, f32),
            shape(total, wide, bf), shape(total, wide, bf),
        ],
        grid_spec=pltpu.PrefetchScalarGridSpec(
            num_scalar_prefetch=1,
            grid=(steps,),
            in_specs=[spec(width)] * 2 + [whole(a) for a in (bo, g1, s1, bi)] + plan.specs()
            + [ANYWHERE()] * len(before),
            out_specs=[spec(n) for n in (width, width, 128, wide, wide)],
            scratch_shapes=[
                pltpu.VMEM((width, width), bf), pltpu.VMEM((width, wide), bf),
                pltpu.SemaphoreType.DMA((len(plan.copies),)),
            ],
        ),
        input_output_aliases=aliases,
        compiler_params=kernel_params(),
        cost_estimate=cost(2 * total * width * (width + wide) / parts * 3, 1.5e7),
        name=f"feed{part}",
    )(plan.me, mixed, x, bo, g1, s1, bi, *plan.arrays, *before)


def column_sum(array):
    return jnp.sum(array, axis=0, keepdims=True)


def turn_kernel(plan, slots, lens, me, active, normed1, slope, cot, bb, g1, s1, g2, s2, *refs):
    (
        layer_out, ffn_grad_out, hidden_grad_out, h2_grad_out, sums_out, wide_sums_out, wb, sems,
    ) = refs[len(plan.arrays) :]
    step = pl.program_id(0)
    fetch(plan, me[0], refs, (wb,), sems, step == 0)
    arrive(plan, me[0], refs, (wb,), sems, step == 0)

    @pl.when(step == 0)
    def _():
        sums_out[...] = jnp.zeros_like(sums_out)
        wide_sums_out[...] = jnp.zeros_like(wide_sums_out)

    rows, width = normed1.shape
    after = normed1[...] * g1[...] + s1[...]
    h2 = after + (nn(active[...], wb[...]) + bb[...])
    centre = h2 - row_mean(h2)
    inverse = lax.rsqrt(row_mean(centre * centre) + NORM_EPS)
    normed = centre * inverse
    layer_out[...] = (normed * g2[...] + s2[...]).astype(jnp.bfloat16)
    first = step * rows
    place_in = first % slots + lax.broadcasted_iota(jnp.int32, (rows, 1), 0)
    grad = jnp.where(place_in < lens[first // slots], cot[...].astype(jnp.float32), 0.0)
    scaled = grad * g2[...]
    h2_grad = inverse * (scaled - row_mean(scaled) - normed * row_mean(scaled * normed))
    h2_grad_out[...] = h2_grad
    low = h2_grad.astype(jnp.bfloat16)
    ffn_grad_out[...] = low
    sums_out[0:1, :] += column_sum(grad * normed)
    sums_out[1:2, :] += column_sum(grad)
    sums_out[2:3, :] += column_sum(low.astype(jnp.float32))
    for at in range(0, wb.shape[0], width):
        cols = slice(at, at + width)
        piece = (nt(low, wb[cols, :]) * slope[:, cols].astype(jnp.float32)).astype(jnp.bfloat16)
        hidden_grad_out[:, cols] = piece
        wide_sums_out[:, cols] += column_sum(piece.astype(jnp.float32))


def turn(lengths, slots, active, normed1, slope, cot, plan, bb, g1, s1, g2, s2):
    total, width = normed1.shape
    wide = active.shape[1]
    rows = min(256, slots)
    bf, f32 = jnp.bfloat16, jnp.float32
    fixed = lambda r, n: pl.BlockSpec((r, n), lambda i, *_: (0, 0))
    return pl.pallas_call(
        functools.partial(turn_kernel, plan, slots),
        out_shape=[
            shape(total, width, bf), shape(total, width, bf), shape(total, wide, bf),
            shape(total, width, f32), shape(8, width, f32), shape(1, wide, f32),
        ],
        grid_spec=pltpu.PrefetchScalarGridSpec(
            num_scalar_prefetch=2,
            grid=(total // rows,),
            in_specs=[by_rows(rows, n) for n in (wide, width, wide, width)]
            + [whole(a) for a in (bb, g1, s1, g2, s2)] + plan.specs(),
            out_specs=[by_rows(rows, n) for n in (width, width, wide, width)]
            + [fixed(8, width), fixed(1, wide)],
            scratch_shapes=[pltpu.VMEM((wide, width), bf), pltpu.SemaphoreType.DMA((len(plan.copies),))],
        ),
        compiler_params=kernel_params(),
        cost_estimate=cost(4 * total * width * wide, 3e7),
        name="turn",
    )(lengths, plan.me, active, normed1, slope, cot, bb, g1, s1, g2, s2, *plan.arrays)


def return_kernel(plan, aliased, me, hidden_grad, h2_grad, normed1, inverse1, g1, *refs):
    h1_grad_out, branch_grad_out, mixed_grad_out, sums_out, wo, wi, sems = refs[len(plan.arrays) + aliased :]
    start = pl.program_id(0) == 0
    fetch(plan, me[0], refs, (wo, wi), sems, start)
    arrive(plan, me[0], refs, (wo, wi), sems, start)

    @pl.when(start)
    def _():
        sums_out[...] = jnp.zeros_like(sums_out)

    after_grad = nt(hidden_grad[...], wi[...]) + h2_grad[...]
    normed = normed1[...]
    scaled = after_grad * g1[...]
    h1_grad = inverse1[:, 0:1] * (scaled - row_mean(scaled) - normed * row_mean(scaled * normed))
    h1_grad_out[...] = h1_grad
    low = h1_grad.astype(jnp.bfloat16)
    branch_grad_out[...] = low
    mixed_grad_out[...] = nt(low, wo[...]).astype(jnp.bfloat16)
    sums_out[0:1, :] += column_sum(after_grad * normed)
    sums_out[1:2, :] += column_sum(after_grad)
    sums_out[2:3, :] += column_sum(low.astype(jnp.float32))


def return_grad(parts, part, hidden_grad, h2_grad, normed1, inverse1, plan, g1, before=()):
    total, width = normed1.shape
    wide = hidden_grad.shape[1]
    rows, steps, spec = row_blocks(total, parts, part)
    bf, f32 = jnp.bfloat16, jnp.float32
    aliases = {6 + len(plan.arrays) + n: n for n in range(len(before))}
    return pl.pallas_call(
        functools.partial(return_kernel, plan, len(before)),
        out_shape=[
            shape(total, width, f32), shape(total, width, bf), shape(total, width, bf), shape(8, width, f32),
        ],
        grid_spec=pltpu.PrefetchScalarGridSpec(
            num_scalar_prefetch=1,
            grid=(steps,),
            in_specs=[spec(n) for n in (wide, width, width, 128)] + [whole(g1)] + plan.specs()
            + [ANYWHERE()] * len(before),
            out_specs=[spec(width)] * 3 + [pl.BlockSpec((8, width), lambda i, *_: (0, 0))],
            scratch_shapes=[
                pltpu.VMEM((width, width), bf), pltpu.VMEM((width, wide), bf),
                pltpu.SemaphoreType.DMA((len(plan.copies),)),
            ],
        ),
        input_output_aliases=aliases,
        compiler_params=kernel_params(),
        cost_estimate=cost(2 * total * width * (width + wide) / parts, 1.5e7),
        name=f"return_grad{part}",
    )(plan.me, hidden_grad, h2_grad, normed1, inverse1, g1, *plan.arrays, *before)


def input_kernel(plan, me, h1_grad, grads, *refs):
    out, wq, wk, wv, sems = refs[len(plan.arrays) :]
    start = pl.program_id(0) == 0
    fetch(plan, me[0], refs, (wq, wk, wv), sems, start)
    arrive(plan, me[0], refs, (wq, wk, wv), sems, start)
    total = h1_grad[...] + nt(grads[0], wq[...]) + nt(grads[1], wk[...]) + nt(grads[2], wv[...])
    out[...] = total.astype(jnp.bfloat16)


def input_grad_of(h1_grad, grads, plan):
    total, width = h1_grad.shape
    rows, steps, spec = row_blocks(total, 1, 0)
    return pl.pallas_call(
        functools.partial(input_kernel, plan),
        out_shape=shape(total, width, jnp.bfloat16),
        grid_spec=pltpu.PrefetchScalarGridSpec(
            num_scalar_prefetch=1,
            grid=(steps,),
            in_specs=[spec(width), pl.BlockSpec((3, rows, width), lambda i, *_: (0, i, 0))] + plan.specs(),
            out_specs=spec(width),
            scratch_shapes=[pltpu.VMEM((width, width), jnp.bfloat16)] * 3
            + [pltpu.SemaphoreType.DMA((len(plan.copies),))],
        ),
        compiler_params=kernel_params(),
        cost_estimate=cost(6 * total * width * width, 2e7),
        name="input_grad",
    )(plan.me, h1_grad, grads, *plan.arrays)


def store_chunks(product, me, own, send):
    count = 2 * own.shape[0]
    rows = product.shape[0] // count
    for g in range(count):
        chunk = product[g * rows : (g + 1) * rows].astype(jnp.bfloat16)
        apart = g ^ me

        @pl.when(apart % 2 == 0)
        def _():
            own[apart // 2] = chunk

        @pl.when(apart % 2 == 1)
        def _():
            send[apart // 2] = chunk


def halves(count, rows, blocks, width):
    return [jax.ShapeDtypeStruct((count // 2, rows * blocks, width), jnp.bfloat16)] * 2


def back_weight_kernel(me, active, grad, own, send):
    step = pl.program_id(0)
    product = tn(active[...], grad[...]).astype(jnp.bfloat16)
    half = pl.num_programs(0) // 2

    @pl.when(step < half)
    def _():
        send[0] = product

    @pl.when(step >= half)
    def _():
        own[0] = product


def plain_weight_kernel(me, active, grad, own, send):
    store_chunks(tn(active[...], grad[...]), me[0], own, send)


def back_weight(me, active, grad, count):
    total, wide = active.shape
    width = grad.shape[1]
    rows = wide // count
    half = count // 2
    common = dict(
        out_shape=halves(count, rows, 1, width),
        compiler_params=kernel_params(),
        cost_estimate=cost(2 * total * wide * width, 1.3e7),
        name="back_weight",
    )
    if rows % 128 == 0:
        chunk = lambda t, me: ((2 * (t % half) + 1 - t // half) ^ me[0])
        return pl.pallas_call(
            back_weight_kernel,
            grid_spec=pltpu.PrefetchScalarGridSpec(
                num_scalar_prefetch=1,
                grid=(count,),
                in_specs=[pl.BlockSpec((total, rows), lambda t, me: (0, chunk(t, me))), whole(grad)],
                out_specs=[
                    pl.BlockSpec((1, rows, width), lambda t, me: (jnp.maximum(t - half, 0), 0, 0)),
                    pl.BlockSpec((1, rows, width), lambda t, me: (jnp.minimum(t, half - 1), 0, 0)),
                ],
            ),
            **common,
        )(me, active, grad)
    block = 256
    return pl.pallas_call(
        plain_weight_kernel,
        grid_spec=pltpu.PrefetchScalarGridSpec(
            num_scalar_prefetch=1,
            grid=(width // block,),
            in_specs=[whole(active), pl.BlockSpec((total, block), lambda j, me: (0, j))],
            out_specs=[pl.BlockSpec((half, rows, block), lambda j, me: (0, 0, j))] * 2,
        ),
        **common,
    )(me, active, grad)


def in_out_kernel(me, after, hidden_grad, mixed, branch_grad, own, send):
    last = pl.program_id(0) == pl.num_programs(0) - 1

    @pl.when(jnp.logical_not(last))
    def _():
        store_chunks(tn(after[...], hidden_grad[...]), me[0], own, send)

    @pl.when(last)
    def _():
        store_chunks(tn(mixed[...], branch_grad[...]), me[0], own, send)


def in_out_weight(me, after, hidden_grad, mixed, branch_grad, count):
    total, width = after.shape
    blocks = hidden_grad.shape[1] // width
    rows = width // count
    return pl.pallas_call(
        in_out_kernel,
        out_shape=halves(count, rows, blocks + 1, width),
        grid_spec=pltpu.PrefetchScalarGridSpec(
            num_scalar_prefetch=1,
            grid=(blocks + 1,),
            in_specs=[
                whole(after),
                pl.BlockSpec((total, width), lambda j, me: (0, jnp.minimum(j, blocks - 1))),
                whole(mixed),
                whole(branch_grad),
            ],
            out_specs=[pl.BlockSpec((count // 2, rows, width), lambda j, me: (0, j, 0))] * 2,
        ),
        compiler_params=kernel_params(),
        cost_estimate=cost(2 * total * width * width * (blocks + 1), 2e7),
        name="in_out_weight",
    )(me, after, hidden_grad, mixed, branch_grad)


def qkv_weight_kernel(me, rows, grads, own, send):
    store_chunks(tn(rows[...], grads[0]), me[0], own, send)


def qkv_weight(me, rows, grads, count):
    total, width = rows.shape
    chunk = width // count
    return pl.pallas_call(
        qkv_weight_kernel,
        out_shape=halves(count, chunk, 3, width),
        grid_spec=pltpu.PrefetchScalarGridSpec(
            num_scalar_prefetch=1,
            grid=(3,),
            in_specs=[whole(rows), pl.BlockSpec((1, total, width), lambda j, me: (j, 0, 0))],
            out_specs=[pl.BlockSpec((count // 2, chunk, width), lambda j, me: (0, j, 0))] * 2,
        ),
        compiler_params=kernel_params(),
        cost_estimate=cost(6 * total * width * width, 1e7),
        name="qkv_weight",
    )(me, rows, grads)


def pack_kernel(*refs):
    out = refs[-1]
    out[...] = jnp.zeros_like(out)
    at = 0
    for ref in refs[:-1]:
        size = ref.shape[1]
        for first in range(0, size, 128):
            n = min(128, size - first)
            out[at : at + 1, 0:n] = ref[:, first : first + n].astype(jnp.float32)
            at += 1


def spread_kernel(me, table, vectors_out, wide_out):
    count = table.shape[0]
    chunk = vectors_out.shape[1] // count
    wide_chunk = wide_out.shape[1] // count
    for g in range(count):
        tile = table[g ^ me[0]]
        vectors_out[:, g * chunk : (g + 1) * chunk] = tile[0:8, 0:chunk]
        for n, first in enumerate(range(0, wide_chunk, 128)):
            size = min(128, wide_chunk - first)
            wide_out[:, g * wide_chunk + first : g * wide_chunk + first + size] = tile[8 + n : 9 + n, 0:size]


def collect_kernel(me, vectors, wide, *outs):
    count = vectors.shape[1] // outs[0].shape[1]
    for g in range(count):

        @pl.when(g == me[0])
        def _():
            for i in range(8):
                n = outs[i].shape[1]
                outs[i][...] = vectors[i : i + 1, g * n : (g + 1) * n]
            n = outs[8].shape[1]
            outs[8][...] = wide[:, g * n : (g + 1) * n]


SMEM = lambda: pl.BlockSpec(memory_space=pltpu.SMEM)
VMEM = lambda: pl.BlockSpec(memory_space=pltpu.VMEM)


def pack(vectors):
    return pl.pallas_call(
        pack_kernel, out_shape=shape(16, 128, jnp.float32), in_specs=[VMEM()] * len(vectors), out_specs=VMEM(),
        compiler_params=kernel_params(), name="pack",
    )(*[v.reshape(1, -1) for v in vectors])


def spread(me, table, width, wide):
    return pl.pallas_call(
        spread_kernel, out_shape=[shape(8, width, jnp.float32), shape(1, wide, jnp.float32)],
        in_specs=[SMEM(), VMEM()], out_specs=[VMEM()] * 2, compiler_params=kernel_params(), name="spread",
    )(me, table)


def collect(me, vectors, wide, count):
    sizes = [vectors.shape[1] // count] * 8 + [wide.shape[1] // count]
    outs = pl.pallas_call(
        collect_kernel, out_shape=[shape(1, n, jnp.float32) for n in sizes],
        in_specs=[SMEM(), VMEM(), VMEM()], out_specs=[VMEM()] * 9, compiler_params=kernel_params(), name="collect",
    )(me, vectors, wide)
    return [o.reshape(-1) for o in outs]


def per_device(
    inputs, cotangent, lengths,
    query_weight, key_weight, value_weight, out_weight, in_weight, back_weight_shard,
    query_bias, value_bias, out_bias, in_bias, back_bias,
    first_gain, first_shift, second_gain, second_shift,
):
    index = lax.axis_index("group")
    me = index.reshape(1).astype(jnp.int32)
    count = lax.axis_size("group")
    bits = count.bit_length() - 1
    seqs, slots, width = inputs.shape
    total = seqs * slots
    chunk = query_weight.shape[0]
    wide = in_weight.shape[1]
    blocks = wide // width
    x = inputs.reshape(total, width)
    cot = cotangent.reshape(total, width)

    table = pack(
        [query_bias, value_bias, out_bias, back_bias, first_gain, first_shift, second_gain, second_shift, in_bias]
    )[None]
    in_blocks = [in_weight[:, n * width : (n + 1) * width] for n in range(blocks)]
    got_a = gather_group(jnp.concatenate([query_weight, key_weight, value_weight]), bits, ())
    for b in range(bits - 1, -1, -1):
        table = jnp.stack([table, swap_with(table, 1 << b)], axis=1).reshape((-1,) + table.shape[1:])
    got_b = gather_group(jnp.concatenate([out_weight] + in_blocks), bits, got_a[2])
    got_c = gather_group(back_weight_shard, bits, got_b[2])
    vectors, bi = spread(me, table, width, wide)
    bq, bv, bo, bb, g1, s1, g2, s2 = (vectors[i : i + 1] for i in range(8))
    third = [(n, n * chunk, chunk, 0) for n in range(3)]
    plan_a = Gathered(got_a[0], me, count, chunk, third)
    plan_b = Gathered(
        got_b[0], me, count, chunk,
        [(0, 0, chunk, 0)] + [(1, (n + 1) * chunk, chunk, n * width) for n in range(blocks)],
    )
    back_chunk = back_weight_shard.shape[0]
    plan_c = Gathered(got_c[0], me, count, back_chunk, [(0, 0, back_chunk, 0)])

    made = ()
    for seq in range(seqs):
        ready = got_b[1] if seq == seqs - 1 else ()
        made = attend(lengths, seq, after(x, *ready) if seq else x, plan_a, bq, bv, made)
    q, k, v, mixed, probs = made
    fed = feed(2, 0, mixed, x, plan_b, bo, g1, s1, bi)
    fed = feed(2, 1, mixed, after(x, *got_c[1]), plan_b, bo, g1, s1, bi, fed)
    after_low, normed1, inverse1, active, slope = fed
    layer_out, ffn_grad, hidden_grad, h2_grad, sums2, in_bias_sum = turn(
        lengths, slots, active, normed1, slope, cot, plan_c, bb, g1, s1, g2, s2
    )
    own, send = back_weight(me, active, ffn_grad, count)
    hidden_grad, send = lax.optimization_barrier((hidden_grad, send))
    red_c = reduction(own, send, bits)
    came = next(red_c)
    back = return_grad(2, 0, hidden_grad, h2_grad, normed1, inverse1, plan_b, g1)
    h2_grad = after(h2_grad, *came, back[3])
    came = next(red_c)
    h1_grad, branch_grad, mixed_grad, more = return_grad(
        2, 1, hidden_grad, h2_grad, normed1, inverse1, plan_b, g1, back[:3]
    )
    sums1 = back[3] + more
    own, send = in_out_weight(me, after_low, hidden_grad, mixed, branch_grad, count)
    red_b = reduction(own, send, bits)
    came_b = next(red_b)
    mixed_grad = after(mixed_grad, send, *came)
    came = next(red_c)
    first = attend_back(seqs, 0, q, k, v, mixed_grad, probs)
    grads, sums_at = first
    attend_sums = sums_at[0]
    for seq in range(1, seqs):
        mixed_grad = after(mixed_grad, attend_sums, *came, *came_b)
        came, came_b = next(red_c), next(red_b)
        grads, sums_at = attend_back(seqs, seq, q, k, v, mixed_grad, probs, (grads,))
        attend_sums = attend_sums + sums_at[0]
    own, send = qkv_weight(me, after(x, *came, *came_b), grads, count)
    came, came_b = next(red_c), next(red_b)
    red_a = reduction(own, send, bits)
    came_a = next(red_a)
    input_grad = input_grad_of(after(h1_grad, own, *came, *came_a), grads, plan_a)
    sum_c, sum_b, sum_a = finish(red_c), finish(red_b), finish(red_a)

    small = jnp.concatenate(
        [
            attend_sums, sums1[2:3], sums2[2:3], sums1[0:2], sums2[0:2],
            in_bias_sum.reshape(blocks, width),
        ]
    )
    small = sum_everywhere(small, bits)
    vector_grads = collect(me, small[0:8], small[8:].reshape(1, wide), count)
    grad_q, grad_v, grad_o, grad_b, grad_g1, grad_s1, grad_g2, grad_s2, grad_i = vector_grads
    up = lambda a: a.astype(jnp.float32)
    in_sum = jnp.concatenate([sum_b[n * chunk : (n + 1) * chunk] for n in range(blocks)], axis=1)
    return (
        layer_out.reshape(inputs.shape), input_grad.reshape(inputs.shape),
        up(sum_a[:chunk]), up(sum_a[chunk : 2 * chunk]), up(sum_a[2 * chunk :]),
        up(sum_b[blocks * chunk :]), up(in_sum), up(sum_c),
        grad_q, grad_v, grad_o, grad_i, grad_b, grad_g1, grad_s1, grad_g2, grad_s2,
    )


def solution(mesh):
    return jax.shard_map(
        per_device,
        mesh=mesh,
        in_specs=(
            P(("group", "replica"), None, None),
            P(("group", "replica"), None, None),
            P(("group", "replica")),
            P("group", None),
            P("group", None),
            P("group", None),
            P("group", None),
            P("group", None),
            P("group", None),
            P("group"),
            P("group"),
            P("group"),
            P("group"),
            P("group"),
            P("group"),
            P("group"),
            P("group"),
            P("group"),
        ),
        out_specs=(
            P(("group", "replica"), None, None),
            P(("group", "replica"), None, None),
            P("group", None),
            P("group", None),
            P("group", None),
            P("group", None),
            P("group", None),
            P("group", None),
            P("group"),
            P("group"),
            P("group"),
            P("group"),
            P("group"),
            P("group"),
            P("group"),
            P("group"),
            P("group"),
        ),
        check_vma=False,
    )
```

```python
import functools

import jax
import jax.numpy as jnp
from jax import lax
from jax.experimental import pallas as pl
from jax.experimental.pallas import tpu as pltpu
from jax.sharding import PartitionSpec as P

HEAD_DIM = 64


NORM_EPS = 1e-12
inverse_root_two = 0.7071067811865476
inverse_root_tau = 0.3989422804014327


AXES = ("group", "replica")


def swap_with(array, group_mask, replica_mask=0):
    groups, replicas = lax.axis_size("group"), lax.axis_size("replica")
    pairs = [
        (g * replicas + r, (g ^ group_mask) * replicas + (r ^ replica_mask))
        for g in range(groups)
        for r in range(replicas)
    ]
    return lax.ppermute(array, AXES, pairs)


def after(array, *others):
    return lax.optimization_barrier((array,) + others)[0] if others else array


def gather_group(shard, bits, wait_for):
    shard = after(shard, *wait_for)
    pieces = {0: [shard]}
    for d in range(2, 1 << bits, 2):
        pieces[d] = [swap_with(shard, d)]
    far = [pieces[d][0] for d in range(2, 1 << bits, 2)]
    for d in list(pieces):
        pieces[d | 1] = [swap_with(p, 1) for p in pieces[d]]
    return pieces, far


def place(pieces, me, group_size):
    rows = sum(p.shape[0] for p in pieces[0])
    full = jnp.zeros((group_size, rows, pieces[0][0].shape[1]), jnp.bfloat16)
    for d, parts in pieces.items():
        at = 0
        for part in parts:
            full = lax.dynamic_update_slice(full, part[None], (me ^ d, at, 0))
            at += part.shape[0]
    return full


def pick(array, axis, index):
    return lax.dynamic_index_in_dim(array, index, axis, keepdims=False)


def add_low(left, right):
    return (left.astype(jnp.float32) + right.astype(jnp.float32)).astype(jnp.bfloat16)


def reduction(own, send, bits):
    received = swap_with(send, 1)
    yield [received]
    rows, width = own.shape[1:]
    chunks = add_low(own, received).reshape((2,) * (bits - 1) + (rows, width))
    half = rows // 32 * 16
    parts = [chunks[..., :half, :], chunks[..., half:, :]]
    lefts = [list(range(1, bits)), list(range(1, bits))]
    for _ in range(1, bits):
        kept, received = [], []
        for part, left, end in zip(parts, lefts, (0, -1)):
            b = left[end]
            axis = len(left) - 1 - left.index(b)
            keep, away = (lax.index_in_dim(part, i, axis, keepdims=False) for i in (0, 1))
            kept.append(keep)
            received.append(swap_with(away, 1 << b))
            left.remove(b)
        yield received
        parts = [add_low(keep, got) for keep, got in zip(kept, received)]
    total = jnp.concatenate(parts)
    replicas = lax.axis_size("replica")
    if replicas > 1:
        at = lax.axis_index("replica")
        pair = total.reshape(2, rows // 2, width)
        received = swap_with(pick(pair, 0, 1 - (at & 1)), 0, 1)
        yield [received]
        kept = add_low(pick(pair, 0, at & 1), received)
        mask = 2
        while mask < replicas:
            received = swap_with(kept, 0, mask)
            yield [received]
            kept = add_low(kept, received)
            mask *= 2
        other = swap_with(kept, 0, 1)
        yield [other]
        total = jnp.where(
            (at & 1) == 0, jnp.concatenate([kept, other]), jnp.concatenate([other, kept])
        )
    yield total


def finish(steps):
    *_, last = steps
    return last


def everywhere(array, bits):
    masks = [(1 << b, 0) for b in range(bits)]
    mask = 1
    while mask < lax.axis_size("replica"):
        masks.append((0, mask))
        mask *= 2
    for group_mask, replica_mask in masks:
        received = swap_with(array, group_mask, replica_mask)
        yield [received]
        array = array + received
    yield array


class Gathered:
    def __init__(self, pieces, me, count, chunk, segments):
        self.me, self.chunk = me, chunk
        self.arrays, self.copies = [], []
        if chunk % 16:
            full = place(pieces, me[0], count)
            self.plain(full, count, segments)
            return
        for d, parts in pieces.items():
            at = 0
            for part in parts:
                for target, low, size, column in segments:
                    start, stop = max(at, low), min(at + part.shape[0], low + size)
                    if start < stop:
                        self.copies.append(
                            (len(self.arrays), start - at, stop - start, target, d, start - low, column)
                        )
                self.arrays.append(part)
                at += part.shape[0]
        self.fixed = False

    def plain(self, full, count, segments):
        width = full.shape[2]
        for target, low, size, column in segments:
            self.copies.append((len(self.arrays), 0, count * size, target, 0, 0, column))
            self.arrays.append(full[:, low : low + size].reshape(count * size, width))
        self.fixed = True

    def specs(self):
        return [pl.BlockSpec(memory_space=pl.ANY)] * len(self.arrays)

    def transfers(self, me, refs, targets, sems, only=None):
        out = []
        for n, (which, row, rows, target, d, inner, column) in enumerate(self.copies):
            if only is not None and target not in only:
                continue
            size = self.chunk
            if self.fixed:
                first = 0
            else:
                first = pl.multiple_of((me ^ d) * size + inner, 16)
            width = self.arrays[which].shape[1]
            out.append(
                pltpu.make_async_copy(
                    refs[which].at[pl.ds(row, rows)],
                    targets[target].at[pl.ds(first, rows), pl.ds(column, width)],
                    sems.at[n],
                )
            )
        return out


def fetch(plan, me, refs, targets, sems, first_step, only=None):
    @pl.when(first_step)
    def _():
        for copy in plan.transfers(me, refs, targets, sems, only):
            copy.start()


def arrive(plan, me, refs, targets, sems, first_step, only=None):
    @pl.when(first_step)
    def _():
        for copy in plan.transfers(me, refs, targets, sems, only):
            copy.wait()


VMEM_LIMIT = 60 * 1024 * 1024
GROUP_HEADS = 4
GROUP_COLS = GROUP_HEADS * HEAD_DIM


def nt(left, right):
    return lax.dot_general(left, right, (((1,), (1,)), ((), ())), preferred_element_type=jnp.float32)


def nn(left, right):
    return lax.dot_general(left, right, (((1,), (0,)), ((), ())), preferred_element_type=jnp.float32)


def tn(left, right):
    return lax.dot_general(left, right, (((0,), (0,)), ((), ())), preferred_element_type=jnp.float32)


def kernel_params(**more):
    return pltpu.CompilerParams(vmem_limit_bytes=VMEM_LIMIT, **more)


def cost(flops, moved):
    return pl.CostEstimate(flops=int(flops), bytes_accessed=int(moved), transcendentals=0)


def one_head(pair, head):
    lanes = lax.broadcasted_iota(jnp.int32, pair.shape, 1)
    keep = lanes < HEAD_DIM if head % 2 == 0 else lanes >= HEAD_DIM
    return jnp.where(keep, pair, jnp.zeros_like(pair))


def attend_kernel(plan, lens, me, x, bq, bv, *refs):
    q_out, k_out, v_out, mixed_out, probs_out, wq, wk, wv, sems = refs[len(plan.arrays) :]
    seq, group = pl.program_id(0), pl.program_id(1)
    start = jnp.logical_and(seq == 0, group == 0)
    fetch(plan, me[0], refs, (wq, wk, wv), sems, start)
    arrive(plan, me[0], refs, (wq, wk, wv), sems, start)
    cols = pl.ds(pl.multiple_of(group * GROUP_COLS, GROUP_COLS), GROUP_COLS)
    slots = x.shape[0]
    rows = x[...]
    q = ((nn(rows, wq[:, cols]) + bq[...]).astype(jnp.bfloat16) * 0.125).astype(jnp.bfloat16)
    k = nn(rows, wk[:, cols]).astype(jnp.bfloat16)
    v = (nn(rows, wv[:, cols]) + bv[...]).astype(jnp.bfloat16)
    q_out[...] = q
    k_out[...] = k
    v_out[...] = v
    turned = v.astype(jnp.float32).T.astype(jnp.bfloat16)
    valid = lax.broadcasted_iota(jnp.int32, (slots, 1), 0) < lens[seq]
    block = min(256, slots)
    for head in range(GROUP_HEADS):
        pair = slice(head // 2 * 128, head // 2 * 128 + 128)
        keys = one_head(k[:, pair], head)
        for at in range(0, slots, block):
            scores = nt(keys, q[at : at + block, pair])
            scores = jnp.where(valid, scores, -1e30)
            lifted = jnp.exp(scores - jnp.max(scores, axis=0, keepdims=True))
            share = 1.0 / jnp.sum(lifted, axis=0, keepdims=True)
            probs_out[head, :, at : at + block] = (lifted * share).astype(jnp.bfloat16)
    joined = jnp.concatenate(
        [
            nn(turned[h * HEAD_DIM : (h + 1) * HEAD_DIM], probs_out[h])
            for h in range(GROUP_HEADS)
        ]
    )
    mixed_out[...] = joined.T.astype(jnp.bfloat16)


def attend(lengths, rows, plan, bq, bv):
    seqs = lengths.shape[0]
    total, width = rows.shape
    slots = total // seqs
    groups = width // GROUP_COLS
    bias = pl.BlockSpec((1, GROUP_COLS), lambda s, j, *_: (0, j))
    part = pl.BlockSpec((slots, GROUP_COLS), lambda s, j, *_: (s, j))
    table = jax.ShapeDtypeStruct((total, width), jnp.bfloat16)
    return pl.pallas_call(
        functools.partial(attend_kernel, plan),
        out_shape=[table] * 4
        + [jax.ShapeDtypeStruct((seqs * groups * GROUP_HEADS, slots, slots), jnp.bfloat16)],
        grid_spec=pltpu.PrefetchScalarGridSpec(
            num_scalar_prefetch=2,
            grid=(seqs, groups),
            in_specs=[pl.BlockSpec((slots, width), lambda s, j, *_: (s, 0))]
            + [bias] * 2
            + plan.specs(),
            out_specs=[part] * 4
            + [pl.BlockSpec((GROUP_HEADS, slots, slots), lambda s, j, *_: (s * groups + j, 0, 0))],
            scratch_shapes=[pltpu.VMEM((width, width), jnp.bfloat16)] * 3
            + [pltpu.SemaphoreType.DMA((len(plan.copies),))],
        ),
        compiler_params=kernel_params(),
        cost_estimate=cost((6 * total * width * width + 8 * total * slots * width), 3e7),
        name="attend",
    )(lengths, plan.me, rows, bq, bv, *plan.arrays)


def attend_back_kernel(q, k, v, grad, probs, *refs):
    grads_out, sums_out, held = refs[-3:]
    slots = q.shape[0]
    block = min(256, slots)
    key_turned = k[...].astype(jnp.float32).T.astype(jnp.bfloat16)
    dq_parts = []
    for which in range(GROUP_HEADS // 2):
        pair = slice(which * 128, which * 128 + 128)
        grads, queries, values = grad[:, pair], q[:, pair], v[:, pair]
        dv = dk = None
        for head in (2 * which, 2 * which + 1):
            own_values = one_head(values, head)
            for at in range(0, slots, block):
                cols = slice(at, at + block)
                grad_probs = nt(own_values, grads[cols])
                soft = probs[head, :, cols].astype(jnp.float32)
                inner = jnp.sum(soft * grad_probs, axis=0, keepdims=True)
                held[:, cols] = (soft * (grad_probs - inner)).astype(jnp.bfloat16)
            scores_grad = held[...]
            more_v = nn(probs[head], one_head(grads, head))
            more_k = nn(scores_grad, one_head(queries, head))
            dv = more_v if dv is None else dv + more_v
            dk = more_k if dk is None else dk + more_k
            dq_parts.append(nn(key_turned[head * HEAD_DIM : (head + 1) * HEAD_DIM], scores_grad))
        grads_out[1, :, pair] = dk.astype(jnp.bfloat16)
        grads_out[2, :, pair] = dv.astype(jnp.bfloat16)
    grads_out[0] = (jnp.concatenate(dq_parts).T * 0.125).astype(jnp.bfloat16)
    sums_out[0, 0:1, :] = jnp.sum(grads_out[0].astype(jnp.float32), axis=0, keepdims=True)
    sums_out[0, 1:2, :] = jnp.sum(grads_out[2].astype(jnp.float32), axis=0, keepdims=True)


def attend_back(seqs, seq, q, k, v, grad, probs, before=()):
    total, width = q.shape
    slots = total // seqs
    groups = width // GROUP_COLS
    part = pl.BlockSpec((slots, GROUP_COLS), lambda j: (seq, j))
    return pl.pallas_call(
        attend_back_kernel,
        out_shape=[
            jax.ShapeDtypeStruct((3, total, width), jnp.bfloat16),
            jax.ShapeDtypeStruct((1, 2, width), jnp.float32),
        ],
        grid=(groups,),
        in_specs=[part] * 4
        + [pl.BlockSpec((GROUP_HEADS, slots, slots), lambda j: (seq * groups + j, 0, 0))]
        + [pl.BlockSpec(memory_space=pl.ANY)] * len(before),
        out_specs=[
            pl.BlockSpec((3, slots, GROUP_COLS), lambda j: (0, seq, j)),
            pl.BlockSpec((1, 2, GROUP_COLS), lambda j: (0, 0, j)),
        ],
        scratch_shapes=[pltpu.VMEM((slots, slots), jnp.bfloat16)],
        input_output_aliases={5: 0} if before else {},
        compiler_params=kernel_params(),
        cost_estimate=cost(14 * total * slots * width / seqs, 1.5e7),
    )(q, k, v, grad, probs, *before)


def row_mean(array):
    return jnp.mean(array, -1, keepdims=True)


def feed_kernel(plan, aliased, me, mixed, x, bo, g1, s1, bi, *refs):
    after_out, normed_out, inverse_out, active_out, slope_out, wo, wi, sems = refs[len(plan.arrays) + aliased :]
    first = pl.program_id(0) == 0
    fetch(plan, me[0], refs, (wo, wi), sems, first)
    arrive(plan, me[0], refs, (wo, wi), sems, first, (0,))
    hidden_in = x[...].astype(jnp.float32) + (nn(mixed[...], wo[...]) + bo[...])
    centre = hidden_in - row_mean(hidden_in)
    inverse = lax.rsqrt(row_mean(centre * centre) + NORM_EPS)
    normed = centre * inverse
    after = (normed * g1[...] + s1[...]).astype(jnp.bfloat16)
    normed_out[...] = normed
    inverse_out[...] = jnp.broadcast_to(inverse, inverse_out.shape)
    after_out[...] = after
    arrive(plan, me[0], refs, (wo, wi), sems, first, (1,))
    width = after.shape[1]
    for at in range(0, wi.shape[1], width):
        cols = slice(at, at + width)
        hidden = nn(after, wi[:, cols]) + bi[:, cols]
        cdf = 0.5 * (1.0 + lax.erf(hidden * inverse_root_two))
        density = jnp.exp(-0.5 * hidden * hidden) * inverse_root_tau
        active_out[:, cols] = (hidden * cdf).astype(jnp.bfloat16)
        slope_out[:, cols] = (cdf + hidden * density).astype(jnp.bfloat16)


def whole(array):
    return pl.BlockSpec(array.shape, lambda *_: (0,) * array.ndim, pipeline_mode=pl.Buffered(1))


def by_rows(rows, width):
    return pl.BlockSpec((rows, width), lambda i, *_: (i, 0))


def shape(rows, width, dtype):
    return jax.ShapeDtypeStruct((rows, width), dtype)


def row_blocks(total, parts, part):
    rows = min(256, total // parts)
    steps = total // parts // rows
    spec = lambda width: pl.BlockSpec((rows, width), lambda i, *_: (i + part * steps, 0))
    return rows, steps, spec


ANYWHERE = lambda: pl.BlockSpec(memory_space=pl.ANY)


def feed(parts, part, mixed, x, plan, bo, g1, s1, bi, before=()):
    total, width = x.shape
    wide = bi.shape[1]
    _, steps, spec = row_blocks(total, parts, part)
    bf, f32 = jnp.bfloat16, jnp.float32
    aliases = {7 + len(plan.arrays) + n: n for n in range(len(before))}
    return pl.pallas_call(
        functools.partial(feed_kernel, plan, len(before)),
        out_shape=[
            shape(total, width, bf), shape(total, width, f32), shape(total, 128, f32),
            shape(total, wide, bf), shape(total, wide, bf),
        ],
        grid_spec=pltpu.PrefetchScalarGridSpec(
            num_scalar_prefetch=1,
            grid=(steps,),
            in_specs=[spec(width)] * 2 + [whole(a) for a in (bo, g1, s1, bi)] + plan.specs()
            + [ANYWHERE()] * len(before),
            out_specs=[spec(n) for n in (width, width, 128, wide, wide)],
            scratch_shapes=[
                pltpu.VMEM((width, width), bf), pltpu.VMEM((width, wide), bf),
                pltpu.SemaphoreType.DMA((len(plan.copies),)),
            ],
        ),
        input_output_aliases=aliases,
        compiler_params=kernel_params(),
        cost_estimate=cost(2 * total * width * (width + wide) / parts * 3, 1.5e7),
    )(plan.me, mixed, x, bo, g1, s1, bi, *plan.arrays, *before)


def column_sum(array):
    return jnp.sum(array, axis=0, keepdims=True)


def turn_kernel(plan, slots, lens, me, active, normed1, slope, cot, bb, g1, s1, g2, s2, *refs):
    (
        layer_out, ffn_grad_out, hidden_grad_out, h2_grad_out, sums_out, wide_sums_out, wb, sems,
    ) = refs[len(plan.arrays) :]
    step = pl.program_id(0)
    fetch(plan, me[0], refs, (wb,), sems, step == 0)
    arrive(plan, me[0], refs, (wb,), sems, step == 0)

    @pl.when(step == 0)
    def _():
        sums_out[...] = jnp.zeros_like(sums_out)
        wide_sums_out[...] = jnp.zeros_like(wide_sums_out)

    rows, width = normed1.shape
    after = normed1[...] * g1[...] + s1[...]
    h2 = after + (nn(active[...], wb[...]) + bb[...])
    centre = h2 - row_mean(h2)
    inverse = lax.rsqrt(row_mean(centre * centre) + NORM_EPS)
    normed = centre * inverse
    layer_out[...] = (normed * g2[...] + s2[...]).astype(jnp.bfloat16)
    first = step * rows
    place_in = first % slots + lax.broadcasted_iota(jnp.int32, (rows, 1), 0)
    grad = jnp.where(place_in < lens[first // slots], cot[...].astype(jnp.float32), 0.0)
    scaled = grad * g2[...]
    h2_grad = inverse * (scaled - row_mean(scaled) - normed * row_mean(scaled * normed))
    h2_grad_out[...] = h2_grad
    low = h2_grad.astype(jnp.bfloat16)
    ffn_grad_out[...] = low
    sums_out[0:1, :] += column_sum(grad * normed)
    sums_out[1:2, :] += column_sum(grad)
    sums_out[2:3, :] += column_sum(low.astype(jnp.float32))
    for at in range(0, wb.shape[0], width):
        cols = slice(at, at + width)
        piece = (nt(low, wb[cols, :]) * slope[:, cols].astype(jnp.float32)).astype(jnp.bfloat16)
        hidden_grad_out[:, cols] = piece
        wide_sums_out[:, cols] += column_sum(piece.astype(jnp.float32))


def turn(lengths, slots, active, normed1, slope, cot, plan, bb, g1, s1, g2, s2):
    total, width = normed1.shape
    wide = active.shape[1]
    rows = min(256, slots)
    bf, f32 = jnp.bfloat16, jnp.float32
    fixed = lambda r, n: pl.BlockSpec((r, n), lambda i, *_: (0, 0))
    return pl.pallas_call(
        functools.partial(turn_kernel, plan, slots),
        out_shape=[
            shape(total, width, bf), shape(total, width, bf), shape(total, wide, bf),
            shape(total, width, f32), shape(8, width, f32), shape(1, wide, f32),
        ],
        grid_spec=pltpu.PrefetchScalarGridSpec(
            num_scalar_prefetch=2,
            grid=(total // rows,),
            in_specs=[by_rows(rows, n) for n in (wide, width, wide, width)]
            + [whole(a) for a in (bb, g1, s1, g2, s2)] + plan.specs(),
            out_specs=[by_rows(rows, n) for n in (width, width, wide, width)]
            + [fixed(8, width), fixed(1, wide)],
            scratch_shapes=[pltpu.VMEM((wide, width), bf), pltpu.SemaphoreType.DMA((len(plan.copies),))],
        ),
        compiler_params=kernel_params(),
        cost_estimate=cost(4 * total * width * wide, 3e7),
        name="turn",
    )(lengths, plan.me, active, normed1, slope, cot, bb, g1, s1, g2, s2, *plan.arrays)


def return_kernel(plan, aliased, me, hidden_grad, h2_grad, normed1, inverse1, g1, *refs):
    h1_grad_out, branch_grad_out, mixed_grad_out, sums_out, wo, wi, sems = refs[len(plan.arrays) + aliased :]
    start = pl.program_id(0) == 0
    fetch(plan, me[0], refs, (wo, wi), sems, start)
    arrive(plan, me[0], refs, (wo, wi), sems, start)

    @pl.when(start)
    def _():
        sums_out[...] = jnp.zeros_like(sums_out)

    after_grad = nt(hidden_grad[...], wi[...]) + h2_grad[...]
    normed = normed1[...]
    scaled = after_grad * g1[...]
    h1_grad = inverse1[:, 0:1] * (scaled - row_mean(scaled) - normed * row_mean(scaled * normed))
    h1_grad_out[...] = h1_grad
    low = h1_grad.astype(jnp.bfloat16)
    branch_grad_out[...] = low
    mixed_grad_out[...] = nt(low, wo[...]).astype(jnp.bfloat16)
    sums_out[0:1, :] += column_sum(after_grad * normed)
    sums_out[1:2, :] += column_sum(after_grad)
    sums_out[2:3, :] += column_sum(low.astype(jnp.float32))


def return_grad(parts, part, hidden_grad, h2_grad, normed1, inverse1, plan, g1, before=()):
    total, width = normed1.shape
    wide = hidden_grad.shape[1]
    _, steps, spec = row_blocks(total, parts, part)
    bf, f32 = jnp.bfloat16, jnp.float32
    aliases = {6 + len(plan.arrays) + n: n for n in range(len(before))}
    return pl.pallas_call(
        functools.partial(return_kernel, plan, len(before)),
        out_shape=[
            shape(total, width, f32), shape(total, width, bf), shape(total, width, bf), shape(8, width, f32),
        ],
        grid_spec=pltpu.PrefetchScalarGridSpec(
            num_scalar_prefetch=1,
            grid=(steps,),
            in_specs=[spec(n) for n in (wide, width, width, 128)] + [whole(g1)] + plan.specs()
            + [ANYWHERE()] * len(before),
            out_specs=[spec(width)] * 3 + [pl.BlockSpec((8, width), lambda i, *_: (0, 0))],
            scratch_shapes=[
                pltpu.VMEM((width, width), bf), pltpu.VMEM((width, wide), bf),
                pltpu.SemaphoreType.DMA((len(plan.copies),)),
            ],
        ),
        input_output_aliases=aliases,
        compiler_params=kernel_params(),
        cost_estimate=cost(2 * total * width * (width + wide) / parts, 1.5e7),
    )(plan.me, hidden_grad, h2_grad, normed1, inverse1, g1, *plan.arrays, *before)


def input_kernel(plan, me, h1_grad, grads, *refs):
    out, wq, wk, wv, sems = refs[len(plan.arrays) :]
    start = pl.program_id(0) == 0
    fetch(plan, me[0], refs, (wq, wk, wv), sems, start)
    arrive(plan, me[0], refs, (wq, wk, wv), sems, start)
    total = h1_grad[...] + nt(grads[0], wq[...]) + nt(grads[1], wk[...]) + nt(grads[2], wv[...])
    out[...] = total.astype(jnp.bfloat16)


def input_grad_of(h1_grad, grads, plan):
    total, width = h1_grad.shape
    rows, steps, spec = row_blocks(total, 1, 0)
    return pl.pallas_call(
        functools.partial(input_kernel, plan),
        out_shape=shape(total, width, jnp.bfloat16),
        grid_spec=pltpu.PrefetchScalarGridSpec(
            num_scalar_prefetch=1,
            grid=(steps,),
            in_specs=[spec(width), pl.BlockSpec((3, rows, width), lambda i, *_: (0, i, 0))] + plan.specs(),
            out_specs=spec(width),
            scratch_shapes=[pltpu.VMEM((width, width), jnp.bfloat16)] * 3
            + [pltpu.SemaphoreType.DMA((len(plan.copies),))],
        ),
        compiler_params=kernel_params(),
        cost_estimate=cost(6 * total * width * width, 2e7),
        name="input_grad",
    )(plan.me, h1_grad, grads, *plan.arrays)


def store_chunks(product, me, own, send):
    count = 2 * own.shape[0]
    rows = product.shape[0] // count
    for g in range(count):
        chunk = product[g * rows : (g + 1) * rows].astype(jnp.bfloat16)
        apart = g ^ me

        @pl.when(apart % 2 == 0)
        def _():
            own[apart // 2] = chunk

        @pl.when(apart % 2 == 1)
        def _():
            send[apart // 2] = chunk


def halves(count, rows, blocks, width):
    return [jax.ShapeDtypeStruct((count // 2, rows * blocks, width), jnp.bfloat16)] * 2


def back_weight_kernel(me, active, grad, own, send):
    step = pl.program_id(0)
    product = tn(active[...], grad[...]).astype(jnp.bfloat16)
    half = pl.num_programs(0) // 2

    @pl.when(step < half)
    def _():
        send[0] = product

    @pl.when(step >= half)
    def _():
        own[0] = product


def plain_weight_kernel(me, active, grad, own, send):
    store_chunks(tn(active[...], grad[...]), me[0], own, send)


def back_weight(me, active, grad, count):
    total, wide = active.shape
    width = grad.shape[1]
    rows = wide // count
    half = count // 2
    common = dict(
        out_shape=halves(count, rows, 1, width),
        compiler_params=kernel_params(),
        cost_estimate=cost(2 * total * wide * width, 1.3e7),
        name="back_weight",
    )
    if rows % 128 == 0:
        chunk = lambda t, me: ((2 * (t % half) + 1 - t // half) ^ me[0])
        return pl.pallas_call(
            back_weight_kernel,
            grid_spec=pltpu.PrefetchScalarGridSpec(
                num_scalar_prefetch=1,
                grid=(count,),
                in_specs=[pl.BlockSpec((total, rows), lambda t, me: (0, chunk(t, me))), whole(grad)],
                out_specs=[
                    pl.BlockSpec((1, rows, width), lambda t, me: (jnp.maximum(t - half, 0), 0, 0)),
                    pl.BlockSpec((1, rows, width), lambda t, me: (jnp.minimum(t, half - 1), 0, 0)),
                ],
            ),
            **common,
        )(me, active, grad)
    block = 256
    return pl.pallas_call(
        plain_weight_kernel,
        grid_spec=pltpu.PrefetchScalarGridSpec(
            num_scalar_prefetch=1,
            grid=(width // block,),
            in_specs=[whole(active), pl.BlockSpec((total, block), lambda j, me: (0, j))],
            out_specs=[pl.BlockSpec((half, rows, block), lambda j, me: (0, 0, j))] * 2,
        ),
        **common,
    )(me, active, grad)


def in_out_kernel(me, after, hidden_grad, mixed, branch_grad, own, send):
    last = pl.program_id(0) == pl.num_programs(0) - 1

    @pl.when(jnp.logical_not(last))
    def _():
        store_chunks(tn(after[...], hidden_grad[...]), me[0], own, send)

    @pl.when(last)
    def _():
        store_chunks(tn(mixed[...], branch_grad[...]), me[0], own, send)


def in_out_weight(me, after, hidden_grad, mixed, branch_grad, count):
    total, width = after.shape
    blocks = hidden_grad.shape[1] // width
    rows = width // count
    return pl.pallas_call(
        in_out_kernel,
        out_shape=halves(count, rows, blocks + 1, width),
        grid_spec=pltpu.PrefetchScalarGridSpec(
            num_scalar_prefetch=1,
            grid=(blocks + 1,),
            in_specs=[
                whole(after),
                pl.BlockSpec((total, width), lambda j, me: (0, jnp.minimum(j, blocks - 1))),
                whole(mixed),
                whole(branch_grad),
            ],
            out_specs=[pl.BlockSpec((count // 2, rows, width), lambda j, me: (0, j, 0))] * 2,
        ),
        compiler_params=kernel_params(),
        cost_estimate=cost(2 * total * width * width * (blocks + 1), 2e7),
        name="in_out_weight",
    )(me, after, hidden_grad, mixed, branch_grad)


def qkv_weight_kernel(me, rows, grads, own, send):
    store_chunks(tn(rows[...], grads[0]), me[0], own, send)


def qkv_weight(me, rows, grads, count):
    total, width = rows.shape
    chunk = width // count
    return pl.pallas_call(
        qkv_weight_kernel,
        out_shape=halves(count, chunk, 3, width),
        grid_spec=pltpu.PrefetchScalarGridSpec(
            num_scalar_prefetch=1,
            grid=(3,),
            in_specs=[whole(rows), pl.BlockSpec((1, total, width), lambda j, me: (j, 0, 0))],
            out_specs=[pl.BlockSpec((count // 2, chunk, width), lambda j, me: (0, j, 0))] * 2,
        ),
        compiler_params=kernel_params(),
        cost_estimate=cost(6 * total * width * width, 1e7),
        name="qkv_weight",
    )(me, rows, grads)


def pack_kernel(*refs):
    out = refs[-1]
    out[...] = jnp.zeros_like(out)
    at = 0
    for ref in refs[:-1]:
        size = ref.shape[1]
        for first in range(0, size, 128):
            n = min(128, size - first)
            out[at : at + 1, 0:n] = ref[:, first : first + n].astype(jnp.float32)
            at += 1


def spread_kernel(me, table, vectors_out, wide_out):
    count = table.shape[0]
    chunk = vectors_out.shape[1] // count
    wide_chunk = wide_out.shape[1] // count
    for g in range(count):
        tile = table[g ^ me[0]]
        vectors_out[:, g * chunk : (g + 1) * chunk] = tile[0:8, 0:chunk]
        for n, first in enumerate(range(0, wide_chunk, 128)):
            size = min(128, wide_chunk - first)
            wide_out[:, g * wide_chunk + first : g * wide_chunk + first + size] = tile[8 + n : 9 + n, 0:size]


def collect_kernel(me, vectors, wide, *outs):
    count = vectors.shape[1] // outs[0].shape[1]
    for g in range(count):

        @pl.when(g == me[0])
        def _():
            for i in range(8):
                n = outs[i].shape[1]
                outs[i][...] = vectors[i : i + 1, g * n : (g + 1) * n]
            n = outs[8].shape[1]
            outs[8][...] = wide[:, g * n : (g + 1) * n]


SMEM = lambda: pl.BlockSpec(memory_space=pltpu.SMEM)
VMEM = lambda: pl.BlockSpec(memory_space=pltpu.VMEM)


def pack(vectors):
    return pl.pallas_call(
        pack_kernel, out_shape=shape(16, 128, jnp.float32), in_specs=[VMEM()] * len(vectors), out_specs=VMEM(),
        compiler_params=kernel_params(), name="pack",
    )(*[v.reshape(1, -1) for v in vectors])


def spread(me, table, width, wide):
    return pl.pallas_call(
        spread_kernel, out_shape=[shape(8, width, jnp.float32), shape(1, wide, jnp.float32)],
        in_specs=[SMEM(), VMEM()], out_specs=[VMEM()] * 2, compiler_params=kernel_params(), name="spread",
    )(me, table)


def collect(me, vectors, wide, count):
    sizes = [vectors.shape[1] // count] * 8 + [wide.shape[1] // count]
    outs = pl.pallas_call(
        collect_kernel, out_shape=[shape(1, n, jnp.float32) for n in sizes],
        in_specs=[SMEM(), VMEM(), VMEM()], out_specs=[VMEM()] * 9, compiler_params=kernel_params(), name="collect",
    )(me, vectors, wide)
    return [o.reshape(-1) for o in outs]


def per_device(
    inputs, cotangent, lengths,
    query_weight, key_weight, value_weight, out_weight, in_weight, back_weight_shard,
    query_bias, value_bias, out_bias, in_bias, back_bias,
    first_gain, first_shift, second_gain, second_shift,
):
    index = lax.axis_index("group")
    me = index.reshape(1).astype(jnp.int32)
    count = lax.axis_size("group")
    bits = count.bit_length() - 1
    seqs, slots, width = inputs.shape
    total = seqs * slots
    chunk = query_weight.shape[0]
    wide = in_weight.shape[1]
    blocks = wide // width
    x = inputs.reshape(total, width)
    cot = cotangent.reshape(total, width)

    in_blocks = [in_weight[:, n * width : (n + 1) * width] for n in range(blocks)]
    got_a, far_a = gather_group(jnp.concatenate([query_weight, key_weight, value_weight]), bits, ())
    table = pack(
        [query_bias, value_bias, out_bias, back_bias, first_gain, first_shift, second_gain, second_shift, in_bias]
    )[None]
    for b in range(bits - 1, -1, -1):
        other = swap_with(table, 1 << b)
        table = jnp.stack([table, other], axis=1).reshape((-1,) + table.shape[1:])
    got_b, far_b = gather_group(jnp.concatenate([out_weight] + in_blocks), bits, far_a + [table])
    vectors, bi = spread(me, table, width, wide)
    bq, bv, bo, bb, g1, s1, g2, s2 = (vectors[i : i + 1] for i in range(8))
    third = [(n, n * chunk, chunk, 0) for n in range(3)]
    plan_a = Gathered(got_a, me, count, chunk, third)
    plan_b = Gathered(
        got_b, me, count, chunk,
        [(0, 0, chunk, 0)] + [(1, (n + 1) * chunk, chunk, n * width) for n in range(blocks)],
    )
    q, k, v, mixed, probs = attend(lengths, x, plan_a, bq, bv)
    back_chunk = back_weight_shard.shape[0]
    got_c, _ = gather_group(back_weight_shard, bits, far_b + [mixed])
    plan_c = Gathered(got_c, me, count, back_chunk, [(0, 0, back_chunk, 0)])
    after_low, normed1, inverse1, active, slope = feed(1, 0, mixed, x, plan_b, bo, g1, s1, bi)
    layer_out, ffn_grad, hidden_grad, h2_grad, sums2, in_bias_sum = turn(
        lengths, slots, active, normed1, slope, cot, plan_c, bb, g1, s1, g2, s2
    )
    own, send = back_weight(me, active, ffn_grad, count)
    hidden_grad, send = lax.optimization_barrier((hidden_grad, send))
    red_c = reduction(own, send, bits)
    came = next(red_c)
    h1_grad, branch_grad, mixed_grad, sums1 = return_grad(
        1, 0, hidden_grad, h2_grad, normed1, inverse1, plan_b, g1
    )
    branch_grad = after(branch_grad, *came)
    came = next(red_c)
    own, send = in_out_weight(me, after_low, hidden_grad, mixed, branch_grad, count)
    red_b = reduction(own, send, bits)
    mixed_grad = after(mixed_grad, send, *came)
    came, came_b = next(red_c), next(red_b)
    grads, sums_at = attend_back(seqs, 0, q, k, v, mixed_grad, probs)
    attend_sums = sums_at[0]
    for seq in range(1, seqs):
        mixed_grad = after(mixed_grad, attend_sums, *came, *came_b)
        came, came_b = next(red_c), next(red_b)
        grads, sums_at = attend_back(seqs, seq, q, k, v, mixed_grad, probs, (grads,))
        attend_sums = attend_sums + sums_at[0]
    small = jnp.concatenate(
        [
            attend_sums, sums1[2:3], sums2[2:3], sums1[0:2], sums2[0:2],
            in_bias_sum.reshape(blocks, width),
        ]
    )
    small_steps = everywhere(small, bits)
    rows_in = after(x, *came, *came_b)
    came, came_b = next(red_c), next(red_b)
    came_s = next(small_steps)
    own, send = qkv_weight(me, rows_in, grads, count)
    red_a = reduction(own, send, bits)
    came_a = next(red_a)
    h1_in = after(h1_grad, own, *came, *came_b, *came_s)
    came, came_b = next(red_c), next(red_b)
    came_s = next(small_steps)
    input_grad = input_grad_of(h1_in, grads, plan_a)
    sum_c, sum_b, sum_a = finish(red_c), finish(red_b), finish(red_a)
    small = finish(small_steps)
    vector_grads = collect(me, small[0:8], small[8:].reshape(1, wide), count)
    grad_q, grad_v, grad_o, grad_b, grad_g1, grad_s1, grad_g2, grad_s2, grad_i = vector_grads
    up = lambda a: a.astype(jnp.float32)
    in_sum = jnp.concatenate([sum_b[n * chunk : (n + 1) * chunk] for n in range(blocks)], axis=1)
    return (
        layer_out.reshape(inputs.shape), input_grad.reshape(inputs.shape),
        up(sum_a[:chunk]), up(sum_a[chunk : 2 * chunk]), up(sum_a[2 * chunk :]),
        up(sum_b[blocks * chunk :]), up(in_sum), up(sum_c),
        grad_q, grad_v, grad_o, grad_i, grad_b, grad_g1, grad_s1, grad_g2, grad_s2,
    )


def solution(mesh):
    return jax.shard_map(
        per_device,
        mesh=mesh,
        in_specs=(
            P(("group", "replica"), None, None),
            P(("group", "replica"), None, None),
            P(("group", "replica")),
            P("group", None),
            P("group", None),
            P("group", None),
            P("group", None),
            P("group", None),
            P("group", None),
            P("group"),
            P("group"),
            P("group"),
            P("group"),
            P("group"),
            P("group"),
            P("group"),
            P("group"),
            P("group"),
        ),
        out_specs=(
            P(("group", "replica"), None, None),
            P(("group", "replica"), None, None),
            P("group", None),
            P("group", None),
            P("group", None),
            P("group", None),
            P("group", None),
            P("group", None),
            P("group"),
            P("group"),
            P("group"),
            P("group"),
            P("group"),
            P("group"),
            P("group"),
            P("group"),
            P("group"),
        ),
        check_vma=False,
    )
```

```python
import functools

import jax
import jax.numpy as jnp
from jax import lax
from jax.experimental import pallas as pl
from jax.experimental.pallas import tpu as pltpu
from jax.sharding import PartitionSpec as P

HEAD_DIM = 64


NORM_EPS = 1e-12
inverse_root_two = 0.7071067811865476
inverse_root_tau = 0.3989422804014327


AXES = ("group", "replica")


def swap_with(array, group_mask, replica_mask=0):
    groups, replicas = lax.axis_size("group"), lax.axis_size("replica")
    pairs = [
        (g * replicas + r, (g ^ group_mask) * replicas + (r ^ replica_mask))
        for g in range(groups)
        for r in range(replicas)
    ]
    return lax.ppermute(array, AXES, pairs)


def after(array, *others):
    return lax.optimization_barrier((array,) + others)[0] if others else array


def gather_group(shard, bits, wait_for):
    shard = after(shard, *wait_for)
    pieces = {0: [shard]}
    for d in range(2, 1 << bits, 2):
        pieces[d] = [swap_with(shard, d)]
    far = [pieces[d][0] for d in range(2, 1 << bits, 2)]
    for d in list(pieces):
        pieces[d | 1] = [swap_with(p, 1) for p in pieces[d]]
    return pieces, far


def place(pieces, me, group_size):
    rows = sum(p.shape[0] for p in pieces[0])
    full = jnp.zeros((group_size, rows, pieces[0][0].shape[1]), jnp.bfloat16)
    for d, parts in pieces.items():
        at = 0
        for part in parts:
            full = lax.dynamic_update_slice(full, part[None], (me ^ d, at, 0))
            at += part.shape[0]
    return full


def pick(array, axis, index):
    return lax.dynamic_index_in_dim(array, index, axis, keepdims=False)


def add_low(left, right):
    return (left.astype(jnp.float32) + right.astype(jnp.float32)).astype(jnp.bfloat16)


def reduction(own, send, bits):
    received = swap_with(send, 1)
    yield [received]
    rows, width = own.shape[1:]
    half = rows // 32 * 16
    lefts = [list(range(1, bits)), list(range(1, bits))]
    split = None
    if bits == 3:
        split = split_add(own, received, half)
    else:
        chunks = add_low(own, received).reshape((2,) * (bits - 1) + (rows, width))
        parts = [chunks[..., :half, :], chunks[..., half:, :]]
    for step in range(1, bits):
        kept, received = [], []
        for n, (left, end) in enumerate(zip(lefts, (0, -1))):
            b = left[end]
            axis = len(left) - 1 - left.index(b)
            if split and step == 1:
                keep, away = split[2 * n : 2 * n + 2]
            else:
                keep, away = (lax.index_in_dim(parts[n], i, axis, keepdims=False) for i in (0, 1))
            kept.append(keep)
            received.append(swap_with(away, 1 << b))
            left.remove(b)
        yield received
        parts = [add_low(keep, got) for keep, got in zip(kept, received)]
    total = jnp.concatenate(parts)
    at = lax.axis_index("replica")
    pair = total.reshape(2, rows // 2, width)
    if lax.axis_size("replica") == 1:
        yield pair[0], pair[1]
        return
    received = swap_with(pick(pair, 0, 1 - (at & 1)), 0, 1)
    yield [received]
    kept = add_low(pick(pair, 0, at & 1), received)
    mask = 2
    while mask < lax.axis_size("replica"):
        received = swap_with(kept, 0, mask)
        yield [received]
        kept = add_low(kept, received)
        mask *= 2
    other = swap_with(kept, 0, 1)
    yield [other]
    yield kept, other


def in_order(odd, kept, other):
    return jnp.where(odd, jnp.concatenate([other, kept]), jnp.concatenate([kept, other]))


def finish(steps):
    *_, last = steps
    return last


class Gathered:
    def __init__(self, pieces, me, count, chunk, segments):
        self.me, self.chunk = me, chunk
        self.arrays, self.copies = [], []
        if chunk % 16:
            full = place(pieces, me[0], count)
            self.plain(full, count, segments)
            return
        for d, parts in pieces.items():
            at = 0
            for part in parts:
                for target, low, size, column in segments:
                    start, stop = max(at, low), min(at + part.shape[0], low + size)
                    if start < stop:
                        self.copies.append(
                            (len(self.arrays), start - at, stop - start, target, d, start - low, column)
                        )
                self.arrays.append(part)
                at += part.shape[0]
        self.fixed = False

    def plain(self, full, count, segments):
        width = full.shape[2]
        for target, low, size, column in segments:
            self.copies.append((len(self.arrays), 0, count * size, target, 0, 0, column))
            self.arrays.append(full[:, low : low + size].reshape(count * size, width))
        self.fixed = True

    def specs(self):
        return [pl.BlockSpec(memory_space=pl.ANY)] * len(self.arrays)

    def transfers(self, me, refs, targets, sems, only=None):
        out = []
        for n, (which, row, rows, target, d, inner, column) in enumerate(self.copies):
            if only is not None and target not in only:
                continue
            size = self.chunk
            if self.fixed:
                first = 0
            else:
                first = pl.multiple_of((me ^ d) * size + inner, 16)
            width = self.arrays[which].shape[1]
            out.append(
                pltpu.make_async_copy(
                    refs[which].at[pl.ds(row, rows)],
                    targets[target].at[pl.ds(first, rows), pl.ds(column, width)],
                    sems.at[n],
                )
            )
        return out


def fetch(plan, me, refs, targets, sems, first_step, only=None):
    @pl.when(first_step)
    def _():
        for copy in plan.transfers(me, refs, targets, sems, only):
            copy.start()


def arrive(plan, me, refs, targets, sems, first_step, only=None):
    @pl.when(first_step)
    def _():
        for copy in plan.transfers(me, refs, targets, sems, only):
            copy.wait()


VMEM_LIMIT = 60 * 1024 * 1024
GROUP_HEADS = 4
GROUP_COLS = GROUP_HEADS * HEAD_DIM


def nt(left, right):
    return lax.dot_general(left, right, (((1,), (1,)), ((), ())), preferred_element_type=jnp.float32)


def nn(left, right):
    return lax.dot_general(left, right, (((1,), (0,)), ((), ())), preferred_element_type=jnp.float32)


def tn(left, right):
    return lax.dot_general(left, right, (((0,), (0,)), ((), ())), preferred_element_type=jnp.float32)


def kernel_params(**more):
    return pltpu.CompilerParams(vmem_limit_bytes=VMEM_LIMIT, **more)


def cost(flops, moved):
    return pl.CostEstimate(flops=int(flops), bytes_accessed=int(moved), transcendentals=0)


def one_head(pair, head):
    lanes = lax.broadcasted_iota(jnp.int32, pair.shape, 1)
    keep = lanes < HEAD_DIM if head % 2 == 0 else lanes >= HEAD_DIM
    return jnp.where(keep, pair, jnp.zeros_like(pair))


def attend_kernel(plan, lens, me, x, bq, bv, *refs):
    q_out, k_out, v_out, mixed_out, probs_out, wq, wk, wv, sems = refs[len(plan.arrays) :]
    seq, group = pl.program_id(0), pl.program_id(1)
    start = jnp.logical_and(seq == 0, group == 0)
    fetch(plan, me[0], refs, (wq, wk, wv), sems, start)
    arrive(plan, me[0], refs, (wq, wk, wv), sems, start)
    cols = pl.ds(pl.multiple_of(group * GROUP_COLS, GROUP_COLS), GROUP_COLS)
    slots = x.shape[0]
    rows = x[...]
    q = ((nn(rows, wq[:, cols]) + bq[...]).astype(jnp.bfloat16) * 0.125).astype(jnp.bfloat16)
    k = nn(rows, wk[:, cols]).astype(jnp.bfloat16)
    v = (nn(rows, wv[:, cols]) + bv[...]).astype(jnp.bfloat16)
    q_out[...] = q
    k_out[...] = k
    v_out[...] = v
    turned = v.astype(jnp.float32).T.astype(jnp.bfloat16)
    valid = lax.broadcasted_iota(jnp.int32, (slots, 1), 0) < lens[seq]
    block = min(256, slots)
    for head in range(GROUP_HEADS):
        pair = slice(head // 2 * 128, head // 2 * 128 + 128)
        keys = one_head(k[:, pair], head)
        for at in range(0, slots, block):
            scores = nt(keys, q[at : at + block, pair])
            scores = jnp.where(valid, scores, -1e30)
            lifted = jnp.exp(scores - jnp.max(scores, axis=0, keepdims=True))
            share = 1.0 / jnp.sum(lifted, axis=0, keepdims=True)
            probs_out[head, :, at : at + block] = (lifted * share).astype(jnp.bfloat16)
    joined = jnp.concatenate(
        [
            nn(turned[h * HEAD_DIM : (h + 1) * HEAD_DIM], probs_out[h])
            for h in range(GROUP_HEADS)
        ]
    )
    mixed_out[...] = joined.T.astype(jnp.bfloat16)


def attend(lengths, rows, plan, bq, bv):
    seqs = lengths.shape[0]
    total, width = rows.shape
    slots = total // seqs
    groups = width // GROUP_COLS
    bias = pl.BlockSpec((1, GROUP_COLS), lambda s, j, *_: (0, j))
    part = pl.BlockSpec((slots, GROUP_COLS), lambda s, j, *_: (s, j))
    table = jax.ShapeDtypeStruct((total, width), jnp.bfloat16)
    return pl.pallas_call(
        functools.partial(attend_kernel, plan),
        out_shape=[table] * 4
        + [jax.ShapeDtypeStruct((seqs * groups * GROUP_HEADS, slots, slots), jnp.bfloat16)],
        grid_spec=pltpu.PrefetchScalarGridSpec(
            num_scalar_prefetch=2,
            grid=(seqs, groups),
            in_specs=[pl.BlockSpec((slots, width), lambda s, j, *_: (s, 0))]
            + [bias] * 2
            + plan.specs(),
            out_specs=[part] * 4
            + [pl.BlockSpec((GROUP_HEADS, slots, slots), lambda s, j, *_: (s * groups + j, 0, 0))],
            scratch_shapes=[pltpu.VMEM((width, width), jnp.bfloat16)] * 3
            + [pltpu.SemaphoreType.DMA((len(plan.copies),))],
        ),
        compiler_params=kernel_params(),
        cost_estimate=cost((6 * total * width * width + 8 * total * slots * width), 3e7),
        name="attend",
    )(lengths, plan.me, rows, bq, bv, *plan.arrays)


def attend_back_kernel(q, k, v, grad, probs, *refs):
    grads_out, sums_out, held = refs[-3:]
    slots = q.shape[0]
    block = min(256, slots)
    key_turned = k[...].astype(jnp.float32).T.astype(jnp.bfloat16)
    dq_parts = []
    for which in range(GROUP_HEADS // 2):
        pair = slice(which * 128, which * 128 + 128)
        grads, queries, values = grad[:, pair], q[:, pair], v[:, pair]
        dv = dk = None
        for head in (2 * which, 2 * which + 1):
            own_values = one_head(values, head)
            for at in range(0, slots, block):
                cols = slice(at, at + block)
                grad_probs = nt(own_values, grads[cols])
                soft = probs[head, :, cols].astype(jnp.float32)
                inner = jnp.sum(soft * grad_probs, axis=0, keepdims=True)
                held[:, cols] = (soft * (grad_probs - inner)).astype(jnp.bfloat16)
            scores_grad = held[...]
            more_v = nn(probs[head], one_head(grads, head))
            more_k = nn(scores_grad, one_head(queries, head))
            dv = more_v if dv is None else dv + more_v
            dk = more_k if dk is None else dk + more_k
            dq_parts.append(nn(key_turned[head * HEAD_DIM : (head + 1) * HEAD_DIM], scores_grad))
        grads_out[1, :, pair] = dk.astype(jnp.bfloat16)
        grads_out[2, :, pair] = dv.astype(jnp.bfloat16)
    grads_out[0] = (jnp.concatenate(dq_parts).T * 0.125).astype(jnp.bfloat16)
    sums_out[0, 0:1, :] = jnp.sum(grads_out[0].astype(jnp.float32), axis=0, keepdims=True)
    sums_out[0, 1:2, :] = jnp.sum(grads_out[2].astype(jnp.float32), axis=0, keepdims=True)


def attend_back(seqs, seq, q, k, v, grad, probs, before=()):
    total, width = q.shape
    slots = total // seqs
    groups = width // GROUP_COLS
    part = pl.BlockSpec((slots, GROUP_COLS), lambda j: (seq, j))
    return pl.pallas_call(
        attend_back_kernel,
        out_shape=[
            jax.ShapeDtypeStruct((3, total, width), jnp.bfloat16),
            jax.ShapeDtypeStruct((1, 2, width), jnp.float32),
        ],
        grid=(groups,),
        in_specs=[part] * 4
        + [pl.BlockSpec((GROUP_HEADS, slots, slots), lambda j: (seq * groups + j, 0, 0))]
        + [pl.BlockSpec(memory_space=pl.ANY)] * len(before),
        out_specs=[
            pl.BlockSpec((3, slots, GROUP_COLS), lambda j: (0, seq, j)),
            pl.BlockSpec((1, 2, GROUP_COLS), lambda j: (0, 0, j)),
        ],
        scratch_shapes=[pltpu.VMEM((slots, slots), jnp.bfloat16)],
        input_output_aliases={5: 0} if before else {},
        compiler_params=kernel_params(),
        cost_estimate=cost(14 * total * slots * width / seqs, 1.5e7),
    )(q, k, v, grad, probs, *before)


def row_mean(array):
    return jnp.mean(array, -1, keepdims=True)


def feed_kernel(plan, aliased, me, mixed, x, bo, g1, s1, bi, *refs):
    after_out, normed_out, inverse_out, active_out, slope_out, wo, wi, sems = refs[len(plan.arrays) + aliased :]
    first = pl.program_id(0) == 0
    fetch(plan, me[0], refs, (wo, wi), sems, first)
    arrive(plan, me[0], refs, (wo, wi), sems, first, (0,))
    hidden_in = x[...].astype(jnp.float32) + (nn(mixed[...], wo[...]) + bo[...])
    centre = hidden_in - row_mean(hidden_in)
    inverse = lax.rsqrt(row_mean(centre * centre) + NORM_EPS)
    normed = centre * inverse
    after = (normed * g1[...] + s1[...]).astype(jnp.bfloat16)
    normed_out[...] = normed
    inverse_out[...] = jnp.broadcast_to(inverse, inverse_out.shape)
    after_out[...] = after
    arrive(plan, me[0], refs, (wo, wi), sems, first, (1,))
    width = after.shape[1]
    for at in range(0, wi.shape[1], width):
        cols = slice(at, at + width)
        hidden = nn(after, wi[:, cols]) + bi[:, cols]
        cdf = 0.5 * (1.0 + lax.erf(hidden * inverse_root_two))
        density = jnp.exp(-0.5 * hidden * hidden) * inverse_root_tau
        active_out[:, cols] = (hidden * cdf).astype(jnp.bfloat16)
        slope_out[:, cols] = (cdf + hidden * density).astype(jnp.bfloat16)


def whole(array):
    return pl.BlockSpec(array.shape, lambda *_: (0,) * array.ndim, pipeline_mode=pl.Buffered(1))


def by_rows(rows, width):
    return pl.BlockSpec((rows, width), lambda i, *_: (i, 0))


def shape(rows, width, dtype):
    return jax.ShapeDtypeStruct((rows, width), dtype)


def row_blocks(total, parts, part):
    rows = min(256, total // parts)
    steps = total // parts // rows
    spec = lambda width: pl.BlockSpec((rows, width), lambda i, *_: (i + part * steps, 0))
    return rows, steps, spec


ANYWHERE = lambda: pl.BlockSpec(memory_space=pl.ANY)


def feed(parts, part, mixed, x, plan, bo, g1, s1, bi, before=()):
    total, width = x.shape
    wide = bi.shape[1]
    _, steps, spec = row_blocks(total, parts, part)
    bf, f32 = jnp.bfloat16, jnp.float32
    aliases = {7 + len(plan.arrays) + n: n for n in range(len(before))}
    return pl.pallas_call(
        functools.partial(feed_kernel, plan, len(before)),
        out_shape=[
            shape(total, width, bf), shape(total, width, f32), shape(total, 128, f32),
            shape(total, wide, bf), shape(total, wide, bf),
        ],
        grid_spec=pltpu.PrefetchScalarGridSpec(
            num_scalar_prefetch=1,
            grid=(steps,),
            in_specs=[spec(width)] * 2 + [whole(a) for a in (bo, g1, s1, bi)] + plan.specs()
            + [ANYWHERE()] * len(before),
            out_specs=[spec(n) for n in (width, width, 128, wide, wide)],
            scratch_shapes=[
                pltpu.VMEM((width, width), bf), pltpu.VMEM((width, wide), bf),
                pltpu.SemaphoreType.DMA((len(plan.copies),)),
            ],
        ),
        input_output_aliases=aliases,
        compiler_params=kernel_params(),
        cost_estimate=cost(2 * total * width * (width + wide) / parts * 3, 1.5e7),
    )(plan.me, mixed, x, bo, g1, s1, bi, *plan.arrays, *before)


def column_sum(array):
    return jnp.sum(array, axis=0, keepdims=True)


def turn_kernel(plan, slots, lens, me, active, normed1, slope, cot, bb, g1, s1, g2, s2, *refs):
    (
        layer_out, ffn_grad_out, hidden_grad_out, h2_grad_out, sums_out, wide_sums_out, wb, sems,
    ) = refs[len(plan.arrays) :]
    step = pl.program_id(0)
    fetch(plan, me[0], refs, (wb,), sems, step == 0)
    arrive(plan, me[0], refs, (wb,), sems, step == 0)

    @pl.when(step == 0)
    def _():
        sums_out[...] = jnp.zeros_like(sums_out)
        wide_sums_out[...] = jnp.zeros_like(wide_sums_out)

    rows, width = normed1.shape
    after = normed1[...] * g1[...] + s1[...]
    h2 = after + (nn(active[...], wb[...]) + bb[...])
    centre = h2 - row_mean(h2)
    inverse = lax.rsqrt(row_mean(centre * centre) + NORM_EPS)
    normed = centre * inverse
    layer_out[...] = (normed * g2[...] + s2[...]).astype(jnp.bfloat16)
    first = step * rows
    place_in = first % slots + lax.broadcasted_iota(jnp.int32, (rows, 1), 0)
    grad = jnp.where(place_in < lens[first // slots], cot[...].astype(jnp.float32), 0.0)
    scaled = grad * g2[...]
    h2_grad = inverse * (scaled - row_mean(scaled) - normed * row_mean(scaled * normed))
    h2_grad_out[...] = h2_grad
    low = h2_grad.astype(jnp.bfloat16)
    ffn_grad_out[...] = low
    sums_out[0:1, :] += column_sum(grad * normed)
    sums_out[1:2, :] += column_sum(grad)
    sums_out[2:3, :] += column_sum(low.astype(jnp.float32))
    for at in range(0, wb.shape[0], width):
        cols = slice(at, at + width)
        piece = (nt(low, wb[cols, :]) * slope[:, cols].astype(jnp.float32)).astype(jnp.bfloat16)
        hidden_grad_out[:, cols] = piece
        wide_sums_out[:, cols] += column_sum(piece.astype(jnp.float32))


def turn(lengths, slots, active, normed1, slope, cot, plan, bb, g1, s1, g2, s2):
    total, width = normed1.shape
    wide = active.shape[1]
    rows = min(256, slots)
    bf, f32 = jnp.bfloat16, jnp.float32
    fixed = lambda r, n: pl.BlockSpec((r, n), lambda i, *_: (0, 0))
    return pl.pallas_call(
        functools.partial(turn_kernel, plan, slots),
        out_shape=[
            shape(total, width, bf), shape(total, width, bf), shape(total, wide, bf),
            shape(total, width, f32), shape(8, width, f32), shape(1, wide, f32),
        ],
        grid_spec=pltpu.PrefetchScalarGridSpec(
            num_scalar_prefetch=2,
            grid=(total // rows,),
            in_specs=[by_rows(rows, n) for n in (wide, width, wide, width)]
            + [whole(a) for a in (bb, g1, s1, g2, s2)] + plan.specs(),
            out_specs=[by_rows(rows, n) for n in (width, width, wide, width)]
            + [fixed(8, width), fixed(1, wide)],
            scratch_shapes=[pltpu.VMEM((wide, width), bf), pltpu.SemaphoreType.DMA((len(plan.copies),))],
        ),
        compiler_params=kernel_params(),
        cost_estimate=cost(4 * total * width * wide, 3e7),
        name="turn",
    )(lengths, plan.me, active, normed1, slope, cot, bb, g1, s1, g2, s2, *plan.arrays)


def return_kernel(plan, aliased, me, hidden_grad, h2_grad, normed1, inverse1, g1, *refs):
    h1_grad_out, branch_grad_out, mixed_grad_out, sums_out, wo, wi, sems = refs[len(plan.arrays) + aliased :]
    start = pl.program_id(0) == 0
    fetch(plan, me[0], refs, (wo, wi), sems, start)
    arrive(plan, me[0], refs, (wo, wi), sems, start)

    @pl.when(start)
    def _():
        sums_out[...] = jnp.zeros_like(sums_out)

    after_grad = nt(hidden_grad[...], wi[...]) + h2_grad[...]
    normed = normed1[...]
    scaled = after_grad * g1[...]
    h1_grad = inverse1[:, 0:1] * (scaled - row_mean(scaled) - normed * row_mean(scaled * normed))
    h1_grad_out[...] = h1_grad
    low = h1_grad.astype(jnp.bfloat16)
    branch_grad_out[...] = low
    mixed_grad_out[...] = nt(low, wo[...]).astype(jnp.bfloat16)
    sums_out[0:1, :] += column_sum(after_grad * normed)
    sums_out[1:2, :] += column_sum(after_grad)
    sums_out[2:3, :] += column_sum(low.astype(jnp.float32))


def return_grad(parts, part, hidden_grad, h2_grad, normed1, inverse1, plan, g1, before=()):
    total, width = normed1.shape
    wide = hidden_grad.shape[1]
    _, steps, spec = row_blocks(total, parts, part)
    bf, f32 = jnp.bfloat16, jnp.float32
    aliases = {6 + len(plan.arrays) + n: n for n in range(len(before))}
    return pl.pallas_call(
        functools.partial(return_kernel, plan, len(before)),
        out_shape=[
            shape(total, width, f32), shape(total, width, bf), shape(total, width, bf), shape(8, width, f32),
        ],
        grid_spec=pltpu.PrefetchScalarGridSpec(
            num_scalar_prefetch=1,
            grid=(steps,),
            in_specs=[spec(n) for n in (wide, width, width, 128)] + [whole(g1)] + plan.specs()
            + [ANYWHERE()] * len(before),
            out_specs=[spec(width)] * 3 + [pl.BlockSpec((8, width), lambda i, *_: (0, 0))],
            scratch_shapes=[
                pltpu.VMEM((width, width), bf), pltpu.VMEM((width, wide), bf),
                pltpu.SemaphoreType.DMA((len(plan.copies),)),
            ],
        ),
        input_output_aliases=aliases,
        compiler_params=kernel_params(),
        cost_estimate=cost(2 * total * width * (width + wide) / parts, 1.5e7),
    )(plan.me, hidden_grad, h2_grad, normed1, inverse1, g1, *plan.arrays, *before)


def input_kernel(plan, me, h1_grad, grads, *refs):
    out, wq, wk, wv, sems = refs[len(plan.arrays) :]
    start = pl.program_id(0) == 0
    fetch(plan, me[0], refs, (wq, wk, wv), sems, start)
    arrive(plan, me[0], refs, (wq, wk, wv), sems, start)
    total = h1_grad[...] + nt(grads[0], wq[...]) + nt(grads[1], wk[...]) + nt(grads[2], wv[...])
    out[...] = total.astype(jnp.bfloat16)


def input_grad_of(h1_grad, grads, plan):
    total, width = h1_grad.shape
    rows, steps, spec = row_blocks(total, 1, 0)
    return pl.pallas_call(
        functools.partial(input_kernel, plan),
        out_shape=shape(total, width, jnp.bfloat16),
        grid_spec=pltpu.PrefetchScalarGridSpec(
            num_scalar_prefetch=1,
            grid=(steps,),
            in_specs=[spec(width), pl.BlockSpec((3, rows, width), lambda i, *_: (0, i, 0))] + plan.specs(),
            out_specs=spec(width),
            scratch_shapes=[pltpu.VMEM((width, width), jnp.bfloat16)] * 3
            + [pltpu.SemaphoreType.DMA((len(plan.copies),))],
        ),
        compiler_params=kernel_params(),
        cost_estimate=cost(6 * total * width * width, 2e7),
        name="input_grad",
    )(plan.me, h1_grad, grads, *plan.arrays)


def store_chunks(product, me, own, send):
    count = 2 * own.shape[0]
    rows = product.shape[0] // count
    for g in range(count):
        chunk = product[g * rows : (g + 1) * rows].astype(jnp.bfloat16)
        apart = g ^ me

        @pl.when(apart % 2 == 0)
        def _():
            own[apart // 2] = chunk

        @pl.when(apart % 2 == 1)
        def _():
            send[apart // 2] = chunk


def halves(count, rows, blocks, width):
    return [jax.ShapeDtypeStruct((count // 2, rows * blocks, width), jnp.bfloat16)] * 2


def back_weight_kernel(me, active, grad, own, send):
    step = pl.program_id(0)
    product = tn(active[...], grad[...]).astype(jnp.bfloat16)
    half = pl.num_programs(0) // 2

    @pl.when(step < half)
    def _():
        send[0] = product

    @pl.when(step >= half)
    def _():
        own[0] = product


def plain_weight_kernel(me, active, grad, own, send):
    store_chunks(tn(active[...], grad[...]), me[0], own, send)


def back_weight(me, active, grad, count):
    total, wide = active.shape
    width = grad.shape[1]
    rows = wide // count
    half = count // 2
    common = dict(
        out_shape=halves(count, rows, 1, width),
        compiler_params=kernel_params(),
        cost_estimate=cost(2 * total * wide * width, 1.3e7),
        name="back_weight",
    )
    if rows % 128 == 0:
        chunk = lambda t, me: ((2 * (t % half) + 1 - t // half) ^ me[0])
        return pl.pallas_call(
            back_weight_kernel,
            grid_spec=pltpu.PrefetchScalarGridSpec(
                num_scalar_prefetch=1,
                grid=(count,),
                in_specs=[pl.BlockSpec((total, rows), lambda t, me: (0, chunk(t, me))), whole(grad)],
                out_specs=[
                    pl.BlockSpec((1, rows, width), lambda t, me: (jnp.maximum(t - half, 0), 0, 0)),
                    pl.BlockSpec((1, rows, width), lambda t, me: (jnp.minimum(t, half - 1), 0, 0)),
                ],
            ),
            **common,
        )(me, active, grad)
    block = 256
    return pl.pallas_call(
        plain_weight_kernel,
        grid_spec=pltpu.PrefetchScalarGridSpec(
            num_scalar_prefetch=1,
            grid=(width // block,),
            in_specs=[whole(active), pl.BlockSpec((total, block), lambda j, me: (0, j))],
            out_specs=[pl.BlockSpec((half, rows, block), lambda j, me: (0, 0, j))] * 2,
        ),
        **common,
    )(me, active, grad)


def in_out_kernel(me, after, hidden_grad, mixed, branch_grad, own, send):
    last = pl.program_id(0) == pl.num_programs(0) - 1

    @pl.when(jnp.logical_not(last))
    def _():
        store_chunks(tn(after[...], hidden_grad[...]), me[0], own, send)

    @pl.when(last)
    def _():
        store_chunks(tn(mixed[...], branch_grad[...]), me[0], own, send)


def in_out_weight(me, after, hidden_grad, mixed, branch_grad, count):
    total, width = after.shape
    blocks = hidden_grad.shape[1] // width
    rows = width // count
    return pl.pallas_call(
        in_out_kernel,
        out_shape=halves(count, rows, blocks + 1, width),
        grid_spec=pltpu.PrefetchScalarGridSpec(
            num_scalar_prefetch=1,
            grid=(blocks + 1,),
            in_specs=[
                whole(after),
                pl.BlockSpec((total, width), lambda j, me: (0, jnp.minimum(j, blocks - 1))),
                whole(mixed),
                whole(branch_grad),
            ],
            out_specs=[pl.BlockSpec((count // 2, rows, width), lambda j, me: (0, j, 0))] * 2,
        ),
        compiler_params=kernel_params(),
        cost_estimate=cost(2 * total * width * width * (blocks + 1), 2e7),
        name="in_out_weight",
    )(me, after, hidden_grad, mixed, branch_grad)


SMALL_ROWS = 16


def row_stride(chunk):
    return -(-chunk // 16) * 16


def small_tile(vectors, wide, g, count, width):
    size, wide_size = width // count, wide.shape[1] // count
    part = slice(g * size, (g + 1) * size)
    tops = [ref[rows, part] for ref, rows in vectors]
    fill = lambda rows, used: jnp.zeros((rows, width - used), jnp.float32)
    top = jnp.concatenate(tops, axis=0)
    eight = jnp.concatenate([top, fill(8, size)], axis=1)
    last = jnp.concatenate([wide[:, g * wide_size : (g + 1) * wide_size], fill(1, wide_size)], axis=1)
    return jnp.concatenate([eight, last, jnp.zeros((7, width), jnp.float32)], axis=0).astype(jnp.bfloat16)


def qkv_weight_kernel(me, rows, grads, attend_sums, sums1, sums2, wide, own, send):
    step = pl.program_id(0)
    count, width = 2 * own.shape[0], own.shape[2]
    chunk = width // count
    stride = row_stride(chunk)
    product = tn(rows[...], grads[0])

    def keep(g, first, value):
        apart = g ^ me[0]
        size = value.shape[0]

        @pl.when(apart % 2 == 0)
        def _():
            own[apart // 2, first : first + size] = value

        @pl.when(apart % 2 == 1)
        def _():
            send[apart // 2, first : first + size] = value

    for n in range(3):

        @pl.when(step == n)
        def _():
            for g in range(count):
                keep(g, n * stride, product[g * chunk : (g + 1) * chunk].astype(jnp.bfloat16))

    @pl.when(step == 0)
    def _():
        vectors = (
            (attend_sums, slice(0, 2)), (sums1, slice(2, 3)), (sums2, slice(2, 3)),
            (sums1, slice(0, 2)), (sums2, slice(0, 2)),
        )
        for g in range(count):
            keep(g, 3 * stride, small_tile(vectors, wide, g, count, width))


def qkv_weight(me, rows, grads, attend_sums, sums1, sums2, wide, count):
    total, width = rows.shape
    tall = 3 * row_stride(width // count) + SMALL_ROWS
    block = pl.BlockSpec((count // 2, tall, width), lambda j, me: (0, 0, 0))
    return pl.pallas_call(
        qkv_weight_kernel,
        out_shape=halves(count, tall, 1, width),
        grid_spec=pltpu.PrefetchScalarGridSpec(
            num_scalar_prefetch=1,
            grid=(3,),
            in_specs=[whole(rows), pl.BlockSpec((1, total, width), lambda j, me: (j, 0, 0))]
            + [whole(a) for a in (attend_sums, sums1, sums2, wide)],
            out_specs=[block] * 2,
        ),
        compiler_params=kernel_params(),
        cost_estimate=cost(6 * total * width * width, 1e7),
        name="qkv_weight",
    )(me, rows, grads, attend_sums, sums1, sums2, wide)


def deliver_kernel(odd, kept, other, *outs):
    first, second = kept[...].astype(jnp.float32), other[...].astype(jnp.float32)
    swap = odd[0] == 1
    both = jnp.concatenate([jnp.where(swap, second, first), jnp.where(swap, first, second)], axis=0)
    chunk = outs[0].shape[0]
    stride = row_stride(chunk)
    for n in range(3):
        outs[n][...] = both[n * stride : n * stride + chunk]
    for n, out in enumerate(outs[3:]):
        out[...] = both[3 * stride + n, 0 : out.shape[0]]


def deliver(odd, kept, other, chunk, wide_chunk):
    width = kept.shape[1]
    sizes = [chunk] * 8 + [wide_chunk]
    return pl.pallas_call(
        deliver_kernel,
        out_shape=[shape(chunk, width, jnp.float32)] * 3
        + [jax.ShapeDtypeStruct((n,), jnp.float32) for n in sizes],
        in_specs=[SMEM(), VMEM(), VMEM()],
        out_specs=[VMEM()] * 12,
        compiler_params=kernel_params(),
        name="deliver",
    )(odd, kept, other)


def split_add_kernel(own, received, keep_x, away_x, keep_y, away_y):
    slot = pl.program_id(0)
    total = (own[0].astype(jnp.float32) + received[0].astype(jnp.float32)).astype(jnp.bfloat16)
    half = keep_x.shape[1]
    top, bottom = total[:half], total[half:]

    @pl.when(slot % 2 == 0)
    def _():
        keep_x[0] = top

    @pl.when(slot % 2 == 1)
    def _():
        away_x[0] = top

    @pl.when(slot < 2)
    def _():
        keep_y[0] = bottom

    @pl.when(slot >= 2)
    def _():
        away_y[0] = bottom


def split_add(own, received, half):
    _, rows, width = own.shape
    block = lambda n, where: pl.BlockSpec((1, n, width), lambda s: (where(s), 0, 0))
    table = lambda n: jax.ShapeDtypeStruct((2, n, width), jnp.bfloat16)
    return pl.pallas_call(
        split_add_kernel,
        out_shape=[table(half)] * 2 + [table(rows - half)] * 2,
        grid=(4,),
        in_specs=[block(rows, lambda s: s)] * 2,
        out_specs=[
            block(half, lambda s: s // 2), block(half, lambda s: s // 2),
            block(rows - half, lambda s: jnp.minimum(s, 1)), block(rows - half, lambda s: jnp.maximum(s - 2, 0)),
        ],
        compiler_params=kernel_params(),
        name="split_add",
    )(own, received)


def pack_kernel(*refs):
    out = refs[-1]
    out[...] = jnp.zeros_like(out)
    at = 0
    for ref in refs[:-1]:
        size = ref.shape[1]
        for first in range(0, size, 128):
            n = min(128, size - first)
            out[at : at + 1, 0:n] = ref[:, first : first + n].astype(jnp.float32)
            at += 1


def spread_kernel(me, table, vectors_out, wide_out):
    count = table.shape[0]
    chunk = vectors_out.shape[1] // count
    wide_chunk = wide_out.shape[1] // count
    for g in range(count):
        tile = table[g ^ me[0]]
        vectors_out[:, g * chunk : (g + 1) * chunk] = tile[0:8, 0:chunk]
        for n, first in enumerate(range(0, wide_chunk, 128)):
            size = min(128, wide_chunk - first)
            wide_out[:, g * wide_chunk + first : g * wide_chunk + first + size] = tile[8 + n : 9 + n, 0:size]


SMEM = lambda: pl.BlockSpec(memory_space=pltpu.SMEM)
VMEM = lambda: pl.BlockSpec(memory_space=pltpu.VMEM)


def pack(vectors):
    return pl.pallas_call(
        pack_kernel, out_shape=shape(16, 128, jnp.float32), in_specs=[VMEM()] * len(vectors), out_specs=VMEM(),
        compiler_params=kernel_params(), name="pack",
    )(*[v.reshape(1, -1) for v in vectors])


def spread(me, table, width, wide):
    return pl.pallas_call(
        spread_kernel, out_shape=[shape(8, width, jnp.float32), shape(1, wide, jnp.float32)],
        in_specs=[SMEM(), VMEM()], out_specs=[VMEM()] * 2, compiler_params=kernel_params(), name="spread",
    )(me, table)


def per_device(
    inputs, cotangent, lengths,
    query_weight, key_weight, value_weight, out_weight, in_weight, back_weight_shard,
    query_bias, value_bias, out_bias, in_bias, back_bias,
    first_gain, first_shift, second_gain, second_shift,
):
    index = lax.axis_index("group")
    me = index.reshape(1).astype(jnp.int32)
    count = lax.axis_size("group")
    bits = count.bit_length() - 1
    seqs, slots, width = inputs.shape
    total = seqs * slots
    chunk = query_weight.shape[0]
    wide = in_weight.shape[1]
    blocks = wide // width
    x = inputs.reshape(total, width)
    cot = cotangent.reshape(total, width)

    in_blocks = [in_weight[:, n * width : (n + 1) * width] for n in range(blocks)]
    got_a, far_a = gather_group(jnp.concatenate([query_weight, key_weight, value_weight]), bits, ())
    table = pack(
        [query_bias, value_bias, out_bias, back_bias, first_gain, first_shift, second_gain, second_shift, in_bias]
    )[None]
    for b in range(bits - 1, -1, -1):
        other = swap_with(table, 1 << b)
        table = jnp.stack([table, other], axis=1).reshape((-1,) + table.shape[1:])
    got_b, far_b = gather_group(jnp.concatenate([out_weight] + in_blocks), bits, far_a + [table])
    vectors, bi = spread(me, table, width, wide)
    bq, bv, bo, bb, g1, s1, g2, s2 = (vectors[i : i + 1] for i in range(8))
    third = [(n, n * chunk, chunk, 0) for n in range(3)]
    plan_a = Gathered(got_a, me, count, chunk, third)
    plan_b = Gathered(
        got_b, me, count, chunk,
        [(0, 0, chunk, 0)] + [(1, (n + 1) * chunk, chunk, n * width) for n in range(blocks)],
    )
    q, k, v, mixed, probs = attend(lengths, x, plan_a, bq, bv)
    back_chunk = back_weight_shard.shape[0]
    got_c, _ = gather_group(back_weight_shard, bits, far_b + [mixed])
    plan_c = Gathered(got_c, me, count, back_chunk, [(0, 0, back_chunk, 0)])
    after_low, normed1, inverse1, active, slope = feed(1, 0, mixed, x, plan_b, bo, g1, s1, bi)
    layer_out, ffn_grad, hidden_grad, h2_grad, sums2, in_bias_sum = turn(
        lengths, slots, active, normed1, slope, cot, plan_c, bb, g1, s1, g2, s2
    )
    own, send = back_weight(me, active, ffn_grad, count)
    hidden_grad, send = lax.optimization_barrier((hidden_grad, send))
    red_c = reduction(own, send, bits)
    came = next(red_c)
    h1_grad, branch_grad, mixed_grad, sums1 = return_grad(
        1, 0, hidden_grad, h2_grad, normed1, inverse1, plan_b, g1
    )
    branch_grad = after(branch_grad, *came)
    came = next(red_c)
    own, send = in_out_weight(me, after_low, hidden_grad, mixed, branch_grad, count)
    red_b = reduction(own, send, bits)
    mixed_grad = after(mixed_grad, send, *came)
    came, came_b = next(red_c), next(red_b)
    grads, sums_at = attend_back(seqs, 0, q, k, v, mixed_grad, probs)
    attend_sums = sums_at[0]
    for seq in range(1, seqs):
        mixed_grad = after(mixed_grad, attend_sums, *came, *came_b)
        came, came_b = next(red_c), next(red_b)
        grads, sums_at = attend_back(seqs, seq, q, k, v, mixed_grad, probs, (grads,))
        attend_sums = attend_sums + sums_at[0]
    rows_in = after(x, *came, *came_b)
    came, came_b = next(red_c), next(red_b)
    own, send = qkv_weight(me, rows_in, grads, attend_sums, sums1, sums2, in_bias_sum, count)
    red_a = reduction(own, send, bits)
    came_a = next(red_a)
    h1_in = after(h1_grad, *came, *came_b, *came_a)
    came, came_b, came_a = next(red_c), next(red_b), next(red_a)
    input_grad = input_grad_of(h1_in, grads, plan_a)
    odd = lax.axis_index("replica") & 1
    sum_c, sum_b = (in_order(odd, *finish(steps)) for steps in (red_c, red_b))
    (
        grad_wq, grad_wk, grad_wv, grad_q, grad_v, grad_o, grad_b, grad_g1, grad_s1, grad_g2, grad_s2, grad_i,
    ) = deliver(odd.reshape(1), *finish(red_a), chunk, wide // count)
    up = lambda a: a.astype(jnp.float32)
    in_sum = jnp.concatenate([sum_b[n * chunk : (n + 1) * chunk] for n in range(blocks)], axis=1)
    return (
        layer_out.reshape(inputs.shape), input_grad.reshape(inputs.shape),
        grad_wq, grad_wk, grad_wv,
        up(sum_b[blocks * chunk :]), up(in_sum), up(sum_c),
        grad_q, grad_v, grad_o, grad_i, grad_b, grad_g1, grad_s1, grad_g2, grad_s2,
    )


def solution(mesh):
    return jax.shard_map(
        per_device,
        mesh=mesh,
        in_specs=(
            P(("group", "replica"), None, None),
            P(("group", "replica"), None, None),
            P(("group", "replica")),
            P("group", None),
            P("group", None),
            P("group", None),
            P("group", None),
            P("group", None),
            P("group", None),
            P("group"),
            P("group"),
            P("group"),
            P("group"),
            P("group"),
            P("group"),
            P("group"),
            P("group"),
            P("group"),
        ),
        out_specs=(
            P(("group", "replica"), None, None),
            P(("group", "replica"), None, None),
            P("group", None),
            P("group", None),
            P("group", None),
            P("group", None),
            P("group", None),
            P("group", None),
            P("group"),
            P("group"),
            P("group"),
            P("group"),
            P("group"),
            P("group"),
            P("group"),
            P("group"),
            P("group"),
        ),
        check_vma=False,
    )
```

```python
import functools

import jax
import jax.numpy as jnp
from jax import lax
from jax.experimental import pallas as pl
from jax.experimental.pallas import tpu as pltpu
from jax.sharding import PartitionSpec as P

HEAD_DIM = 64


NORM_EPS = 1e-12
inverse_root_two = 0.7071067811865476
inverse_root_tau = 0.3989422804014327


AXES = ("group", "replica")


def swap_with(array, group_mask, replica_mask=0):
    groups, replicas = lax.axis_size("group"), lax.axis_size("replica")
    pairs = [
        (g * replicas + r, (g ^ group_mask) * replicas + (r ^ replica_mask))
        for g in range(groups)
        for r in range(replicas)
    ]
    return lax.ppermute(array, AXES, pairs)


def after(array, *others):
    return lax.optimization_barrier((array,) + others)[0] if others else array


def gather_group(shard, bits, wait_for):
    shard = after(shard, *wait_for)
    pieces = {0: [shard]}
    for d in range(2, 1 << bits, 2):
        pieces[d] = [swap_with(shard, d)]
    far = [pieces[d][0] for d in range(2, 1 << bits, 2)]
    for d in list(pieces):
        pieces[d | 1] = [swap_with(p, 1) for p in pieces[d]]
    return pieces, far


def place(pieces, me, group_size):
    rows = sum(p.shape[0] for p in pieces[0])
    full = jnp.zeros((group_size, rows, pieces[0][0].shape[1]), jnp.bfloat16)
    for d, parts in pieces.items():
        at = 0
        for part in parts:
            full = lax.dynamic_update_slice(full, part[None], (me ^ d, at, 0))
            at += part.shape[0]
    return full


def pick(array, axis, index):
    return lax.dynamic_index_in_dim(array, index, axis, keepdims=False)


def add_low(left, right):
    return (left.astype(jnp.float32) + right.astype(jnp.float32)).astype(jnp.bfloat16)


def reduction(own, send, bits):
    received = swap_with(send, 1)
    yield [received]
    rows, width = own.shape[1:]
    half = rows // 32 * 16
    lefts = [list(range(1, bits)), list(range(1, bits))]
    chunks = add_low(own, received).reshape((2,) * (bits - 1) + (rows, width))
    parts = [chunks[..., :half, :], chunks[..., half:, :]]
    for _ in range(1, bits):
        kept, received = [], []
        for n, (left, end) in enumerate(zip(lefts, (0, -1))):
            b = left[end]
            axis = len(left) - 1 - left.index(b)
            keep, away = (lax.index_in_dim(parts[n], i, axis, keepdims=False) for i in (0, 1))
            kept.append(keep)
            received.append(swap_with(away, 1 << b))
            left.remove(b)
        yield received
        parts = [add_low(keep, got) for keep, got in zip(kept, received)]
    total = jnp.concatenate(parts)
    at = lax.axis_index("replica")
    pair = total.reshape(2, rows // 2, width)
    if lax.axis_size("replica") == 1:
        yield pair[0], pair[1]
        return
    received = swap_with(pick(pair, 0, 1 - (at & 1)), 0, 1)
    yield [received]
    kept = add_low(pick(pair, 0, at & 1), received)
    mask = 2
    while mask < lax.axis_size("replica"):
        received = swap_with(kept, 0, mask)
        wait_for = yield [received]
        received = after(received, *(wait_for or ()))
        kept = add_low(kept, received)
        mask *= 2
    other = swap_with(kept, 0, 1)
    yield [other]
    yield kept, other


def in_order(odd, kept, other):
    return jnp.where(odd, jnp.concatenate([other, kept]), jnp.concatenate([kept, other]))


def finish(steps):
    *_, last = steps
    return last


class Gathered:
    def __init__(self, pieces, me, count, chunk, segments):
        self.me, self.chunk = me, chunk
        self.arrays, self.copies = [], []
        if chunk % 16:
            full = place(pieces, me[0], count)
            self.plain(full, count, segments)
            return
        for d, parts in pieces.items():
            at = 0
            for part in parts:
                for target, low, size, column in segments:
                    start, stop = max(at, low), min(at + part.shape[0], low + size)
                    if start < stop:
                        self.copies.append(
                            (len(self.arrays), start - at, stop - start, target, d, start - low, column)
                        )
                self.arrays.append(part)
                at += part.shape[0]
        self.fixed = False

    def plain(self, full, count, segments):
        width = full.shape[2]
        for target, low, size, column in segments:
            self.copies.append((len(self.arrays), 0, count * size, target, 0, 0, column))
            self.arrays.append(full[:, low : low + size].reshape(count * size, width))
        self.fixed = True

    def specs(self):
        return [pl.BlockSpec(memory_space=pl.ANY)] * len(self.arrays)

    def transfers(self, me, refs, targets, sems, only=None):
        out = []
        for n, (which, row, rows, target, d, inner, column) in enumerate(self.copies):
            if only is not None and target not in only:
                continue
            size = self.chunk
            if self.fixed:
                first = 0
            else:
                first = pl.multiple_of((me ^ d) * size + inner, 16)
            width = self.arrays[which].shape[1]
            out.append(
                pltpu.make_async_copy(
                    refs[which].at[pl.ds(row, rows)],
                    targets[target].at[pl.ds(first, rows), pl.ds(column, width)],
                    sems.at[n],
                )
            )
        return out


def fetch(plan, me, refs, targets, sems, first_step, only=None):
    @pl.when(first_step)
    def _():
        for copy in plan.transfers(me, refs, targets, sems, only):
            copy.start()


def arrive(plan, me, refs, targets, sems, first_step, only=None):
    @pl.when(first_step)
    def _():
        for copy in plan.transfers(me, refs, targets, sems, only):
            copy.wait()


VMEM_LIMIT = 60 * 1024 * 1024
GROUP_HEADS = 4
GROUP_COLS = GROUP_HEADS * HEAD_DIM


def nt(left, right):
    return lax.dot_general(left, right, (((1,), (1,)), ((), ())), preferred_element_type=jnp.float32)


def nn(left, right):
    return lax.dot_general(left, right, (((1,), (0,)), ((), ())), preferred_element_type=jnp.float32)


def tn(left, right):
    return lax.dot_general(left, right, (((0,), (0,)), ((), ())), preferred_element_type=jnp.float32)


def kernel_params(**more):
    return pltpu.CompilerParams(vmem_limit_bytes=VMEM_LIMIT, **more)


def cost(flops, moved):
    return pl.CostEstimate(flops=int(flops), bytes_accessed=int(moved), transcendentals=0)


def one_head(pair, head):
    lanes = lax.broadcasted_iota(jnp.int32, pair.shape, 1)
    keep = lanes < HEAD_DIM if head % 2 == 0 else lanes >= HEAD_DIM
    return jnp.where(keep, pair, jnp.zeros_like(pair))


def attend_kernel(plan, lens, me, x, bq, bv, *refs):
    q_out, k_out, v_out, mixed_out, probs_out, wq, wk, wv, sems = refs[len(plan.arrays) :]
    seq, group = pl.program_id(0), pl.program_id(1)
    start = jnp.logical_and(seq == 0, group == 0)
    fetch(plan, me[0], refs, (wq, wk, wv), sems, start)
    arrive(plan, me[0], refs, (wq, wk, wv), sems, start)
    cols = pl.ds(pl.multiple_of(group * GROUP_COLS, GROUP_COLS), GROUP_COLS)
    slots = x.shape[0]
    rows = x[...]
    q = ((nn(rows, wq[:, cols]) + bq[...]).astype(jnp.bfloat16) * 0.125).astype(jnp.bfloat16)
    k = nn(rows, wk[:, cols]).astype(jnp.bfloat16)
    v = (nn(rows, wv[:, cols]) + bv[...]).astype(jnp.bfloat16)
    q_out[...] = q
    k_out[...] = k
    v_out[...] = v
    turned = v.astype(jnp.float32).T.astype(jnp.bfloat16)
    valid = lax.broadcasted_iota(jnp.int32, (slots, 1), 0) < lens[seq]
    block = min(256, slots)
    for head in range(GROUP_HEADS):
        pair = slice(head // 2 * 128, head // 2 * 128 + 128)
        keys = one_head(k[:, pair], head)
        for at in range(0, slots, block):
            scores = nt(keys, q[at : at + block, pair])
            scores = jnp.where(valid, scores, -1e30)
            lifted = jnp.exp(scores - jnp.max(scores, axis=0, keepdims=True))
            share = 1.0 / jnp.sum(lifted, axis=0, keepdims=True)
            probs_out[head, :, at : at + block] = (lifted * share).astype(jnp.bfloat16)
    joined = jnp.concatenate(
        [
            nn(turned[h * HEAD_DIM : (h + 1) * HEAD_DIM], probs_out[h])
            for h in range(GROUP_HEADS)
        ]
    )
    mixed_out[...] = joined.T.astype(jnp.bfloat16)


def attend(lengths, rows, plan, bq, bv):
    seqs = lengths.shape[0]
    total, width = rows.shape
    slots = total // seqs
    groups = width // GROUP_COLS
    bias = pl.BlockSpec((1, GROUP_COLS), lambda s, j, *_: (0, j))
    part = pl.BlockSpec((slots, GROUP_COLS), lambda s, j, *_: (s, j))
    table = jax.ShapeDtypeStruct((total, width), jnp.bfloat16)
    return pl.pallas_call(
        functools.partial(attend_kernel, plan),
        out_shape=[table] * 4
        + [jax.ShapeDtypeStruct((seqs * groups * GROUP_HEADS, slots, slots), jnp.bfloat16)],
        grid_spec=pltpu.PrefetchScalarGridSpec(
            num_scalar_prefetch=2,
            grid=(seqs, groups),
            in_specs=[pl.BlockSpec((slots, width), lambda s, j, *_: (s, 0))]
            + [bias] * 2
            + plan.specs(),
            out_specs=[part] * 4
            + [pl.BlockSpec((GROUP_HEADS, slots, slots), lambda s, j, *_: (s * groups + j, 0, 0))],
            scratch_shapes=[pltpu.VMEM((width, width), jnp.bfloat16)] * 3
            + [pltpu.SemaphoreType.DMA((len(plan.copies),))],
        ),
        compiler_params=kernel_params(),
        cost_estimate=cost((6 * total * width * width + 8 * total * slots * width), 3e7),
        name="attend",
    )(lengths, plan.me, rows, bq, bv, *plan.arrays)


def attend_back_kernel(q, k, v, grad, probs, *refs):
    grads_out, sums_out, held = refs[-3:]
    slots = q.shape[0]
    block = min(256, slots)
    key_turned = k[...].astype(jnp.float32).T.astype(jnp.bfloat16)
    dq_parts = []
    for which in range(GROUP_HEADS // 2):
        pair = slice(which * 128, which * 128 + 128)
        grads, queries, values = grad[:, pair], q[:, pair], v[:, pair]
        dv = dk = None
        for head in (2 * which, 2 * which + 1):
            own_values = one_head(values, head)
            for at in range(0, slots, block):
                cols = slice(at, at + block)
                grad_probs = nt(own_values, grads[cols])
                soft = probs[head, :, cols].astype(jnp.float32)
                inner = jnp.sum(soft * grad_probs, axis=0, keepdims=True)
                held[:, cols] = (soft * (grad_probs - inner)).astype(jnp.bfloat16)
            scores_grad = held[...]
            more_v = nn(probs[head], one_head(grads, head))
            more_k = nn(scores_grad, one_head(queries, head))
            dv = more_v if dv is None else dv + more_v
            dk = more_k if dk is None else dk + more_k
            dq_parts.append(nn(key_turned[head * HEAD_DIM : (head + 1) * HEAD_DIM], scores_grad))
        grads_out[1, :, pair] = dk.astype(jnp.bfloat16)
        grads_out[2, :, pair] = dv.astype(jnp.bfloat16)
    grads_out[0] = (jnp.concatenate(dq_parts).T * 0.125).astype(jnp.bfloat16)
    sums_out[0, 0:1, :] = jnp.sum(grads_out[0].astype(jnp.float32), axis=0, keepdims=True)
    sums_out[0, 1:2, :] = jnp.sum(grads_out[2].astype(jnp.float32), axis=0, keepdims=True)


def attend_back(seqs, seq, q, k, v, grad, probs, before=()):
    total, width = q.shape
    slots = total // seqs
    groups = width // GROUP_COLS
    part = pl.BlockSpec((slots, GROUP_COLS), lambda j: (seq, j))
    return pl.pallas_call(
        attend_back_kernel,
        out_shape=[
            jax.ShapeDtypeStruct((3, total, width), jnp.bfloat16),
            jax.ShapeDtypeStruct((1, 2, width), jnp.float32),
        ],
        grid=(groups,),
        in_specs=[part] * 4
        + [pl.BlockSpec((GROUP_HEADS, slots, slots), lambda j: (seq * groups + j, 0, 0))]
        + [pl.BlockSpec(memory_space=pl.ANY)] * len(before),
        out_specs=[
            pl.BlockSpec((3, slots, GROUP_COLS), lambda j: (0, seq, j)),
            pl.BlockSpec((1, 2, GROUP_COLS), lambda j: (0, 0, j)),
        ],
        scratch_shapes=[pltpu.VMEM((slots, slots), jnp.bfloat16)],
        input_output_aliases={5: 0} if before else {},
        compiler_params=kernel_params(),
        cost_estimate=cost(14 * total * slots * width / seqs, 1.5e7),
    )(q, k, v, grad, probs, *before)


def row_mean(array):
    return jnp.mean(array, -1, keepdims=True)


def feed_kernel(plan, aliased, me, mixed, x, bo, g1, s1, bi, *refs):
    after_out, normed_out, inverse_out, active_out, slope_out, wo, wi, sems = refs[len(plan.arrays) + aliased :]
    first = pl.program_id(0) == 0
    fetch(plan, me[0], refs, (wo, wi), sems, first)
    arrive(plan, me[0], refs, (wo, wi), sems, first, (0,))
    hidden_in = x[...].astype(jnp.float32) + (nn(mixed[...], wo[...]) + bo[...])
    centre = hidden_in - row_mean(hidden_in)
    inverse = lax.rsqrt(row_mean(centre * centre) + NORM_EPS)
    normed = centre * inverse
    after = (normed * g1[...] + s1[...]).astype(jnp.bfloat16)
    normed_out[...] = normed
    inverse_out[...] = jnp.broadcast_to(inverse, inverse_out.shape)
    after_out[...] = after
    arrive(plan, me[0], refs, (wo, wi), sems, first, (1,))
    width = after.shape[1]
    for at in range(0, wi.shape[1], width):
        cols = slice(at, at + width)
        hidden = nn(after, wi[:, cols]) + bi[:, cols]
        cdf = 0.5 * (1.0 + lax.erf(hidden * inverse_root_two))
        density = jnp.exp(-0.5 * hidden * hidden) * inverse_root_tau
        active_out[:, cols] = (hidden * cdf).astype(jnp.bfloat16)
        slope_out[:, cols] = (cdf + hidden * density).astype(jnp.bfloat16)


def whole(array):
    return pl.BlockSpec(array.shape, lambda *_: (0,) * array.ndim, pipeline_mode=pl.Buffered(1))


def by_rows(rows, width):
    return pl.BlockSpec((rows, width), lambda i, *_: (i, 0))


def shape(rows, width, dtype):
    return jax.ShapeDtypeStruct((rows, width), dtype)


def row_blocks(total, parts, part):
    rows = min(256, total // parts)
    steps = total // parts // rows
    spec = lambda width: pl.BlockSpec((rows, width), lambda i, *_: (i + part * steps, 0))
    return rows, steps, spec


ANYWHERE = lambda: pl.BlockSpec(memory_space=pl.ANY)


def feed(parts, part, mixed, x, plan, bo, g1, s1, bi, before=()):
    total, width = x.shape
    wide = bi.shape[1]
    _, steps, spec = row_blocks(total, parts, part)
    bf, f32 = jnp.bfloat16, jnp.float32
    aliases = {7 + len(plan.arrays) + n: n for n in range(len(before))}
    return pl.pallas_call(
        functools.partial(feed_kernel, plan, len(before)),
        out_shape=[
            shape(total, width, bf), shape(total, width, f32), shape(total, 128, f32),
            shape(total, wide, bf), shape(total, wide, bf),
        ],
        grid_spec=pltpu.PrefetchScalarGridSpec(
            num_scalar_prefetch=1,
            grid=(steps,),
            in_specs=[spec(width)] * 2 + [whole(a) for a in (bo, g1, s1, bi)] + plan.specs()
            + [ANYWHERE()] * len(before),
            out_specs=[spec(n) for n in (width, width, 128, wide, wide)],
            scratch_shapes=[
                pltpu.VMEM((width, width), bf), pltpu.VMEM((width, wide), bf),
                pltpu.SemaphoreType.DMA((len(plan.copies),)),
            ],
        ),
        input_output_aliases=aliases,
        compiler_params=kernel_params(),
        cost_estimate=cost(2 * total * width * (width + wide) / parts * 3, 1.5e7),
    )(plan.me, mixed, x, bo, g1, s1, bi, *plan.arrays, *before)


def column_sum(array):
    return jnp.sum(array, axis=0, keepdims=True)


def turn_kernel(plan, slots, lens, me, active, normed1, slope, cot, bb, g1, s1, g2, s2, *refs):
    (
        layer_out, ffn_grad_out, hidden_grad_out, h2_grad_out, sums_out, wide_sums_out, wb, sems,
    ) = refs[len(plan.arrays) :]
    step = pl.program_id(0)
    fetch(plan, me[0], refs, (wb,), sems, step == 0)
    arrive(plan, me[0], refs, (wb,), sems, step == 0)

    @pl.when(step == 0)
    def _():
        sums_out[...] = jnp.zeros_like(sums_out)
        wide_sums_out[...] = jnp.zeros_like(wide_sums_out)

    rows, width = normed1.shape
    after = normed1[...] * g1[...] + s1[...]
    h2 = after + (nn(active[...], wb[...]) + bb[...])
    centre = h2 - row_mean(h2)
    inverse = lax.rsqrt(row_mean(centre * centre) + NORM_EPS)
    normed = centre * inverse
    layer_out[...] = (normed * g2[...] + s2[...]).astype(jnp.bfloat16)
    first = step * rows
    place_in = first % slots + lax.broadcasted_iota(jnp.int32, (rows, 1), 0)
    grad = jnp.where(place_in < lens[first // slots], cot[...].astype(jnp.float32), 0.0)
    scaled = grad * g2[...]
    h2_grad = inverse * (scaled - row_mean(scaled) - normed * row_mean(scaled * normed))
    h2_grad_out[...] = h2_grad
    low = h2_grad.astype(jnp.bfloat16)
    ffn_grad_out[...] = low
    sums_out[0:1, :] += column_sum(grad * normed)
    sums_out[1:2, :] += column_sum(grad)
    sums_out[2:3, :] += column_sum(low.astype(jnp.float32))
    for at in range(0, wb.shape[0], width):
        cols = slice(at, at + width)
        piece = (nt(low, wb[cols, :]) * slope[:, cols].astype(jnp.float32)).astype(jnp.bfloat16)
        hidden_grad_out[:, cols] = piece
        wide_sums_out[:, cols] += column_sum(piece.astype(jnp.float32))


def turn(lengths, slots, active, normed1, slope, cot, plan, bb, g1, s1, g2, s2):
    total, width = normed1.shape
    wide = active.shape[1]
    rows = min(256, slots)
    bf, f32 = jnp.bfloat16, jnp.float32
    fixed = lambda r, n: pl.BlockSpec((r, n), lambda i, *_: (0, 0))
    return pl.pallas_call(
        functools.partial(turn_kernel, plan, slots),
        out_shape=[
            shape(total, width, bf), shape(total, width, bf), shape(total, wide, bf),
            shape(total, width, f32), shape(8, width, f32), shape(1, wide, f32),
        ],
        grid_spec=pltpu.PrefetchScalarGridSpec(
            num_scalar_prefetch=2,
            grid=(total // rows,),
            in_specs=[by_rows(rows, n) for n in (wide, width, wide, width)]
            + [whole(a) for a in (bb, g1, s1, g2, s2)] + plan.specs(),
            out_specs=[by_rows(rows, n) for n in (width, width, wide, width)]
            + [fixed(8, width), fixed(1, wide)],
            scratch_shapes=[pltpu.VMEM((wide, width), bf), pltpu.SemaphoreType.DMA((len(plan.copies),))],
        ),
        compiler_params=kernel_params(),
        cost_estimate=cost(4 * total * width * wide, 3e7),
        name="turn",
    )(lengths, plan.me, active, normed1, slope, cot, bb, g1, s1, g2, s2, *plan.arrays)


def return_kernel(plan, aliased, me, hidden_grad, h2_grad, normed1, inverse1, g1, *refs):
    h1_grad_out, branch_grad_out, mixed_grad_out, sums_out, wo, wi, sems = refs[len(plan.arrays) + aliased :]
    start = pl.program_id(0) == 0
    fetch(plan, me[0], refs, (wo, wi), sems, start)
    arrive(plan, me[0], refs, (wo, wi), sems, start)

    @pl.when(start)
    def _():
        sums_out[...] = jnp.zeros_like(sums_out)

    after_grad = nt(hidden_grad[...], wi[...]) + h2_grad[...]
    normed = normed1[...]
    scaled = after_grad * g1[...]
    h1_grad = inverse1[:, 0:1] * (scaled - row_mean(scaled) - normed * row_mean(scaled * normed))
    h1_grad_out[...] = h1_grad
    low = h1_grad.astype(jnp.bfloat16)
    branch_grad_out[...] = low
    mixed_grad_out[...] = nt(low, wo[...]).astype(jnp.bfloat16)
    sums_out[0:1, :] += column_sum(after_grad * normed)
    sums_out[1:2, :] += column_sum(after_grad)
    sums_out[2:3, :] += column_sum(low.astype(jnp.float32))


def return_grad(parts, part, hidden_grad, h2_grad, normed1, inverse1, plan, g1, before=()):
    total, width = normed1.shape
    wide = hidden_grad.shape[1]
    _, steps, spec = row_blocks(total, parts, part)
    bf, f32 = jnp.bfloat16, jnp.float32
    aliases = {6 + len(plan.arrays) + n: n for n in range(len(before))}
    return pl.pallas_call(
        functools.partial(return_kernel, plan, len(before)),
        out_shape=[
            shape(total, width, f32), shape(total, width, bf), shape(total, width, bf), shape(8, width, f32),
        ],
        grid_spec=pltpu.PrefetchScalarGridSpec(
            num_scalar_prefetch=1,
            grid=(steps,),
            in_specs=[spec(n) for n in (wide, width, width, 128)] + [whole(g1)] + plan.specs()
            + [ANYWHERE()] * len(before),
            out_specs=[spec(width)] * 3 + [pl.BlockSpec((8, width), lambda i, *_: (0, 0))],
            scratch_shapes=[
                pltpu.VMEM((width, width), bf), pltpu.VMEM((width, wide), bf),
                pltpu.SemaphoreType.DMA((len(plan.copies),)),
            ],
        ),
        input_output_aliases=aliases,
        compiler_params=kernel_params(),
        cost_estimate=cost(2 * total * width * (width + wide) / parts, 1.5e7),
    )(plan.me, hidden_grad, h2_grad, normed1, inverse1, g1, *plan.arrays, *before)


def input_kernel(plan, me, h1_grad, grads, *refs):
    out, wq, wk, wv, sems = refs[len(plan.arrays) :]
    start = pl.program_id(0) == 0
    fetch(plan, me[0], refs, (wq, wk, wv), sems, start)
    arrive(plan, me[0], refs, (wq, wk, wv), sems, start)
    total = h1_grad[...] + nt(grads[0], wq[...]) + nt(grads[1], wk[...]) + nt(grads[2], wv[...])
    out[...] = total.astype(jnp.bfloat16)


def input_grad_of(h1_grad, grads, plan):
    total, width = h1_grad.shape
    rows, steps, spec = row_blocks(total, 1, 0)
    return pl.pallas_call(
        functools.partial(input_kernel, plan),
        out_shape=shape(total, width, jnp.bfloat16),
        grid_spec=pltpu.PrefetchScalarGridSpec(
            num_scalar_prefetch=1,
            grid=(steps,),
            in_specs=[spec(width), pl.BlockSpec((3, rows, width), lambda i, *_: (0, i, 0))] + plan.specs(),
            out_specs=spec(width),
            scratch_shapes=[pltpu.VMEM((width, width), jnp.bfloat16)] * 3
            + [pltpu.SemaphoreType.DMA((len(plan.copies),))],
        ),
        compiler_params=kernel_params(),
        cost_estimate=cost(6 * total * width * width, 2e7),
        name="input_grad",
    )(plan.me, h1_grad, grads, *plan.arrays)


def store_chunks(product, me, own, send):
    count = 2 * own.shape[0]
    rows = product.shape[0] // count
    for g in range(count):
        chunk = product[g * rows : (g + 1) * rows].astype(jnp.bfloat16)
        apart = g ^ me

        @pl.when(apart % 2 == 0)
        def _():
            own[apart // 2] = chunk

        @pl.when(apart % 2 == 1)
        def _():
            send[apart // 2] = chunk


def halves(count, rows, blocks, width):
    return [jax.ShapeDtypeStruct((count // 2, rows * blocks, width), jnp.bfloat16)] * 2


def back_weight_kernel(me, active, grad, own, send):
    step = pl.program_id(0)
    product = tn(active[...], grad[...]).astype(jnp.bfloat16)
    half = pl.num_programs(0) // 2

    @pl.when(step < half)
    def _():
        send[0] = product

    @pl.when(step >= half)
    def _():
        own[0] = product


def plain_weight_kernel(me, active, grad, own, send):
    store_chunks(tn(active[...], grad[...]), me[0], own, send)


def back_weight(me, active, grad, count):
    total, wide = active.shape
    width = grad.shape[1]
    rows = wide // count
    half = count // 2
    common = dict(
        out_shape=halves(count, rows, 1, width),
        compiler_params=kernel_params(),
        cost_estimate=cost(2 * total * wide * width, 1.3e7),
        name="back_weight",
    )
    if rows % 128 == 0:
        chunk = lambda t, me: ((2 * (t % half) + 1 - t // half) ^ me[0])
        return pl.pallas_call(
            back_weight_kernel,
            grid_spec=pltpu.PrefetchScalarGridSpec(
                num_scalar_prefetch=1,
                grid=(count,),
                in_specs=[pl.BlockSpec((total, rows), lambda t, me: (0, chunk(t, me))), whole(grad)],
                out_specs=[
                    pl.BlockSpec((1, rows, width), lambda t, me: (jnp.maximum(t - half, 0), 0, 0)),
                    pl.BlockSpec((1, rows, width), lambda t, me: (jnp.minimum(t, half - 1), 0, 0)),
                ],
            ),
            **common,
        )(me, active, grad)
    block = 256
    return pl.pallas_call(
        plain_weight_kernel,
        grid_spec=pltpu.PrefetchScalarGridSpec(
            num_scalar_prefetch=1,
            grid=(width // block,),
            in_specs=[whole(active), pl.BlockSpec((total, block), lambda j, me: (0, j))],
            out_specs=[pl.BlockSpec((half, rows, block), lambda j, me: (0, 0, j))] * 2,
        ),
        **common,
    )(me, active, grad)


def in_out_kernel(me, after, hidden_grad, mixed, branch_grad, own, send):
    last = pl.program_id(0) == pl.num_programs(0) - 1

    @pl.when(jnp.logical_not(last))
    def _():
        store_chunks(tn(after[...], hidden_grad[...]), me[0], own, send)

    @pl.when(last)
    def _():
        store_chunks(tn(mixed[...], branch_grad[...]), me[0], own, send)


def in_out_weight(me, after, hidden_grad, mixed, branch_grad, count):
    total, width = after.shape
    blocks = hidden_grad.shape[1] // width
    rows = width // count
    return pl.pallas_call(
        in_out_kernel,
        out_shape=halves(count, rows, blocks + 1, width),
        grid_spec=pltpu.PrefetchScalarGridSpec(
            num_scalar_prefetch=1,
            grid=(blocks + 1,),
            in_specs=[
                whole(after),
                pl.BlockSpec((total, width), lambda j, me: (0, jnp.minimum(j, blocks - 1))),
                whole(mixed),
                whole(branch_grad),
            ],
            out_specs=[pl.BlockSpec((count // 2, rows, width), lambda j, me: (0, j, 0))] * 2,
        ),
        compiler_params=kernel_params(),
        cost_estimate=cost(2 * total * width * width * (blocks + 1), 2e7),
        name="in_out_weight",
    )(me, after, hidden_grad, mixed, branch_grad)


SMALL_ROWS = 16


def row_stride(chunk):
    return -(-chunk // 16) * 16


def small_tile(vectors, wide, g, count, width):
    size, wide_size = width // count, wide.shape[1] // count
    part = slice(g * size, (g + 1) * size)
    tops = [ref[rows, part] for ref, rows in vectors]
    fill = lambda rows, used: jnp.zeros((rows, width - used), jnp.float32)
    top = jnp.concatenate(tops, axis=0)
    eight = jnp.concatenate([top, fill(8, size)], axis=1)
    last = jnp.concatenate([wide[:, g * wide_size : (g + 1) * wide_size], fill(1, wide_size)], axis=1)
    return jnp.concatenate([eight, last, jnp.zeros((7, width), jnp.float32)], axis=0).astype(jnp.bfloat16)


def qkv_weight_kernel(me, rows, grads, attend_sums, sums1, sums2, wide, own, send):
    step = pl.program_id(0)
    count, width = 2 * own.shape[0], own.shape[2]
    chunk = width // count
    stride = row_stride(chunk)
    product = tn(rows[...], grads[0])

    def keep(g, first, value):
        apart = g ^ me[0]
        size = value.shape[0]

        @pl.when(apart % 2 == 0)
        def _():
            own[apart // 2, first : first + size] = value

        @pl.when(apart % 2 == 1)
        def _():
            send[apart // 2, first : first + size] = value

    for n in range(3):

        @pl.when(step == n)
        def _():
            for g in range(count):
                keep(g, n * stride, product[g * chunk : (g + 1) * chunk].astype(jnp.bfloat16))

    @pl.when(step == 0)
    def _():
        vectors = (
            (attend_sums, slice(0, 2)), (sums1, slice(2, 3)), (sums2, slice(2, 3)),
            (sums1, slice(0, 2)), (sums2, slice(0, 2)),
        )
        for g in range(count):
            keep(g, 3 * stride, small_tile(vectors, wide, g, count, width))


def qkv_weight(me, rows, grads, attend_sums, sums1, sums2, wide, count):
    total, width = rows.shape
    tall = 3 * row_stride(width // count) + SMALL_ROWS
    block = pl.BlockSpec((count // 2, tall, width), lambda j, me: (0, 0, 0))
    return pl.pallas_call(
        qkv_weight_kernel,
        out_shape=halves(count, tall, 1, width),
        grid_spec=pltpu.PrefetchScalarGridSpec(
            num_scalar_prefetch=1,
            grid=(3,),
            in_specs=[whole(rows), pl.BlockSpec((1, total, width), lambda j, me: (j, 0, 0))]
            + [whole(a) for a in (attend_sums, sums1, sums2, wide)],
            out_specs=[block] * 2,
        ),
        compiler_params=kernel_params(),
        cost_estimate=cost(6 * total * width * width, 1e7),
        name="qkv_weight",
    )(me, rows, grads, attend_sums, sums1, sums2, wide)


def deliver_kernel(odd, kept, other, *outs):
    first, second = kept[...].astype(jnp.float32), other[...].astype(jnp.float32)
    swap = odd[0] == 1
    both = jnp.concatenate([jnp.where(swap, second, first), jnp.where(swap, first, second)], axis=0)
    chunk = outs[0].shape[0]
    stride = row_stride(chunk)
    for n in range(3):
        outs[n][...] = both[n * stride : n * stride + chunk]
    for n, out in enumerate(outs[3:]):
        out[...] = both[3 * stride + n, 0 : out.shape[0]]


def deliver(odd, kept, other, chunk, wide_chunk):
    width = kept.shape[1]
    sizes = [chunk] * 8 + [wide_chunk]
    return pl.pallas_call(
        deliver_kernel,
        out_shape=[shape(chunk, width, jnp.float32)] * 3
        + [jax.ShapeDtypeStruct((n,), jnp.float32) for n in sizes],
        in_specs=[SMEM(), VMEM(), VMEM()],
        out_specs=[VMEM()] * 12,
        compiler_params=kernel_params(),
        name="deliver",
    )(odd, kept, other)


def pack_kernel(*refs):
    out = refs[-1]
    out[...] = jnp.zeros_like(out)
    at = 0
    for ref in refs[:-1]:
        size = ref.shape[1]
        for first in range(0, size, 128):
            n = min(128, size - first)
            out[at : at + 1, 0:n] = ref[:, first : first + n].astype(jnp.float32)
            at += 1


def spread_kernel(me, table, vectors_out, wide_out):
    count = table.shape[0]
    chunk = vectors_out.shape[1] // count
    wide_chunk = wide_out.shape[1] // count
    for g in range(count):
        tile = table[g ^ me[0]]
        vectors_out[:, g * chunk : (g + 1) * chunk] = tile[0:8, 0:chunk]
        for n, first in enumerate(range(0, wide_chunk, 128)):
            size = min(128, wide_chunk - first)
            wide_out[:, g * wide_chunk + first : g * wide_chunk + first + size] = tile[8 + n : 9 + n, 0:size]


SMEM = lambda: pl.BlockSpec(memory_space=pltpu.SMEM)
VMEM = lambda: pl.BlockSpec(memory_space=pltpu.VMEM)


def pack(vectors):
    return pl.pallas_call(
        pack_kernel, out_shape=shape(16, 128, jnp.float32), in_specs=[VMEM()] * len(vectors), out_specs=VMEM(),
        compiler_params=kernel_params(), name="pack",
    )(*[v.reshape(1, -1) for v in vectors])


def spread(me, table, width, wide):
    return pl.pallas_call(
        spread_kernel, out_shape=[shape(8, width, jnp.float32), shape(1, wide, jnp.float32)],
        in_specs=[SMEM(), VMEM()], out_specs=[VMEM()] * 2, compiler_params=kernel_params(), name="spread",
    )(me, table)


def per_device(
    inputs, cotangent, lengths,
    query_weight, key_weight, value_weight, out_weight, in_weight, back_weight_shard,
    query_bias, value_bias, out_bias, in_bias, back_bias,
    first_gain, first_shift, second_gain, second_shift,
):
    index = lax.axis_index("group")
    me = index.reshape(1).astype(jnp.int32)
    count = lax.axis_size("group")
    bits = count.bit_length() - 1
    seqs, slots, width = inputs.shape
    total = seqs * slots
    chunk = query_weight.shape[0]
    wide = in_weight.shape[1]
    blocks = wide // width
    x = inputs.reshape(total, width)
    cot = cotangent.reshape(total, width)

    in_blocks = [in_weight[:, n * width : (n + 1) * width] for n in range(blocks)]
    got_a, far_a = gather_group(jnp.concatenate([query_weight, key_weight, value_weight]), bits, ())
    table = pack(
        [query_bias, value_bias, out_bias, back_bias, first_gain, first_shift, second_gain, second_shift, in_bias]
    )[None]
    for b in range(bits - 1, -1, -1):
        other = swap_with(table, 1 << b)
        table = jnp.stack([table, other], axis=1).reshape((-1,) + table.shape[1:])
    got_b, far_b = gather_group(jnp.concatenate([out_weight] + in_blocks), bits, far_a + [table])
    vectors, bi = spread(me, table, width, wide)
    bq, bv, bo, bb, g1, s1, g2, s2 = (vectors[i : i + 1] for i in range(8))
    third = [(n, n * chunk, chunk, 0) for n in range(3)]
    plan_a = Gathered(got_a, me, count, chunk, third)
    plan_b = Gathered(
        got_b, me, count, chunk,
        [(0, 0, chunk, 0)] + [(1, (n + 1) * chunk, chunk, n * width) for n in range(blocks)],
    )
    q, k, v, mixed, probs = attend(lengths, x, plan_a, bq, bv)
    back_chunk = back_weight_shard.shape[0]
    got_c, _ = gather_group(back_weight_shard, bits, far_b + [mixed])
    plan_c = Gathered(got_c, me, count, back_chunk, [(0, 0, back_chunk, 0)])
    after_low, normed1, inverse1, active, slope = feed(1, 0, mixed, x, plan_b, bo, g1, s1, bi)
    layer_out, ffn_grad, hidden_grad, h2_grad, sums2, in_bias_sum = turn(
        lengths, slots, active, normed1, slope, cot, plan_c, bb, g1, s1, g2, s2
    )
    own, send = back_weight(me, active, ffn_grad, count)
    hidden_grad, send = lax.optimization_barrier((hidden_grad, send))
    red_c = reduction(own, send, bits)
    came = next(red_c)
    h1_grad, branch_grad, mixed_grad, sums1 = return_grad(
        1, 0, hidden_grad, h2_grad, normed1, inverse1, plan_b, g1
    )
    branch_grad = after(branch_grad, *came)
    came = next(red_c)
    own, send = in_out_weight(me, after_low, hidden_grad, mixed, branch_grad, count)
    red_b = reduction(own, send, bits)
    mixed_grad = after(mixed_grad, send, *came)
    came, came_b = next(red_c), next(red_b)
    grads, sums_at = attend_back(seqs, 0, q, k, v, mixed_grad, probs)
    attend_sums = sums_at[0]
    for seq in range(1, seqs):
        mixed_grad = after(mixed_grad, attend_sums, *came, *came_b)
        came, came_b = next(red_c), next(red_b)
        grads, sums_at = attend_back(seqs, seq, q, k, v, mixed_grad, probs, (grads,))
        attend_sums = attend_sums + sums_at[0]
    rows_in = after(x, *came, *came_b)
    came, came_b = next(red_c), next(red_b)
    own, send = qkv_weight(me, rows_in, grads, attend_sums, sums1, sums2, in_bias_sum, count)
    red_a = reduction(own, send, bits)
    came_a = next(red_a)
    came_b = came_b + next(red_b)
    h1_in = after(h1_grad, *came, *came_b, *came_a)
    came, came_b, came_a = next(red_c), next(red_b), next(red_a)
    input_grad = input_grad_of(h1_in, grads, plan_a)
    next(red_a)
    red_b.send(next(red_a))
    odd = lax.axis_index("replica") & 1
    sum_c, sum_b = (in_order(odd, *finish(steps)) for steps in (red_c, red_b))
    (
        grad_wq, grad_wk, grad_wv, grad_q, grad_v, grad_o, grad_b, grad_g1, grad_s1, grad_g2, grad_s2, grad_i,
    ) = deliver(odd.reshape(1), *finish(red_a), chunk, wide // count)
    up = lambda a: a.astype(jnp.float32)
    in_sum = jnp.concatenate([sum_b[n * chunk : (n + 1) * chunk] for n in range(blocks)], axis=1)
    return (
        layer_out.reshape(inputs.shape), input_grad.reshape(inputs.shape),
        grad_wq, grad_wk, grad_wv,
        up(sum_b[blocks * chunk :]), up(in_sum), up(sum_c),
        grad_q, grad_v, grad_o, grad_i, grad_b, grad_g1, grad_s1, grad_g2, grad_s2,
    )


def solution(mesh):
    return jax.shard_map(
        per_device,
        mesh=mesh,
        in_specs=(
            P(("group", "replica"), None, None),
            P(("group", "replica"), None, None),
            P(("group", "replica")),
            P("group", None),
            P("group", None),
            P("group", None),
            P("group", None),
            P("group", None),
            P("group", None),
            P("group"),
            P("group"),
            P("group"),
            P("group"),
            P("group"),
            P("group"),
            P("group"),
            P("group"),
            P("group"),
        ),
        out_specs=(
            P(("group", "replica"), None, None),
            P(("group", "replica"), None, None),
            P("group", None),
            P("group", None),
            P("group", None),
            P("group", None),
            P("group", None),
            P("group", None),
            P("group"),
            P("group"),
            P("group"),
            P("group"),
            P("group"),
            P("group"),
            P("group"),
            P("group"),
            P("group"),
        ),
        check_vma=False,
    )
```

```python
import functools

import jax
import jax.numpy as jnp
from jax import lax
from jax.experimental import pallas as pl
from jax.experimental.pallas import tpu as pltpu
from jax.sharding import PartitionSpec as P

HEAD_DIM = 64


NORM_EPS = 1e-12
inverse_root_two = 0.7071067811865476
inverse_root_tau = 0.3989422804014327


AXES = ("group", "replica")


def swap_with(array, group_mask, replica_mask=0):
    groups, replicas = lax.axis_size("group"), lax.axis_size("replica")
    pairs = [
        (g * replicas + r, (g ^ group_mask) * replicas + (r ^ replica_mask))
        for g in range(groups)
        for r in range(replicas)
    ]
    return lax.ppermute(array, AXES, pairs)


def after(array, *others):
    return lax.optimization_barrier((array,) + others)[0] if others else array


def gather_group(shard, bits, wait_for):
    shard = after(shard, *wait_for)
    pieces = {0: [shard]}
    for d in range(2, 1 << bits, 2):
        pieces[d] = [swap_with(shard, d)]
    far = [pieces[d][0] for d in range(2, 1 << bits, 2)]
    for d in list(pieces):
        pieces[d | 1] = [swap_with(p, 1) for p in pieces[d]]
    return pieces, far


def place(pieces, me, group_size):
    rows = sum(p.shape[0] for p in pieces[0])
    full = jnp.zeros((group_size, rows, pieces[0][0].shape[1]), jnp.bfloat16)
    for d, parts in pieces.items():
        at = 0
        for part in parts:
            full = lax.dynamic_update_slice(full, part[None], (me ^ d, at, 0))
            at += part.shape[0]
    return full


def pick(array, axis, index):
    return lax.dynamic_index_in_dim(array, index, axis, keepdims=False)


def add_low(left, right):
    return (left.astype(jnp.float32) + right.astype(jnp.float32)).astype(jnp.bfloat16)


def reduction(own, send, bits):
    received = swap_with(send, 1)
    yield [received]
    rows, width = own.shape[1:]
    half = rows // 32 * 16
    lefts = [list(range(1, bits)), list(range(1, bits))]
    chunks = add_low(own, received).reshape((2,) * (bits - 1) + (rows, width))
    parts = [chunks[..., :half, :], chunks[..., half:, :]]
    for _ in range(1, bits):
        kept, received, leaving = [], [], []
        for n, (left, end) in enumerate(zip(lefts, (0, -1))):
            b = left[end]
            axis = len(left) - 1 - left.index(b)
            keep, away = (lax.index_in_dim(parts[n], i, axis, keepdims=False) for i in (0, 1))
            kept.append(keep)
            leaving.append(away)
            received.append(swap_with(away, 1 << b))
            left.remove(b)
        yield received + leaving
        parts = [add_low(keep, got) for keep, got in zip(kept, received)]
    total = jnp.concatenate(parts)
    at = lax.axis_index("replica")
    pair = total.reshape(2, rows // 2, width)
    if lax.axis_size("replica") == 1:
        yield pair[0], pair[1]
        return
    received = swap_with(pick(pair, 0, 1 - (at & 1)), 0, 1)
    wait_for = yield [received]
    received = after(received, *(wait_for or ()))
    kept = add_low(pick(pair, 0, at & 1), received)
    mask = 2
    while mask < lax.axis_size("replica"):
        received = swap_with(kept, 0, mask)
        wait_for = yield [received]
        received = after(received, *(wait_for or ()))
        kept = add_low(kept, received)
        mask *= 2
    other = swap_with(kept, 0, 1)
    yield [other]
    yield kept, other


def in_order(odd, kept, other):
    return jnp.where(odd, jnp.concatenate([other, kept]), jnp.concatenate([kept, other]))


def finish(steps):
    *_, last = steps
    return last


class Gathered:
    def __init__(self, pieces, me, count, chunk, segments):
        self.me, self.chunk = me, chunk
        self.arrays, self.copies = [], []
        if chunk % 16:
            full = place(pieces, me[0], count)
            self.plain(full, count, segments)
            return
        for d, parts in pieces.items():
            at = 0
            for part in parts:
                for target, low, size, column in segments:
                    start, stop = max(at, low), min(at + part.shape[0], low + size)
                    if start < stop:
                        self.copies.append(
                            (len(self.arrays), start - at, stop - start, target, d, start - low, column)
                        )
                self.arrays.append(part)
                at += part.shape[0]
        self.fixed = False

    def plain(self, full, count, segments):
        width = full.shape[2]
        for target, low, size, column in segments:
            self.copies.append((len(self.arrays), 0, count * size, target, 0, 0, column))
            self.arrays.append(full[:, low : low + size].reshape(count * size, width))
        self.fixed = True

    def specs(self):
        return [pl.BlockSpec(memory_space=pl.ANY)] * len(self.arrays)

    def transfers(self, me, refs, targets, sems, only=None):
        out = []
        for n, (which, row, rows, target, d, inner, column) in enumerate(self.copies):
            if only is not None and target not in only:
                continue
            size = self.chunk
            if self.fixed:
                first = 0
            else:
                first = pl.multiple_of((me ^ d) * size + inner, 16)
            width = self.arrays[which].shape[1]
            out.append(
                pltpu.make_async_copy(
                    refs[which].at[pl.ds(row, rows)],
                    targets[target].at[pl.ds(first, rows), pl.ds(column, width)],
                    sems.at[n],
                )
            )
        return out


def fetch(plan, me, refs, targets, sems, first_step, only=None):
    @pl.when(first_step)
    def _():
        for copy in plan.transfers(me, refs, targets, sems, only):
            copy.start()


def arrive(plan, me, refs, targets, sems, first_step, only=None):
    @pl.when(first_step)
    def _():
        for copy in plan.transfers(me, refs, targets, sems, only):
            copy.wait()


VMEM_LIMIT = 60 * 1024 * 1024
GROUP_HEADS = 4
GROUP_COLS = GROUP_HEADS * HEAD_DIM


def nt(left, right):
    return lax.dot_general(left, right, (((1,), (1,)), ((), ())), preferred_element_type=jnp.float32)


def nn(left, right):
    return lax.dot_general(left, right, (((1,), (0,)), ((), ())), preferred_element_type=jnp.float32)


def tn(left, right):
    return lax.dot_general(left, right, (((0,), (0,)), ((), ())), preferred_element_type=jnp.float32)


def kernel_params(**more):
    return pltpu.CompilerParams(vmem_limit_bytes=VMEM_LIMIT, **more)


def cost(flops, moved):
    return pl.CostEstimate(flops=int(flops), bytes_accessed=int(moved), transcendentals=0)


def one_head(pair, head):
    lanes = lax.broadcasted_iota(jnp.int32, pair.shape, 1)
    keep = lanes < HEAD_DIM if head % 2 == 0 else lanes >= HEAD_DIM
    return jnp.where(keep, pair, jnp.zeros_like(pair))


def attend_kernel(plan, lens, me, x, bq, bv, *refs):
    q_out, k_out, v_out, mixed_out, probs_out, wq, wk, wv, sems = refs[len(plan.arrays) :]
    seq, group = pl.program_id(0), pl.program_id(1)
    start = jnp.logical_and(seq == 0, group == 0)
    fetch(plan, me[0], refs, (wq, wk, wv), sems, start)
    arrive(plan, me[0], refs, (wq, wk, wv), sems, start)
    cols = pl.ds(pl.multiple_of(group * GROUP_COLS, GROUP_COLS), GROUP_COLS)
    slots = x.shape[0]
    rows = x[...]
    q = ((nn(rows, wq[:, cols]) + bq[...]).astype(jnp.bfloat16) * 0.125).astype(jnp.bfloat16)
    k = nn(rows, wk[:, cols]).astype(jnp.bfloat16)
    v = (nn(rows, wv[:, cols]) + bv[...]).astype(jnp.bfloat16)
    q_out[...] = q
    k_out[...] = k
    v_out[...] = v
    turned = v.astype(jnp.float32).T.astype(jnp.bfloat16)
    valid = lax.broadcasted_iota(jnp.int32, (slots, 1), 0) < lens[seq]
    block = min(256, slots)
    for head in range(GROUP_HEADS):
        pair = slice(head // 2 * 128, head // 2 * 128 + 128)
        keys = one_head(k[:, pair], head)
        for at in range(0, slots, block):
            scores = nt(keys, q[at : at + block, pair])
            scores = jnp.where(valid, scores, -1e30)
            lifted = jnp.exp(scores - jnp.max(scores, axis=0, keepdims=True))
            share = 1.0 / jnp.sum(lifted, axis=0, keepdims=True)
            probs_out[head, :, at : at + block] = (lifted * share).astype(jnp.bfloat16)
    joined = jnp.concatenate(
        [
            nn(turned[h * HEAD_DIM : (h + 1) * HEAD_DIM], probs_out[h])
            for h in range(GROUP_HEADS)
        ]
    )
    mixed_out[...] = joined.T.astype(jnp.bfloat16)


def attend(lengths, rows, plan, bq, bv):
    seqs = lengths.shape[0]
    total, width = rows.shape
    slots = total // seqs
    groups = width // GROUP_COLS
    bias = pl.BlockSpec((1, GROUP_COLS), lambda s, j, *_: (0, j))
    part = pl.BlockSpec((slots, GROUP_COLS), lambda s, j, *_: (s, j))
    table = jax.ShapeDtypeStruct((total, width), jnp.bfloat16)
    return pl.pallas_call(
        functools.partial(attend_kernel, plan),
        out_shape=[table] * 4
        + [jax.ShapeDtypeStruct((seqs * groups * GROUP_HEADS, slots, slots), jnp.bfloat16)],
        grid_spec=pltpu.PrefetchScalarGridSpec(
            num_scalar_prefetch=2,
            grid=(seqs, groups),
            in_specs=[pl.BlockSpec((slots, width), lambda s, j, *_: (s, 0))]
            + [bias] * 2
            + plan.specs(),
            out_specs=[part] * 4
            + [pl.BlockSpec((GROUP_HEADS, slots, slots), lambda s, j, *_: (s * groups + j, 0, 0))],
            scratch_shapes=[pltpu.VMEM((width, width), jnp.bfloat16)] * 3
            + [pltpu.SemaphoreType.DMA((len(plan.copies),))],
        ),
        compiler_params=kernel_params(),
        cost_estimate=cost((6 * total * width * width + 8 * total * slots * width), 3e7),
        name="attend",
    )(lengths, plan.me, rows, bq, bv, *plan.arrays)


def attend_back_kernel(q, k, v, grad, probs, *refs):
    grads_out, sums_out, held = refs[-3:]
    slots = q.shape[0]
    block = min(256, slots)
    key_turned = k[...].astype(jnp.float32).T.astype(jnp.bfloat16)
    dq_parts = []
    for which in range(GROUP_HEADS // 2):
        pair = slice(which * 128, which * 128 + 128)
        grads, queries, values = grad[:, pair], q[:, pair], v[:, pair]
        dv = dk = None
        for head in (2 * which, 2 * which + 1):
            own_values = one_head(values, head)
            for at in range(0, slots, block):
                cols = slice(at, at + block)
                grad_probs = nt(own_values, grads[cols])
                soft = probs[head, :, cols].astype(jnp.float32)
                inner = jnp.sum(soft * grad_probs, axis=0, keepdims=True)
                held[:, cols] = (soft * (grad_probs - inner)).astype(jnp.bfloat16)
            scores_grad = held[...]
            more_v = nn(probs[head], one_head(grads, head))
            more_k = nn(scores_grad, one_head(queries, head))
            dv = more_v if dv is None else dv + more_v
            dk = more_k if dk is None else dk + more_k
            dq_parts.append(nn(key_turned[head * HEAD_DIM : (head + 1) * HEAD_DIM], scores_grad))
        grads_out[1, :, pair] = dk.astype(jnp.bfloat16)
        grads_out[2, :, pair] = dv.astype(jnp.bfloat16)
    grads_out[0] = (jnp.concatenate(dq_parts).T * 0.125).astype(jnp.bfloat16)
    sums_out[0, 0:1, :] = jnp.sum(grads_out[0].astype(jnp.float32), axis=0, keepdims=True)
    sums_out[0, 1:2, :] = jnp.sum(grads_out[2].astype(jnp.float32), axis=0, keepdims=True)


def attend_back(seqs, seq, q, k, v, grad, probs, before=()):
    total, width = q.shape
    slots = total // seqs
    groups = width // GROUP_COLS
    part = pl.BlockSpec((slots, GROUP_COLS), lambda j: (seq, j))
    return pl.pallas_call(
        attend_back_kernel,
        out_shape=[
            jax.ShapeDtypeStruct((3, total, width), jnp.bfloat16),
            jax.ShapeDtypeStruct((1, 2, width), jnp.float32),
        ],
        grid=(groups,),
        in_specs=[part] * 4
        + [pl.BlockSpec((GROUP_HEADS, slots, slots), lambda j: (seq * groups + j, 0, 0))]
        + [pl.BlockSpec(memory_space=pl.ANY)] * len(before),
        out_specs=[
            pl.BlockSpec((3, slots, GROUP_COLS), lambda j: (0, seq, j)),
            pl.BlockSpec((1, 2, GROUP_COLS), lambda j: (0, 0, j)),
        ],
        scratch_shapes=[pltpu.VMEM((slots, slots), jnp.bfloat16)],
        input_output_aliases={5: 0} if before else {},
        compiler_params=kernel_params(),
        cost_estimate=cost(14 * total * slots * width / seqs, 1.5e7),
    )(q, k, v, grad, probs, *before)


def row_mean(array):
    return jnp.mean(array, -1, keepdims=True)


def feed_kernel(plan, aliased, me, mixed, x, bo, g1, s1, bi, *refs):
    after_out, normed_out, inverse_out, active_out, slope_out, wo, wi, sems = refs[len(plan.arrays) + aliased :]
    first = pl.program_id(0) == 0
    fetch(plan, me[0], refs, (wo, wi), sems, first)
    arrive(plan, me[0], refs, (wo, wi), sems, first, (0,))
    hidden_in = x[...].astype(jnp.float32) + (nn(mixed[...], wo[...]) + bo[...])
    centre = hidden_in - row_mean(hidden_in)
    inverse = lax.rsqrt(row_mean(centre * centre) + NORM_EPS)
    normed = centre * inverse
    after = (normed * g1[...] + s1[...]).astype(jnp.bfloat16)
    normed_out[...] = normed
    inverse_out[...] = jnp.broadcast_to(inverse, inverse_out.shape)
    after_out[...] = after
    arrive(plan, me[0], refs, (wo, wi), sems, first, (1,))
    width = after.shape[1]
    for at in range(0, wi.shape[1], width):
        cols = slice(at, at + width)
        hidden = nn(after, wi[:, cols]) + bi[:, cols]
        cdf = 0.5 * (1.0 + lax.erf(hidden * inverse_root_two))
        density = jnp.exp(-0.5 * hidden * hidden) * inverse_root_tau
        active_out[:, cols] = (hidden * cdf).astype(jnp.bfloat16)
        slope_out[:, cols] = (cdf + hidden * density).astype(jnp.bfloat16)


def whole(array):
    return pl.BlockSpec(array.shape, lambda *_: (0,) * array.ndim, pipeline_mode=pl.Buffered(1))


def by_rows(rows, width):
    return pl.BlockSpec((rows, width), lambda i, *_: (i, 0))


def shape(rows, width, dtype):
    return jax.ShapeDtypeStruct((rows, width), dtype)


def row_blocks(total, parts, part):
    rows = min(256, total // parts)
    steps = total // parts // rows
    spec = lambda width: pl.BlockSpec((rows, width), lambda i, *_: (i + part * steps, 0))
    return rows, steps, spec


ANYWHERE = lambda: pl.BlockSpec(memory_space=pl.ANY)


def feed(parts, part, mixed, x, plan, bo, g1, s1, bi, before=()):
    total, width = x.shape
    wide = bi.shape[1]
    _, steps, spec = row_blocks(total, parts, part)
    bf, f32 = jnp.bfloat16, jnp.float32
    aliases = {7 + len(plan.arrays) + n: n for n in range(len(before))}
    return pl.pallas_call(
        functools.partial(feed_kernel, plan, len(before)),
        out_shape=[
            shape(total, width, bf), shape(total, width, f32), shape(total, 128, f32),
            shape(total, wide, bf), shape(total, wide, bf),
        ],
        grid_spec=pltpu.PrefetchScalarGridSpec(
            num_scalar_prefetch=1,
            grid=(steps,),
            in_specs=[spec(width)] * 2 + [whole(a) for a in (bo, g1, s1, bi)] + plan.specs()
            + [ANYWHERE()] * len(before),
            out_specs=[spec(n) for n in (width, width, 128, wide, wide)],
            scratch_shapes=[
                pltpu.VMEM((width, width), bf), pltpu.VMEM((width, wide), bf),
                pltpu.SemaphoreType.DMA((len(plan.copies),)),
            ],
        ),
        input_output_aliases=aliases,
        compiler_params=kernel_params(),
        cost_estimate=cost(2 * total * width * (width + wide) / parts * 3, 1.5e7),
    )(plan.me, mixed, x, bo, g1, s1, bi, *plan.arrays, *before)


def column_sum(array):
    return jnp.sum(array, axis=0, keepdims=True)


def turn_kernel(plan, slots, lens, me, active, normed1, slope, cot, bb, g1, s1, g2, s2, *refs):
    (
        layer_out, ffn_grad_out, hidden_grad_out, h2_grad_out, sums_out, wide_sums_out, wb, sems,
    ) = refs[len(plan.arrays) :]
    step = pl.program_id(0)
    fetch(plan, me[0], refs, (wb,), sems, step == 0)
    arrive(plan, me[0], refs, (wb,), sems, step == 0)

    @pl.when(step == 0)
    def _():
        sums_out[...] = jnp.zeros_like(sums_out)
        wide_sums_out[...] = jnp.zeros_like(wide_sums_out)

    rows, width = normed1.shape
    after = normed1[...] * g1[...] + s1[...]
    h2 = after + (nn(active[...], wb[...]) + bb[...])
    centre = h2 - row_mean(h2)
    inverse = lax.rsqrt(row_mean(centre * centre) + NORM_EPS)
    normed = centre * inverse
    layer_out[...] = (normed * g2[...] + s2[...]).astype(jnp.bfloat16)
    first = step * rows
    place_in = first % slots + lax.broadcasted_iota(jnp.int32, (rows, 1), 0)
    grad = jnp.where(place_in < lens[first // slots], cot[...].astype(jnp.float32), 0.0)
    scaled = grad * g2[...]
    h2_grad = inverse * (scaled - row_mean(scaled) - normed * row_mean(scaled * normed))
    h2_grad_out[...] = h2_grad
    low = h2_grad.astype(jnp.bfloat16)
    ffn_grad_out[...] = low
    sums_out[0:1, :] += column_sum(grad * normed)
    sums_out[1:2, :] += column_sum(grad)
    sums_out[2:3, :] += column_sum(low.astype(jnp.float32))
    for at in range(0, wb.shape[0], width):
        cols = slice(at, at + width)
        piece = (nt(low, wb[cols, :]) * slope[:, cols].astype(jnp.float32)).astype(jnp.bfloat16)
        hidden_grad_out[:, cols] = piece
        wide_sums_out[:, cols] += column_sum(piece.astype(jnp.float32))


def turn(lengths, slots, active, normed1, slope, cot, plan, bb, g1, s1, g2, s2):
    total, width = normed1.shape
    wide = active.shape[1]
    rows = min(256, slots)
    bf, f32 = jnp.bfloat16, jnp.float32
    fixed = lambda r, n: pl.BlockSpec((r, n), lambda i, *_: (0, 0))
    return pl.pallas_call(
        functools.partial(turn_kernel, plan, slots),
        out_shape=[
            shape(total, width, bf), shape(total, width, bf), shape(total, wide, bf),
            shape(total, width, f32), shape(8, width, f32), shape(1, wide, f32),
        ],
        grid_spec=pltpu.PrefetchScalarGridSpec(
            num_scalar_prefetch=2,
            grid=(total // rows,),
            in_specs=[by_rows(rows, n) for n in (wide, width, wide, width)]
            + [whole(a) for a in (bb, g1, s1, g2, s2)] + plan.specs(),
            out_specs=[by_rows(rows, n) for n in (width, width, wide, width)]
            + [fixed(8, width), fixed(1, wide)],
            scratch_shapes=[pltpu.VMEM((wide, width), bf), pltpu.SemaphoreType.DMA((len(plan.copies),))],
        ),
        compiler_params=kernel_params(),
        cost_estimate=cost(4 * total * width * wide, 3e7),
        name="turn",
    )(lengths, plan.me, active, normed1, slope, cot, bb, g1, s1, g2, s2, *plan.arrays)


def return_kernel(plan, aliased, me, hidden_grad, h2_grad, normed1, inverse1, g1, *refs):
    h1_grad_out, branch_grad_out, mixed_grad_out, sums_out, wo, wi, sems = refs[len(plan.arrays) + aliased :]
    start = pl.program_id(0) == 0
    fetch(plan, me[0], refs, (wo, wi), sems, start)
    arrive(plan, me[0], refs, (wo, wi), sems, start)

    @pl.when(start)
    def _():
        sums_out[...] = jnp.zeros_like(sums_out)

    after_grad = nt(hidden_grad[...], wi[...]) + h2_grad[...]
    normed = normed1[...]
    scaled = after_grad * g1[...]
    h1_grad = inverse1[:, 0:1] * (scaled - row_mean(scaled) - normed * row_mean(scaled * normed))
    h1_grad_out[...] = h1_grad
    low = h1_grad.astype(jnp.bfloat16)
    branch_grad_out[...] = low
    mixed_grad_out[...] = nt(low, wo[...]).astype(jnp.bfloat16)
    sums_out[0:1, :] += column_sum(after_grad * normed)
    sums_out[1:2, :] += column_sum(after_grad)
    sums_out[2:3, :] += column_sum(low.astype(jnp.float32))


def return_grad(parts, part, hidden_grad, h2_grad, normed1, inverse1, plan, g1, before=()):
    total, width = normed1.shape
    wide = hidden_grad.shape[1]
    _, steps, spec = row_blocks(total, parts, part)
    bf, f32 = jnp.bfloat16, jnp.float32
    aliases = {6 + len(plan.arrays) + n: n for n in range(len(before))}
    return pl.pallas_call(
        functools.partial(return_kernel, plan, len(before)),
        out_shape=[
            shape(total, width, f32), shape(total, width, bf), shape(total, width, bf), shape(8, width, f32),
        ],
        grid_spec=pltpu.PrefetchScalarGridSpec(
            num_scalar_prefetch=1,
            grid=(steps,),
            in_specs=[spec(n) for n in (wide, width, width, 128)] + [whole(g1)] + plan.specs()
            + [ANYWHERE()] * len(before),
            out_specs=[spec(width)] * 3 + [pl.BlockSpec((8, width), lambda i, *_: (0, 0))],
            scratch_shapes=[
                pltpu.VMEM((width, width), bf), pltpu.VMEM((width, wide), bf),
                pltpu.SemaphoreType.DMA((len(plan.copies),)),
            ],
        ),
        input_output_aliases=aliases,
        compiler_params=kernel_params(),
        cost_estimate=cost(2 * total * width * (width + wide) / parts, 1.5e7),
    )(plan.me, hidden_grad, h2_grad, normed1, inverse1, g1, *plan.arrays, *before)


def input_kernel(plan, me, h1_grad, grads, *refs):
    out, wq, wk, wv, sems = refs[len(plan.arrays) :]
    start = pl.program_id(0) == 0
    fetch(plan, me[0], refs, (wq, wk, wv), sems, start)
    arrive(plan, me[0], refs, (wq, wk, wv), sems, start)
    total = h1_grad[...] + nt(grads[0], wq[...]) + nt(grads[1], wk[...]) + nt(grads[2], wv[...])
    out[...] = total.astype(jnp.bfloat16)


def input_grad_of(h1_grad, grads, plan):
    total, width = h1_grad.shape
    rows, steps, spec = row_blocks(total, 1, 0)
    return pl.pallas_call(
        functools.partial(input_kernel, plan),
        out_shape=shape(total, width, jnp.bfloat16),
        grid_spec=pltpu.PrefetchScalarGridSpec(
            num_scalar_prefetch=1,
            grid=(steps,),
            in_specs=[spec(width), pl.BlockSpec((3, rows, width), lambda i, *_: (0, i, 0))] + plan.specs(),
            out_specs=spec(width),
            scratch_shapes=[pltpu.VMEM((width, width), jnp.bfloat16)] * 3
            + [pltpu.SemaphoreType.DMA((len(plan.copies),))],
        ),
        compiler_params=kernel_params(),
        cost_estimate=cost(6 * total * width * width, 2e7),
        name="input_grad",
    )(plan.me, h1_grad, grads, *plan.arrays)


def store_chunks(product, me, own, send):
    count = 2 * own.shape[0]
    rows = product.shape[0] // count
    for g in range(count):
        chunk = product[g * rows : (g + 1) * rows].astype(jnp.bfloat16)
        apart = g ^ me

        @pl.when(apart % 2 == 0)
        def _():
            own[apart // 2] = chunk

        @pl.when(apart % 2 == 1)
        def _():
            send[apart // 2] = chunk


def halves(count, rows, blocks, width):
    return [jax.ShapeDtypeStruct((count // 2, rows * blocks, width), jnp.bfloat16)] * 2


def back_weight_kernel(me, active, grad, own, send):
    step = pl.program_id(0)
    product = tn(active[...], grad[...]).astype(jnp.bfloat16)
    half = pl.num_programs(0) // 2

    @pl.when(step < half)
    def _():
        send[0] = product

    @pl.when(step >= half)
    def _():
        own[0] = product


def plain_weight_kernel(me, active, grad, own, send):
    store_chunks(tn(active[...], grad[...]), me[0], own, send)


def back_weight(me, active, grad, count):
    total, wide = active.shape
    width = grad.shape[1]
    rows = wide // count
    half = count // 2
    common = dict(
        out_shape=halves(count, rows, 1, width),
        compiler_params=kernel_params(),
        cost_estimate=cost(2 * total * wide * width, 1.3e7),
        name="back_weight",
    )
    if rows % 128 == 0:
        chunk = lambda t, me: ((2 * (t % half) + 1 - t // half) ^ me[0])
        return pl.pallas_call(
            back_weight_kernel,
            grid_spec=pltpu.PrefetchScalarGridSpec(
                num_scalar_prefetch=1,
                grid=(count,),
                in_specs=[pl.BlockSpec((total, rows), lambda t, me: (0, chunk(t, me))), whole(grad)],
                out_specs=[
                    pl.BlockSpec((1, rows, width), lambda t, me: (jnp.maximum(t - half, 0), 0, 0)),
                    pl.BlockSpec((1, rows, width), lambda t, me: (jnp.minimum(t, half - 1), 0, 0)),
                ],
            ),
            **common,
        )(me, active, grad)
    block = 256
    return pl.pallas_call(
        plain_weight_kernel,
        grid_spec=pltpu.PrefetchScalarGridSpec(
            num_scalar_prefetch=1,
            grid=(width // block,),
            in_specs=[whole(active), pl.BlockSpec((total, block), lambda j, me: (0, j))],
            out_specs=[pl.BlockSpec((half, rows, block), lambda j, me: (0, 0, j))] * 2,
        ),
        **common,
    )(me, active, grad)


def in_out_kernel(me, after, hidden_grad, mixed, branch_grad, own, send):
    last = pl.program_id(0) == pl.num_programs(0) - 1

    @pl.when(jnp.logical_not(last))
    def _():
        store_chunks(tn(after[...], hidden_grad[...]), me[0], own, send)

    @pl.when(last)
    def _():
        store_chunks(tn(mixed[...], branch_grad[...]), me[0], own, send)


def in_out_weight(me, after, hidden_grad, mixed, branch_grad, count):
    total, width = after.shape
    blocks = hidden_grad.shape[1] // width
    rows = width // count
    return pl.pallas_call(
        in_out_kernel,
        out_shape=halves(count, rows, blocks + 1, width),
        grid_spec=pltpu.PrefetchScalarGridSpec(
            num_scalar_prefetch=1,
            grid=(blocks + 1,),
            in_specs=[
                whole(after),
                pl.BlockSpec((total, width), lambda j, me: (0, jnp.minimum(j, blocks - 1))),
                whole(mixed),
                whole(branch_grad),
            ],
            out_specs=[pl.BlockSpec((count // 2, rows, width), lambda j, me: (0, j, 0))] * 2,
        ),
        compiler_params=kernel_params(),
        cost_estimate=cost(2 * total * width * width * (blocks + 1), 2e7),
        name="in_out_weight",
    )(me, after, hidden_grad, mixed, branch_grad)


SMALL_ROWS = 16


def row_stride(chunk):
    return -(-chunk // 16) * 16


def small_tile(vectors, wide, g, count, width):
    size, wide_size = width // count, wide.shape[1] // count
    part = slice(g * size, (g + 1) * size)
    tops = [sum(ref[0, :, part] for ref in vectors[0])] + [ref[rows, part] for ref, rows in vectors[1:]]
    fill = lambda rows, used: jnp.zeros((rows, width - used), jnp.float32)
    top = jnp.concatenate(tops, axis=0)
    eight = jnp.concatenate([top, fill(8, size)], axis=1)
    last = jnp.concatenate([wide[:, g * wide_size : (g + 1) * wide_size], fill(1, wide_size)], axis=1)
    return jnp.concatenate([eight, last, jnp.zeros((7, width), jnp.float32)], axis=0).astype(jnp.bfloat16)


def qkv_weight_kernel(me, rows, grads, sums1, sums2, wide, *refs):
    attend_sums, (own, send) = refs[:-2], refs[-2:]
    step = pl.program_id(0)
    count, width = 2 * own.shape[0], own.shape[2]
    chunk = width // count
    stride = row_stride(chunk)
    product = tn(rows[...], grads[0])

    def keep(g, first, value):
        apart = g ^ me[0]
        size = value.shape[0]

        @pl.when(apart % 2 == 0)
        def _():
            own[apart // 2, first : first + size] = value

        @pl.when(apart % 2 == 1)
        def _():
            send[apart // 2, first : first + size] = value

    for n in range(3):

        @pl.when(step == n)
        def _():
            for g in range(count):
                keep(g, n * stride, product[g * chunk : (g + 1) * chunk].astype(jnp.bfloat16))

    @pl.when(step == 0)
    def _():
        vectors = (
            attend_sums, (sums1, slice(2, 3)), (sums2, slice(2, 3)),
            (sums1, slice(0, 2)), (sums2, slice(0, 2)),
        )
        for g in range(count):
            keep(g, 3 * stride, small_tile(vectors, wide, g, count, width))


def qkv_weight(me, rows, grads, attend_sums, sums1, sums2, wide, count):
    total, width = rows.shape
    tall = 3 * row_stride(width // count) + SMALL_ROWS
    block = pl.BlockSpec((count // 2, tall, width), lambda j, me: (0, 0, 0))
    return pl.pallas_call(
        qkv_weight_kernel,
        out_shape=halves(count, tall, 1, width),
        grid_spec=pltpu.PrefetchScalarGridSpec(
            num_scalar_prefetch=1,
            grid=(3,),
            in_specs=[whole(rows), pl.BlockSpec((1, total, width), lambda j, me: (j, 0, 0))]
            + [whole(a) for a in (sums1, sums2, wide, *attend_sums)],
            out_specs=[block] * 2,
        ),
        compiler_params=kernel_params(),
        cost_estimate=cost(6 * total * width * width, 1e7),
        name="qkv_weight",
    )(me, rows, grads, sums1, sums2, wide, *attend_sums)


def deliver_kernel(odd, kept, other, *outs):
    first, second = kept[...].astype(jnp.float32), other[...].astype(jnp.float32)
    swap = odd[0] == 1
    both = jnp.concatenate([jnp.where(swap, second, first), jnp.where(swap, first, second)], axis=0)
    chunk = outs[0].shape[0]
    stride = row_stride(chunk)
    for n in range(3):
        outs[n][...] = both[n * stride : n * stride + chunk]
    for n, out in enumerate(outs[3:]):
        out[...] = both[3 * stride + n, 0 : out.shape[0]]


def deliver(odd, kept, other, chunk, wide_chunk):
    width = kept.shape[1]
    sizes = [chunk] * 8 + [wide_chunk]
    return pl.pallas_call(
        deliver_kernel,
        out_shape=[shape(chunk, width, jnp.float32)] * 3
        + [jax.ShapeDtypeStruct((n,), jnp.float32) for n in sizes],
        in_specs=[SMEM(), VMEM(), VMEM()],
        out_specs=[VMEM()] * 12,
        compiler_params=kernel_params(),
        name="deliver",
    )(odd, kept, other)


def pack_kernel(*refs):
    out = refs[-1]
    out[...] = jnp.zeros_like(out)
    at = 0
    for ref in refs[:-1]:
        size = ref.shape[1]
        for first in range(0, size, 128):
            n = min(128, size - first)
            out[at : at + 1, 0:n] = ref[:, first : first + n].astype(jnp.float32)
            at += 1


def spread_kernel(me, table, vectors_out, wide_out):
    count = table.shape[0]
    chunk = vectors_out.shape[1] // count
    wide_chunk = wide_out.shape[1] // count
    for g in range(count):
        tile = table[g ^ me[0]]
        vectors_out[:, g * chunk : (g + 1) * chunk] = tile[0:8, 0:chunk]
        for n, first in enumerate(range(0, wide_chunk, 128)):
            size = min(128, wide_chunk - first)
            wide_out[:, g * wide_chunk + first : g * wide_chunk + first + size] = tile[8 + n : 9 + n, 0:size]


SMEM = lambda: pl.BlockSpec(memory_space=pltpu.SMEM)
VMEM = lambda: pl.BlockSpec(memory_space=pltpu.VMEM)


def pack(vectors):
    return pl.pallas_call(
        pack_kernel, out_shape=shape(16, 128, jnp.float32), in_specs=[VMEM()] * len(vectors), out_specs=VMEM(),
        compiler_params=kernel_params(), name="pack",
    )(*[v.reshape(1, -1) for v in vectors])


def spread(me, table, width, wide):
    return pl.pallas_call(
        spread_kernel, out_shape=[shape(8, width, jnp.float32), shape(1, wide, jnp.float32)],
        in_specs=[SMEM(), VMEM()], out_specs=[VMEM()] * 2, compiler_params=kernel_params(), name="spread",
    )(me, table)


def per_device(
    inputs, cotangent, lengths,
    query_weight, key_weight, value_weight, out_weight, in_weight, back_weight_shard,
    query_bias, value_bias, out_bias, in_bias, back_bias,
    first_gain, first_shift, second_gain, second_shift,
):
    index = lax.axis_index("group")
    me = index.reshape(1).astype(jnp.int32)
    count = lax.axis_size("group")
    bits = count.bit_length() - 1
    seqs, slots, width = inputs.shape
    total = seqs * slots
    chunk = query_weight.shape[0]
    wide = in_weight.shape[1]
    blocks = wide // width
    x = inputs.reshape(total, width)
    cot = cotangent.reshape(total, width)

    in_blocks = [in_weight[:, n * width : (n + 1) * width] for n in range(blocks)]
    got_a, far_a = gather_group(jnp.concatenate([query_weight, key_weight, value_weight]), bits, ())
    table = pack(
        [query_bias, value_bias, out_bias, back_bias, first_gain, first_shift, second_gain, second_shift, in_bias]
    )[None]
    for b in range(bits - 1, -1, -1):
        other = swap_with(table, 1 << b)
        table = jnp.stack([table, other], axis=1).reshape((-1,) + table.shape[1:])
    got_b, far_b = gather_group(jnp.concatenate([out_weight] + in_blocks), bits, far_a + [table])
    vectors, bi = spread(me, table, width, wide)
    bq, bv, bo, bb, g1, s1, g2, s2 = (vectors[i : i + 1] for i in range(8))
    third = [(n, n * chunk, chunk, 0) for n in range(3)]
    plan_a = Gathered(got_a, me, count, chunk, third)
    plan_b = Gathered(
        got_b, me, count, chunk,
        [(0, 0, chunk, 0)] + [(1, (n + 1) * chunk, chunk, n * width) for n in range(blocks)],
    )
    q, k, v, mixed, probs = attend(lengths, x, plan_a, bq, bv)
    back_chunk = back_weight_shard.shape[0]
    got_c, _ = gather_group(back_weight_shard, bits, far_b + [mixed])
    plan_c = Gathered(got_c, me, count, back_chunk, [(0, 0, back_chunk, 0)])
    after_low, normed1, inverse1, active, slope = feed(1, 0, mixed, x, plan_b, bo, g1, s1, bi)
    layer_out, ffn_grad, hidden_grad, h2_grad, sums2, in_bias_sum = turn(
        lengths, slots, active, normed1, slope, cot, plan_c, bb, g1, s1, g2, s2
    )
    own, send = back_weight(me, active, ffn_grad, count)
    hidden_grad, send = lax.optimization_barrier((hidden_grad, send))
    red_c = reduction(own, send, bits)
    came = next(red_c)
    h1_grad, branch_grad, mixed_grad, sums1 = return_grad(
        1, 0, hidden_grad, h2_grad, normed1, inverse1, plan_b, g1
    )
    branch_grad = after(branch_grad, *came)
    came = next(red_c)
    own, send = in_out_weight(me, after_low, hidden_grad, mixed, branch_grad, count)
    red_b = reduction(own, send, bits)
    mixed_grad = after(mixed_grad, send, *came)
    came, came_b = next(red_c), next(red_b)
    grads, sums_at = attend_back(seqs, 0, q, k, v, mixed_grad, probs)
    attend_sums = [sums_at]
    for seq in range(1, seqs):
        mixed_grad = after(mixed_grad, *attend_sums, *came, *came_b)
        came, came_b = next(red_c), next(red_b)
        grads, sums_at = attend_back(seqs, seq, q, k, v, mixed_grad, probs, (grads,))
        attend_sums = attend_sums + [sums_at]
    rows_in = after(x, *came, *came_b)
    came, came_b = next(red_c), next(red_b)
    own, send = qkv_weight(me, rows_in, grads, attend_sums, sums1, sums2, in_bias_sum, count)
    red_a = reduction(own, send, bits)
    came_a = next(red_a)
    came_b = came_b[:2] + next(red_b)
    leaving = next(red_a)[-2:]
    h1_in = after(h1_grad, *came, *came_b, *leaving)
    came, _ = next(red_c), red_b.send(leaving)
    input_grad = input_grad_of(h1_in, grads, plan_a)
    next(red_a)
    red_b.send(next(red_a))
    odd = lax.axis_index("replica") & 1
    sum_c, sum_b = (in_order(odd, *finish(steps)) for steps in (red_c, red_b))
    (
        grad_wq, grad_wk, grad_wv, grad_q, grad_v, grad_o, grad_b, grad_g1, grad_s1, grad_g2, grad_s2, grad_i,
    ) = deliver(odd.reshape(1), *finish(red_a), chunk, wide // count)
    up = lambda a: a.astype(jnp.float32)
    in_sum = jnp.concatenate([sum_b[n * chunk : (n + 1) * chunk] for n in range(blocks)], axis=1)
    return (
        layer_out.reshape(inputs.shape), input_grad.reshape(inputs.shape),
        grad_wq, grad_wk, grad_wv,
        up(sum_b[blocks * chunk :]), up(in_sum), up(sum_c),
        grad_q, grad_v, grad_o, grad_i, grad_b, grad_g1, grad_s1, grad_g2, grad_s2,
    )


def solution(mesh):
    return jax.shard_map(
        per_device,
        mesh=mesh,
        in_specs=(
            P(("group", "replica"), None, None),
            P(("group", "replica"), None, None),
            P(("group", "replica")),
            P("group", None),
            P("group", None),
            P("group", None),
            P("group", None),
            P("group", None),
            P("group", None),
            P("group"),
            P("group"),
            P("group"),
            P("group"),
            P("group"),
            P("group"),
            P("group"),
            P("group"),
            P("group"),
        ),
        out_specs=(
            P(("group", "replica"), None, None),
            P(("group", "replica"), None, None),
            P("group", None),
            P("group", None),
            P("group", None),
            P("group", None),
            P("group", None),
            P("group", None),
            P("group"),
            P("group"),
            P("group"),
            P("group"),
            P("group"),
            P("group"),
            P("group"),
            P("group"),
            P("group"),
        ),
        check_vma=False,
    )
```
